128 devices in a mesh: tm: 16 (over z, x), mp: 8 (over y, core).
Axes of the slice: x: 4, y: 4, z: 4, core: 2. Of those that a mesh axis runs over, the one named last changes fastest.
Arguments:
- frames: bfloat16 [1536, 8192], P('mp', 'tm'), may hold values from -40 to 40
- norm_gain: float32 [1536], replicated, may hold values from 0.1 to 1.9
- w_qkv: bfloat16 [3, 1536, 1536], P(None, 'mp'), may hold values from -0.76546554 to 0.76546554
- w_out: bfloat16 [1536, 1536], P('mp'), may hold values from -0.15625 to 0.15625
- conv_kernel: float32 [31, 1536], P(None, 'mp'), may hold values from -1 to 1
- grad_out: bfloat16 [1536, 8192], P('mp', 'tm'), may hold values from -6 to 6
Outputs:
- block_out: bfloat16 [1536, 8192], P('mp', 'tm')
- grad_frames: bfloat16 [1536, 8192], P('mp', 'tm')
- grad_gain: float32 [1536], P('mp')
- grad_qkv: float32 [3, 1536, 1536], P(None, 'mp')
- grad_out_proj: float32 [1536, 1536], P('mp')
- grad_kernel: float32 [31, 1536], P(None, 'mp')
The draws below stay inside these ranges and needn't reach their ends.
All inputs are finite; a program needn't handle non-finite values.
Results may differ from the reference program's by a relative error of at most 0.023.
The reference program's roundings to bfloat16 on the way (of `normed`, `packed`, `attended`, `residual_sum`, `back_cast`, `grad_attn`, `grad_score` and `grad_packed`) count: a program that leaves them out, or rounds other values in their place, can miss the bound.
Values may be sent and summed in bfloat16 or wider, within the bound.
No kernel may reach another device: no remote copies, remote signals or barrier semaphores. Data moves between devices by JAX's collectives and lax.ppermute only.
A program may use at most 128 MiB of HBM per device.

```python
import math
import jax
import jax.numpy as jnp
from jax import lax

D = 1536
HEADS = 24
HEAD_DIM = 64
KERNEL = 31
TOKENS = 8192


def draw_frames(key, part):
    first_key, second_key, third_key = jax.random.split(key, 3)
    entries = jax.random.truncated_normal(first_key, -4.0, 4.0, (TOKENS, D), jnp.float32)
    row_scale = jnp.exp(jax.random.uniform(second_key, (TOKENS, 1), jnp.float32, -0.8, 0.8))
    col_scale = jnp.exp(jax.random.uniform(third_key, (1, D), jnp.float32, -0.8, 0.8))
    return jnp.clip(entries * row_scale * col_scale, -40.0, 40.0).T.astype(jnp.bfloat16)


def draw_w_qkv(key, part):
    first_key, second_key = jax.random.split(key, 2)
    strength = jnp.exp(jax.random.uniform(second_key, (HEADS,), jnp.float32, -0.5, 0.3))
    column = jnp.repeat(strength, HEAD_DIM)
    entries = jax.random.truncated_normal(first_key, -4.0, 4.0, (3, HEADS * HEAD_DIM, D), jnp.float32)
    factors = jnp.stack([column, column, jnp.ones_like(column)])[:, :, None]
    return (entries * factors / math.sqrt(D)).astype(jnp.bfloat16)


def level_of(rng, dims, pieces, least, top_value):
    level, own = 1.0, jax.random.fold_in(rng, 6)
    for position, parts in pieces:
        heights = jnp.exp(jax.random.uniform(jax.random.fold_in(own, position), (parts,), jnp.float32, least / len(pieces), top_value / len(pieces)))
        level = level * jnp.repeat(heights, dims[position] // parts).reshape([-1 if axis == position else 1 for axis in range(len(dims))])
    return level


def gaussian(key, dims, width, reach, shards=(), held_as=jnp.bfloat16):
    gain = level_of(key, dims, shards, -0.22, 0.18) if shards else 1.0
    result = jax.random.normal(key, dims, jnp.float32) * width * gain
    return jnp.minimum(jnp.maximum(result, -reach), reach).astype(held_as)


def setup_inputs(seed: int = 0) -> dict:
    key_list = jax.random.split(jax.random.key(seed), 7)
    frames = draw_frames(jax.random.fold_in(key_list[6], 71), 0)
    norm_gain = jnp.clip(1.0 + 0.18 * jax.random.normal(key_list[1], (D,), jnp.float32), 0.1, 1.9)
    w_qkv = draw_w_qkv(jax.random.fold_in(key_list[6], 71), 0)
    w_out = gaussian(key_list[3], (HEADS * HEAD_DIM, D), (HEADS * HEAD_DIM) ** -0.5, 0.15625, ((0, 8),))
    conv_kernel = gaussian(key_list[4], (KERNEL, D), 0.2, 1.0, ((1, 8),), jnp.float32)
    grad_out = gaussian(key_list[5], (D, TOKENS), 1.0, 6.0, ((0, 8), (1, 16)))
    return dict(frames=frames, norm_gain=norm_gain, w_qkv=w_qkv, w_out=w_out, conv_kernel=conv_kernel, grad_out=grad_out)


def head_forward(operands):
    queries, key_rows, values = operands
    scores = jnp.dot(queries, key_rows.T, preferred_element_type=jnp.float32) * HEAD_DIM ** (-0.5)
    row_max = lax.optimization_barrier(jnp.max(scores, axis=1, keepdims=True))
    weights = jnp.exp(scores - row_max)
    row_total = lax.optimization_barrier(jnp.sum(weights, axis=1, keepdims=True))
    attended = jnp.dot(weights.astype(jnp.bfloat16), values, preferred_element_type=jnp.float32) / row_total
    return (attended.astype(jnp.bfloat16), (row_max + jnp.log(row_total))[:, 0])

def head_backward(operands):
    queries, key_rows, values, attended, grad_attn, logsum = operands
    score_scale = HEAD_DIM ** (-0.5)
    offset = lax.optimization_barrier(jnp.sum(grad_attn.astype(jnp.float32) * attended.astype(jnp.float32), axis=1, keepdims=True))
    scores = jnp.dot(queries, key_rows.T, preferred_element_type=jnp.float32) * score_scale
    probabilities = jnp.exp(scores - logsum[:, None])
    grad_prob = jnp.dot(grad_attn, values.T, preferred_element_type=jnp.float32)
    grad_score = (probabilities * (grad_prob - offset)).astype(jnp.bfloat16)
    grad_queries = jnp.dot(grad_score, key_rows, preferred_element_type=jnp.float32) * score_scale
    grad_keys = jnp.dot(grad_score.T, queries, preferred_element_type=jnp.float32) * score_scale
    grad_values = jnp.dot(probabilities.astype(jnp.bfloat16).T, grad_attn, preferred_element_type=jnp.float32)
    return (grad_queries, grad_keys, grad_values)

def reference(frames, norm_gain, w_qkv, w_out, conv_kernel, grad_out):
    inputs = frames.T.astype(jnp.float32)
    inverse = lax.rsqrt(lax.optimization_barrier(jnp.mean(inputs * inputs, axis=1, keepdims=True)) + 1e-06)
    normed = (inputs * inverse * norm_gain).astype(jnp.bfloat16)
    head_width = HEADS * HEAD_DIM
    qkv_rows = w_qkv.reshape(3 * head_width, D)
    packed = jnp.dot(normed, qkv_rows.T, preferred_element_type=jnp.float32).astype(jnp.bfloat16)
    packed = packed.reshape(TOKENS, 3, HEADS, HEAD_DIM).transpose(1, 2, 0, 3)
    attended, logsum = lax.map(head_forward, (packed[0], packed[1], packed[2]))
    attn_flat = attended.transpose(1, 0, 2).reshape(TOKENS, head_width)
    residual_sum = (inputs + jnp.dot(attn_flat, w_out, preferred_element_type=jnp.float32)).astype(jnp.bfloat16)
    half_width = KERNEL // 2
    resid = residual_sum.astype(jnp.float32)
    resid_pad = jnp.pad(resid, ((half_width, half_width), (0, 0)))
    upstream = grad_out.T.astype(jnp.float32)
    upstream_pad = jnp.pad(upstream, ((half_width, half_width), (0, 0)))
    conv_sum = jnp.zeros_like(resid)
    back_sum = upstream
    kernel_rows = []
    for tap_index in range(KERNEL):
        conv_sum = conv_sum + conv_kernel[tap_index] * resid_pad[tap_index:tap_index + TOKENS]
        mirror = 2 * half_width - tap_index
        back_sum = back_sum + conv_kernel[tap_index] * upstream_pad[mirror:mirror + TOKENS]
        kernel_rows.append(lax.optimization_barrier(jnp.sum(upstream * resid_pad[tap_index:tap_index + TOKENS], axis=0)))
    block_out = (resid + conv_sum).astype(jnp.bfloat16).T
    grad_kernel = jnp.stack(kernel_rows)
    back_cast = back_sum.astype(jnp.bfloat16)
    grad_out_proj = jnp.dot(attn_flat.T, back_cast, preferred_element_type=jnp.float32)
    grad_attn = jnp.dot(back_cast, w_out.T, preferred_element_type=jnp.float32).astype(jnp.bfloat16)
    grad_attn = grad_attn.reshape(TOKENS, HEADS, HEAD_DIM).transpose(1, 0, 2)
    grad_parts = lax.map(head_backward, (packed[0], packed[1], packed[2], attended, grad_attn, logsum))
    grad_packed = jnp.stack(grad_parts).transpose(2, 0, 1, 3).reshape(TOKENS, 3 * head_width).astype(jnp.bfloat16)
    grad_qkv = jnp.dot(grad_packed.T, normed, preferred_element_type=jnp.float32).reshape(3, head_width, D)
    grad_normed = jnp.dot(grad_packed, qkv_rows, preferred_element_type=jnp.float32)
    scaled = grad_normed * norm_gain
    grad_gain = lax.optimization_barrier(jnp.sum(grad_normed * inputs * inverse, axis=0))
    average = lax.optimization_barrier(jnp.mean(inputs * scaled, axis=1, keepdims=True))
    grad_frames = (back_sum + inverse * scaled - inputs * inverse ** 3 * average).astype(jnp.bfloat16).T
    return (block_out, grad_frames, grad_gain, grad_qkv, grad_out_proj, grad_kernel)
```

```python
import functools

import jax
import jax.numpy as jnp
from jax import lax
from jax.experimental import pallas as pl
from jax.experimental.pallas import tpu as pltpu
from jax.sharding import PartitionSpec as P

HEAD_DIM = 64
SIDE = 4
PAD = 16
F32 = jnp.float32
BF16 = jnp.bfloat16


def nn(a, b):
    return jnp.dot(a, b, preferred_element_type=F32)


def nt(a, b):
    return lax.dot_general(a, b, (((1,), (1,)), ((), ())), preferred_element_type=F32)


def tn(a, b):
    return lax.dot_general(a, b, (((0,), (0,)), ((), ())), preferred_element_type=F32)


VM = pl.BlockSpec(memory_space=pltpu.VMEM)


def fwd_kernel(heads, q_block, k_block, q_ref, k_ref, v_ref, o_ref, lse_ref, keys, top, total, acc):
    q_count, k_count = q_ref.shape[1], k_ref.shape[1]
    for h in range(heads):
        keys[h] = k_ref[h * HEAD_DIM : (h + 1) * HEAD_DIM, :].T

    def q_step(qi, carry):
        q_cols = pl.ds(pl.multiple_of(qi * q_block, q_block), q_block)
        top[...] = jnp.full_like(top, -jnp.inf)
        total[...] = jnp.zeros_like(total)
        acc[...] = jnp.zeros_like(acc)

        def k_step(ki, carry):
            k_rows = pl.ds(pl.multiple_of(ki * k_block, k_block), k_block)
            for h in range(heads):
                rows = slice(h * HEAD_DIM, (h + 1) * HEAD_DIM)
                one = slice(h, h + 1)
                scores = nn(keys[h, k_rows, :], q_ref[rows, q_cols])
                old = top[one, :]
                new = jnp.maximum(old, jnp.max(scores, axis=0, keepdims=True))
                weights = jnp.exp(scores - new)
                factor = jnp.exp(old - new)
                top[one, :] = new
                total[one, :] = total[one, :] * factor + jnp.sum(weights, axis=0, keepdims=True)
                acc[rows, :] = acc[rows, :] * factor + nn(v_ref[rows, k_rows], weights.astype(BF16))
            return carry

        lax.fori_loop(0, k_count // k_block, k_step, 0)
        for h in range(heads):
            rows = slice(h * HEAD_DIM, (h + 1) * HEAD_DIM)
            one = slice(h, h + 1)
            o_ref[rows, q_cols] = acc[rows, :] / total[one, :]
            lse_ref[one, q_cols] = top[one, :] + jnp.log(total[one, :])
        return carry

    lax.fori_loop(0, q_count // q_block, q_step, 0)


def attention(q, k, v, q_block=512, k_block=2048):
    width, q_count = q.shape
    k_count = k.shape[1]
    heads = width // HEAD_DIM
    return pl.pallas_call(
        functools.partial(fwd_kernel, heads, min(q_block, q_count), min(k_block, k_count)),
        out_shape=(
            jax.ShapeDtypeStruct((width, q_count), F32),
            jax.ShapeDtypeStruct((heads, q_count), F32),
        ),
        in_specs=[VM] * 3,
        out_specs=[VM] * 2,
        scratch_shapes=[
            pltpu.VMEM((heads, k_count, HEAD_DIM), BF16),
            pltpu.VMEM((heads, min(q_block, q_count)), F32),
            pltpu.VMEM((heads, min(q_block, q_count)), F32),
            pltpu.VMEM((width, min(q_block, q_count)), F32),
        ],
        cost_estimate=pl.CostEstimate(
            flops=16 * width * q_count * k_count,
            bytes_accessed=2 * width * (3 * q_count + 2 * k_count),
            transcendentals=heads * q_count * k_count,
        ),
        name="attn_fwd",
    )(q, k, v)


def bwd_kernel(
    heads, q_block, k_block, q_ref, k_ref, v_ref, g_ref, lse_ref, off_ref,
    dq_ref, dk_ref, dv_ref, keys, vals, dq, dk, dv,
):
    q_count, k_count = q_ref.shape[1], k_ref.shape[1]
    for h in range(heads):
        rows = slice(h * HEAD_DIM, (h + 1) * HEAD_DIM)
        keys[h] = k_ref[rows, :].T
        vals[h] = v_ref[rows, :].T
    dq[...] = jnp.zeros_like(dq)
    dk[...] = jnp.zeros_like(dk)
    dv[...] = jnp.zeros_like(dv)

    def q_step(qi, carry):
        q_cols = pl.ds(pl.multiple_of(qi * q_block, q_block), q_block)

        def k_step(ki, carry):
            k_rows = pl.ds(pl.multiple_of(ki * k_block, k_block), k_block)
            for h in range(heads):
                rows = slice(h * HEAD_DIM, (h + 1) * HEAD_DIM)
                one = slice(h, h + 1)
                q = q_ref[rows, q_cols]
                g = g_ref[rows, q_cols]
                scores = nn(keys[h, k_rows, :], q)
                prob = jnp.exp(scores - lse_ref[one, q_cols])
                grad_prob = nn(vals[h, k_rows, :], g)
                grad_score = (prob * (grad_prob - off_ref[one, q_cols])).astype(BF16)
                dq[rows, q_cols] += nn(k_ref[rows, k_rows], grad_score)
                dk[rows, k_rows] += nt(q, grad_score)
                dv[rows, k_rows] += nt(g, prob.astype(BF16))
            return carry

        lax.fori_loop(0, k_count // k_block, k_step, 0)
        return carry

    lax.fori_loop(0, q_count // q_block, q_step, 0)
    dq_ref[...] = (dq[...] * HEAD_DIM ** (-0.5)).astype(BF16)
    dk_ref[...] = dk[...].astype(BF16)
    dv_ref[...] = dv[...].astype(BF16)


def attention_grads(q, k, v, g, lse, off, q_block=1024, k_block=512):
    width, q_count = q.shape
    k_count = k.shape[1]
    heads = width // HEAD_DIM
    return pl.pallas_call(
        functools.partial(bwd_kernel, heads, min(q_block, q_count), min(k_block, k_count)),
        out_shape=(
            jax.ShapeDtypeStruct((width, q_count), BF16),
            jax.ShapeDtypeStruct((width, k_count), BF16),
            jax.ShapeDtypeStruct((width, k_count), BF16),
        ),
        in_specs=[VM] * 6,
        out_specs=[VM] * 3,
        scratch_shapes=[
            pltpu.VMEM((heads, k_count, HEAD_DIM), BF16),
            pltpu.VMEM((heads, k_count, HEAD_DIM), BF16),
            pltpu.VMEM((width, q_count), F32),
            pltpu.VMEM((width, k_count), F32),
            pltpu.VMEM((width, k_count), F32),
        ],
        cost_estimate=pl.CostEstimate(
            flops=40 * width * q_count * k_count,
            bytes_accessed=6 * width * (q_count + k_count),
            transcendentals=heads * q_count * k_count,
        ),
        name="attn_bwd",
    )(q, k, v, g, lse, off)


def fill(pad_ref, left_ref, own_ref, right_ref):
    count = own_ref.shape[1]
    slab = left_ref.shape[1]
    pad_ref[PAD : PAD + count, :] = own_ref[...].astype(F32).T
    pad_ref[:PAD, :] = left_ref[...].astype(F32).T[slab - PAD :, :]
    pad_ref[PAD + count :, :] = right_ref[...].astype(F32).T[:PAD, :]


def back_kernel(left_ref, own_ref, right_ref, taps_ref, sum_ref, cast_ref, pad_ref):
    count = own_ref.shape[1]
    fill(pad_ref, left_ref, own_ref, right_ref)
    taps = taps_ref.shape[0]
    half = taps // 2
    acc = pad_ref[PAD : PAD + count, :]
    for j in range(taps):
        start = PAD + half - j
        acc = acc + taps_ref[j : j + 1, :] * pad_ref[start : start + count, :]
    acc = acc.T
    sum_ref[...] = acc
    cast_ref[...] = acc.astype(BF16)


def conv_back(left, own, right, taps):
    width, count = own.shape
    return pl.pallas_call(
        back_kernel,
        out_shape=(
            jax.ShapeDtypeStruct((width, count), F32),
            jax.ShapeDtypeStruct((width, count), BF16),
        ),
        in_specs=[VM] * 4,
        out_specs=[VM] * 2,
        scratch_shapes=[pltpu.VMEM((count + 2 * PAD, width), F32)],
        cost_estimate=pl.CostEstimate(
            flops=8 * width * count * 31, bytes_accessed=8 * width * count, transcendentals=0
        ),
        name="conv_back",
    )(left, own, right, taps)


def conv_kernel_body(left_ref, own_ref, right_ref, up_ref, taps_ref, out_ref, grad_ref, pad_ref, upt_ref):
    count = own_ref.shape[1]
    fill(pad_ref, left_ref, own_ref, right_ref)
    upt_ref[...] = up_ref[...].astype(F32).T
    taps = taps_ref.shape[0]
    half = taps // 2
    acc = pad_ref[PAD : PAD + count, :]
    for j in range(taps):
        start = PAD + j - half
        part = pad_ref[start : start + count, :]
        acc = acc + taps_ref[j : j + 1, :] * part
        grad_ref[j : j + 1, :] = jnp.sum(upt_ref[...] * part, axis=0, keepdims=True)
    out_ref[...] = acc.T.astype(BF16)


def conv_forward(left, own, right, upstream, taps):
    width, count = own.shape
    return pl.pallas_call(
        conv_kernel_body,
        out_shape=(
            jax.ShapeDtypeStruct((width, count), BF16),
            jax.ShapeDtypeStruct((taps.shape[0], width), F32),
        ),
        in_specs=[VM] * 5,
        out_specs=[VM] * 2,
        scratch_shapes=[
            pltpu.VMEM((count + 2 * PAD, width), F32),
            pltpu.VMEM((count, width), F32),
        ],
        cost_estimate=pl.CostEstimate(
            flops=16 * width * count * 31, bytes_accessed=8 * width * count, transcendentals=0
        ),
        name="conv_fwd",
    )(left, own, right, upstream, taps)


def shift_x(a, by):
    pairs = [
        (z * SIDE + x, z * SIDE + (x + by) % SIDE) for z in range(SIDE) for x in range(SIDE)
    ]
    return lax.ppermute(a, "tm", pairs)


def shift_z(a, by):
    pairs = [
        (z * SIDE + x, ((z + by) % SIDE) * SIDE + x) for z in range(SIDE) for x in range(SIDE)
    ]
    return lax.ppermute(a, "tm", pairs)


def ring_gather(shift, a):
    return [a] + [shift(a, s) for s in range(1, SIDE)]


def ring_scatter(shift, blocks):
    terms = [blocks[0]] + [shift(blocks[s], -s) for s in range(1, SIDE)]
    return sum(t.astype(F32) for t in terms)


def halos(a, slab=128):
    count = lax.axis_size("tm")
    ends = count - 1
    left = lax.ppermute(a[:, a.shape[1] - slab :], "tm", [(i, i + 1) for i in range(ends)])
    right = lax.ppermute(a[:, :slab], "tm", [(i + 1, i) for i in range(ends)])
    return left, right


def shards(frames, norm_gain, w_qkv, w_out, conv_kernel, grad_out):
    own_width, rows = frames.shape
    head_cols, width = w_qkv.shape[1:]
    heads = head_cols // HEAD_DIM
    scale = HEAD_DIM ** (-0.5)
    members = lax.axis_size("tm")
    parts = lax.axis_size("mp")
    column_start = lax.axis_index("mp") * own_width
    taps = conv_kernel.shape[0]
    w_rows = w_qkv.reshape(3 * head_cols, width)

    inputs = lax.all_gather(frames, "mp", axis=0, tiled=True)
    up_left, up_right = halos(grad_out)
    back_sum, back_cast = conv_back(up_left, grad_out, up_right, conv_kernel)
    back_full = lax.all_gather(back_cast, "mp", axis=0, tiled=True)

    inputs32 = inputs.astype(F32)
    inverse = lax.rsqrt(jnp.mean(inputs32 * inputs32, axis=0, keepdims=True) + 1e-06)
    normed = (inputs32 * inverse * norm_gain[:, None]).astype(BF16)
    packed = nn(w_rows, normed).astype(BF16)
    queries = packed[:head_cols] * jnp.asarray(scale, BF16)

    keys_values = jnp.concatenate(ring_gather(shift_z, packed[head_cols:]), axis=1)
    group_q = jnp.concatenate(ring_gather(shift_x, queries), axis=1)
    group_k = keys_values[:head_cols]
    group_v = keys_values[head_cols:]

    part_out, part_lse = attention(group_q, group_k, group_v)

    grad_attn = nn(w_out, back_full).astype(BF16)
    group_g = jnp.concatenate(ring_gather(shift_x, grad_attn), axis=1)

    span = group_q.shape[1]
    part_off = jnp.sum(
        (part_out * group_g.astype(F32)).reshape(heads, HEAD_DIM, span), axis=1
    )
    stats = jnp.concatenate([part_lse, part_off], axis=0)
    peers = [stats] + [jnp.roll(shift_x(stats, s), s * rows, axis=1) for s in range(1, SIDE)]
    peers = jnp.stack(peers)
    lse_all, off_all = peers[:, :heads], peers[:, heads:]
    top = jnp.max(lse_all, axis=0)
    logsum = top + jnp.log(jnp.sum(jnp.exp(lse_all - top), axis=0))
    offset = jnp.sum(jnp.exp(lse_all - logsum) * off_all, axis=0)

    share = jnp.exp(part_lse - logsum)
    scaled_out = (
        (part_out.reshape(heads, HEAD_DIM, span) * share[:, None, :])
        .astype(BF16)
        .reshape(head_cols, span)
    )
    blocks = [scaled_out[:, r * rows : (r + 1) * rows] for r in range(SIDE)]
    attended = ring_scatter(shift_x, blocks).astype(BF16)

    part_dq, part_dk, part_dv = attention_grads(
        group_q, group_k, group_v, group_g, logsum, offset
    )

    projected = tn(w_out, attended).astype(BF16)
    mixed = lax.psum_scatter(projected, "mp", scatter_dimension=0, tiled=True)
    residual = (frames.astype(F32) + mixed.astype(F32)).astype(BF16)
    res_left, res_right = halos(residual)
    block_out, kernel_part = conv_forward(res_left, residual, res_right, grad_out, conv_kernel)
    out_proj_part = nt(attended, back_full).astype(BF16)

    def cut(a, r):
        return a[:, r * rows : (r + 1) * rows]

    grad_q = ring_scatter(shift_x, [cut(part_dq, r) for r in range(SIDE)])
    grad_kv = ring_scatter(
        shift_z,
        [jnp.concatenate([cut(part_dk, r), cut(part_dv, r)], axis=0) for r in range(SIDE)],
    )
    grad_packed = jnp.concatenate([grad_q.astype(BF16), grad_kv.astype(BF16)], axis=0)

    grad_normed = tn(w_rows, grad_packed)
    dots = jnp.sum(grad_packed.astype(F32) * packed.astype(F32), axis=0, keepdims=True) / width
    chunks = jnp.concatenate(
        [
            grad_normed.astype(BF16).reshape(parts, own_width, rows),
            jnp.broadcast_to(dots.astype(BF16)[None], (parts, PAD, rows)),
        ],
        axis=1,
    ).reshape(parts * (own_width + PAD), rows)
    summed = lax.psum_scatter(chunks, "mp", scatter_dimension=0, tiled=True).astype(F32)
    grad_own = summed[:own_width]
    dots_sum = summed[own_width : own_width + 1]

    qkv_part = nt(grad_packed, normed).astype(BF16)
    weight_part = jnp.concatenate([qkv_part, out_proj_part], axis=0)
    weight_rows = weight_part.shape[0]
    each = weight_rows // members
    exchanged = lax.all_to_all(
        weight_part.reshape(members, each, width), "tm", 0, 0, tiled=True
    )
    reduced = jnp.sum(exchanged.astype(F32), axis=0).astype(BF16)

    inputs_own = frames.astype(F32)
    gain_own = lax.dynamic_slice_in_dim(norm_gain, column_start, own_width, 0)[:, None]
    normed_own = inputs_own * inverse
    grad_frames = (
        back_sum + inverse * (grad_own * gain_own) - normed_own * inverse * dots_sum
    ).astype(BF16)
    gain_part = jnp.sum(grad_own * normed_own, axis=1)

    small = jnp.concatenate([kernel_part.reshape(-1), gain_part]).astype(BF16)
    small_rows = -(-small.shape[0] // width)
    extra = -(-small_rows // PAD) * PAD
    small = jnp.pad(small, (0, extra * width - small.shape[0])).reshape(extra, width)
    payload = jnp.concatenate([reduced, small], axis=0)
    spread = lax.all_to_all(
        jnp.broadcast_to(payload[None], (members, each + extra, width)), "tm", 0, 0, tiled=True
    )
    weights = spread[:, :each].reshape(weight_rows, width).astype(F32)
    small_sum = jnp.sum(spread[:, each:].astype(F32), axis=0).reshape(-1)
    kernel_size = taps * own_width
    return (
        block_out,
        grad_frames,
        small_sum[kernel_size : kernel_size + own_width],
        weights[: 3 * head_cols].reshape(3, head_cols, width),
        weights[3 * head_cols :],
        small_sum[:kernel_size].reshape(taps, own_width),
    )


def solution(mesh):
    return jax.shard_map(
        shards,
        mesh=mesh,
        in_specs=(
            P("mp", "tm"),
            P(),
            P(None, "mp", None),
            P("mp", None),
            P(None, "mp"),
            P("mp", "tm"),
        ),
        out_specs=(
            P("mp", "tm"),
            P("mp", "tm"),
            P("mp"),
            P(None, "mp", None),
            P("mp", None),
            P(None, "mp"),
        ),
        check_vma=False,
    )
```

```python
import functools

import jax
import jax.numpy as jnp
from jax import lax
from jax.experimental import pallas as pl
from jax.experimental.pallas import tpu as pltpu
from jax.sharding import PartitionSpec as P

HEAD_DIM = 64
SIDE = 4
PAD = 16
F32 = jnp.float32
BF16 = jnp.bfloat16


def nn(a, b):
    return jnp.dot(a, b, preferred_element_type=F32)


def nt(a, b):
    return lax.dot_general(a, b, (((1,), (1,)), ((), ())), preferred_element_type=F32)


def tn(a, b):
    return lax.dot_general(a, b, (((0,), (0,)), ((), ())), preferred_element_type=F32)


VM = pl.BlockSpec(memory_space=pltpu.VMEM)


def fill(pad_ref, left_ref, own_ref, right_ref):
    count = own_ref.shape[1]
    slab = left_ref.shape[1]
    pad_ref[PAD : PAD + count, :] = own_ref[...].astype(F32).T
    pad_ref[:PAD, :] = left_ref[...].astype(F32).T[slab - PAD :, :]
    pad_ref[PAD + count :, :] = right_ref[...].astype(F32).T[:PAD, :]


def back_kernel(left_ref, own_ref, right_ref, taps_ref, sum_ref, cast_ref, pad_ref):
    count = own_ref.shape[1]
    fill(pad_ref, left_ref, own_ref, right_ref)
    taps = taps_ref.shape[0]
    half = taps // 2
    acc = pad_ref[PAD : PAD + count, :]
    for j in range(taps):
        start = PAD + half - j
        acc = acc + taps_ref[j : j + 1, :] * pad_ref[start : start + count, :]
    acc = acc.T
    sum_ref[...] = acc
    cast_ref[...] = acc.astype(BF16)


def conv_back(left, own, right, taps):
    width, count = own.shape
    return pl.pallas_call(
        back_kernel,
        out_shape=(
            jax.ShapeDtypeStruct((width, count), F32),
            jax.ShapeDtypeStruct((width, count), BF16),
        ),
        in_specs=[VM] * 4,
        out_specs=[VM] * 2,
        scratch_shapes=[pltpu.VMEM((count + 2 * PAD, width), F32)],
        cost_estimate=pl.CostEstimate(
            flops=8 * width * count * 31, bytes_accessed=8 * width * count, transcendentals=0
        ),
        name="conv_back",
    )(left, own, right, taps)


def conv_kernel_body(left_ref, own_ref, right_ref, up_ref, taps_ref, out_ref, grad_ref, pad_ref, upt_ref):
    count = own_ref.shape[1]
    fill(pad_ref, left_ref, own_ref, right_ref)
    upt_ref[...] = up_ref[...].astype(F32).T
    taps = taps_ref.shape[0]
    half = taps // 2
    acc = pad_ref[PAD : PAD + count, :]
    for j in range(taps):
        start = PAD + j - half
        part = pad_ref[start : start + count, :]
        acc = acc + taps_ref[j : j + 1, :] * part
        grad_ref[j : j + 1, :] = jnp.sum(upt_ref[...] * part, axis=0, keepdims=True)
    out_ref[...] = acc.T.astype(BF16)


def conv_forward(left, own, right, upstream, taps):
    width, count = own.shape
    return pl.pallas_call(
        conv_kernel_body,
        out_shape=(
            jax.ShapeDtypeStruct((width, count), BF16),
            jax.ShapeDtypeStruct((taps.shape[0], width), F32),
        ),
        in_specs=[VM] * 5,
        out_specs=[VM] * 2,
        scratch_shapes=[
            pltpu.VMEM((count + 2 * PAD, width), F32),
            pltpu.VMEM((count, width), F32),
        ],
        cost_estimate=pl.CostEstimate(
            flops=16 * width * count * 31, bytes_accessed=8 * width * count, transcendentals=0
        ),
        name="conv_fwd",
    )(left, own, right, upstream, taps)


def shift_x(a, by):
    pairs = [
        (z * SIDE + x, z * SIDE + (x + by) % SIDE) for z in range(SIDE) for x in range(SIDE)
    ]
    return lax.ppermute(a, "tm", pairs)


def shift_z(a, by):
    pairs = [
        (z * SIDE + x, ((z + by) % SIDE) * SIDE + x) for z in range(SIDE) for x in range(SIDE)
    ]
    return lax.ppermute(a, "tm", pairs)


def halos(a, slab=128):
    count = lax.axis_size("tm")
    ends = count - 1
    left = lax.ppermute(a[:, a.shape[1] - slab :], "tm", [(i, i + 1) for i in range(ends)])
    right = lax.ppermute(a[:, :slab], "tm", [(i + 1, i) for i in range(ends)])
    return left, right


SM = pl.BlockSpec(memory_space=pltpu.SMEM)


def shift_y(a, by):
    count = lax.axis_size("mp") // 2
    pairs = [(y * 2 + c, ((y + by) % count) * 2 + c) for y in range(count) for c in range(2)]
    return lax.ppermute(a, "mp", pairs)


def swap_core(a):
    count = lax.axis_size("mp")
    return lax.ppermute(a, "mp", [(i, i ^ 1) for i in range(count)])


def call(body, name, outs, args, specs=None, scratch=(), flops=0, exps=0):
    out_shape = tuple(jax.ShapeDtypeStruct(s, t) for s, t in outs)
    moved = sum(a.size * a.dtype.itemsize for a in args)
    moved += sum(o.size * o.dtype.itemsize for o in out_shape)
    return pl.pallas_call(
        body,
        out_shape=out_shape,
        in_specs=specs or [VM] * len(args),
        out_specs=[VM] * len(outs),
        scratch_shapes=list(scratch),
        cost_estimate=pl.CostEstimate(flops=flops, bytes_accessed=moved, transcendentals=exps),
        name=name,
    )(*args)


def head_rows(h):
    return slice(h * HEAD_DIM, (h + 1) * HEAD_DIM)


def prep_body(pos_ref, w_ref, wo_ref, wq_out, wo_out, mixed, turned, turned_out):
    head_cols, width = wo_ref.shape
    heads = head_cols // HEAD_DIM
    for h in range(heads):
        for j in range(3):
            at = (h * 3 + j) * HEAD_DIM
            mixed[at : at + HEAD_DIM, :] = w_ref[j, head_rows(h), :]
    turned[...] = mixed[...].T
    turned_out[...] = wo_ref[...].T
    chunk = width // 8
    for r in range(8):
        rows = pl.ds(pl.multiple_of(pos_ref[r] * chunk, chunk), chunk)
        wq_out[r * chunk : (r + 1) * chunk, :] = turned[rows, :]
        wo_out[r * chunk : (r + 1) * chunk, :] = turned_out[rows, :]


def norm_body(pos_ref, b0, b1, b2, b3, other, gain_ref, w_ref, normed_out, inv_out, q_out, kv_out):
    own = [b0, b1, b2, b3]
    chunk, rows = b0.shape
    width = normed_out.shape[0]

    def block(r):
        part = own[r][...] if r < 4 else other[(r - 4) * chunk : (r - 3) * chunk, :]
        return part.astype(F32)

    total = jnp.zeros((1, rows), F32)
    for r in range(8):
        x = block(r)
        total = total + jnp.sum(x * x, axis=0, keepdims=True)
    inverse = lax.rsqrt(total / width + 1e-06)
    inv_out[...] = inverse
    for r in range(8):
        at = pl.ds(pl.multiple_of(pos_ref[r] * chunk, chunk), chunk)
        normed_out[at, :] = (block(r) * inverse * gain_ref[at, :]).astype(BF16)
    normed = normed_out[...]
    q_out[...] = nn(w_ref[0], normed).astype(BF16) * jnp.asarray(HEAD_DIM ** (-0.5), BF16)
    head_cols = q_out.shape[0]
    for j in (1, 2):
        kv_out[(j - 1) * head_cols : j * head_cols, :] = nn(w_ref[j], normed).astype(BF16)


def back_arrange_body(pos_ref, b0, b1, b2, b3, other, wo_ref, full_out, grad_out):
    own = [b0, b1, b2, b3]
    chunk = b0.shape[0]
    for r in range(8):
        at = pl.ds(pl.multiple_of(pos_ref[r] * chunk, chunk), chunk)
        full_out[at, :] = own[r][...] if r < 4 else other[(r - 4) * chunk : (r - 3) * chunk, :]
    grad_out[...] = nn(wo_ref[...], full_out[...]).astype(BF16)


def fwd_loop_body(heads, *refs):
    q_refs, kv_refs = refs[:SIDE], refs[SIDE : 2 * SIDE]
    o_ref, lse_ref, keys, vals, queries = refs[2 * SIDE :]
    rows = q_refs[0].shape[1]
    width = heads * HEAD_DIM
    for r in range(SIDE):
        cols = slice(r * rows, (r + 1) * rows)
        vals[:, cols] = kv_refs[r][width:, :]
        queries[:, cols] = q_refs[r][...]
        for h in range(heads):
            keys[h, cols, :] = kv_refs[r][head_rows(h), :].T

    def step(r, carry):
        cols = pl.ds(pl.multiple_of(r * rows, rows), rows)
        for h in range(heads):
            at = head_rows(h)
            scores = nn(keys[h], queries[at, cols])
            top = jnp.max(scores, axis=0, keepdims=True)
            weights = jnp.exp(scores - top)
            total = jnp.sum(weights, axis=0, keepdims=True)
            o_ref[at, cols] = nn(vals[at, :], weights.astype(BF16)) / total
            lse_ref[h : h + 1, cols] = top + jnp.log(total)
        return carry

    lax.fori_loop(0, SIDE, step, 0)


def stats_body(heads, o_ref, lse_ref, *refs):
    g_refs, out_ref = refs[:SIDE], refs[SIDE]
    rows = g_refs[0].shape[1]
    out_ref[...] = jnp.zeros_like(out_ref)
    out_ref[:heads, :] = lse_ref[...]
    for r in range(SIDE):
        cols = slice(r * rows, (r + 1) * rows)
        for h in range(heads):
            at = head_rows(h)
            out_ref[heads + h : heads + h + 1, cols] = jnp.sum(
                o_ref[at, cols] * g_refs[r][at, :].astype(F32), axis=0, keepdims=True
            )


def combine_body(heads, o_ref, *refs):
    peers, outs = refs[:SIDE], refs[SIDE:]
    lse_out, off_out, blocks = outs[0], outs[1], outs[2:]
    rows = o_ref.shape[1] // SIDE
    for r in range(SIDE):
        cols = slice(r * rows, (r + 1) * rows)
        theirs = []
        for s in range(SIDE):
            at = (r - s) % SIDE
            theirs.append(peers[s][:, at * rows : (at + 1) * rows])
        lse = [t[:heads] for t in theirs]
        off = [t[heads : 2 * heads] for t in theirs]
        top = jnp.maximum(jnp.maximum(lse[0], lse[1]), jnp.maximum(lse[2], lse[3]))
        logsum = top + jnp.log(sum(jnp.exp(v - top) for v in lse))
        shares = [jnp.exp(v - logsum) for v in lse]
        lse_out[:heads, cols] = logsum
        off_out[:heads, cols] = sum(w * v for w, v in zip(shares, off))
        for h in range(heads):
            at = head_rows(h)
            blocks[r][at, :] = (o_ref[at, cols] * shares[0][h : h + 1]).astype(BF16)


def bwd_body(h, heads, q_block, k_block, *refs):
    q_refs, kv_refs, g_refs = refs[:SIDE], refs[SIDE : 2 * SIDE], refs[2 * SIDE : 3 * SIDE]
    lse_ref, off_ref = refs[3 * SIDE : 3 * SIDE + 2]
    dq_refs = refs[3 * SIDE + 2 : 4 * SIDE + 2]
    dkv_refs = refs[4 * SIDE + 2 : 5 * SIDE + 2]
    keys, vals, kt, qt, gt, stat, dq, dk, dv = refs[5 * SIDE + 2 :]
    rows = q_refs[0].shape[1]
    span = SIDE * rows
    at = head_rows(h)
    v_at = head_rows(heads + h)
    for r in range(SIDE):
        cols = slice(r * rows, (r + 1) * rows)
        qt[:, cols] = q_refs[r][at, :]
        gt[:, cols] = g_refs[r][at, :]
        kt[:, cols] = kv_refs[r][at, :]
        keys[cols, :] = kv_refs[r][at, :].T
        vals[cols, :] = kv_refs[r][v_at, :].T
    stat[0:1, :] = lse_ref[h : h + 1, :]
    stat[1:2, :] = off_ref[h : h + 1, :]
    dk[...] = jnp.zeros_like(dk)
    dv[...] = jnp.zeros_like(dv)
    dq[...] = jnp.zeros_like(dq)

    def k_step(ki, carry):
        k_rows = pl.ds(pl.multiple_of(ki * k_block, k_block), k_block)
        for qi in range(span // q_block):
            q_cols = slice(qi * q_block, (qi + 1) * q_block)
            q = qt[:, q_cols]
            g = gt[:, q_cols]
            scores = nn(keys[k_rows, :], q)
            prob = jnp.exp(scores - stat[0:1, q_cols])
            grad_prob = nn(vals[k_rows, :], g)
            grad_score = (prob * (grad_prob - stat[1:2, q_cols])).astype(BF16)
            dq[:, q_cols] += nn(kt[:, k_rows], grad_score)
            dk[:, k_rows] += nt(q, grad_score)
            dv[:, k_rows] += nt(g, prob.astype(BF16))
        return carry

    lax.fori_loop(0, span // k_block, k_step, 0)
    for r in range(SIDE):
        cols = slice(r * rows, (r + 1) * rows)
        dq_refs[r][...] = (dq[:, cols] * HEAD_DIM ** (-0.5)).astype(BF16)
        dkv_refs[r][:HEAD_DIM, :] = dk[:, cols].astype(BF16)
        dkv_refs[r][HEAD_DIM:, :] = dv[:, cols].astype(BF16)


def sum_terms(refs):
    return sum(t[...].astype(F32) for t in refs)


def proj_body(*refs):
    terms, wo_ref = refs[:SIDE], refs[SIDE]
    att_out, own_out, other_out = refs[SIDE + 1 :]
    attended = sum_terms(terms).astype(BF16)
    att_out[...] = attended
    half = own_out.shape[0]
    other_out[...] = nn(wo_ref[half:, :], attended).astype(BF16)
    own_out[...] = nn(wo_ref[:half, :], attended)


def pair_body(own_ref, got_ref, *outs):
    chunk = outs[0].shape[0]
    for d in range(SIDE):
        at = slice(d * chunk, (d + 1) * chunk)
        outs[d][...] = (own_ref[at, :] + got_ref[at, :].astype(F32)).astype(BF16)


def packed_grads_body(*refs):
    dq, dkv, out = refs[:SIDE], refs[SIDE : 2 * SIDE], refs[2 * SIDE]
    out[:HEAD_DIM, :] = sum_terms(dq).astype(BF16)
    out[HEAD_DIM:, :] = sum_terms(dkv).astype(BF16)


def first_weights_body(*refs):
    dq, dkv = refs[:SIDE], refs[SIDE : 2 * SIDE]
    normed_ref, att_ref, full_ref, gp_out, part_out = refs[2 * SIDE :]
    packed_grads_body(*dq, *dkv, gp_out)
    rows = gp_out.shape[0]
    part_out[:rows, :] = nt(gp_out[...], normed_ref[...]).astype(BF16)
    part_out[rows:, :] = nt(att_ref[...], full_ref[...]).astype(BF16)


def split(v):
    high = v.astype(BF16)
    return high, (v - high.astype(F32)).astype(BF16)


def grads_body(heads, width, *refs):
    gp0 = refs[0]
    terms = refs[1 : 1 + (heads - 1) * 2 * SIDE]
    q_ref, kv_ref, wq_ref, gp_out, own_out, other_out, all_gp = refs[1 + (heads - 1) * 2 * SIDE :]
    size = 3 * HEAD_DIM
    all_gp[:size, :] = gp0[...]
    for h in range(1, heads):
        some = terms[(h - 1) * 2 * SIDE : h * 2 * SIDE]
        at = h * size
        all_gp[at : at + HEAD_DIM, :] = sum_terms(some[:SIDE]).astype(BF16)
        all_gp[at + HEAD_DIM : at + size, :] = sum_terms(some[SIDE:]).astype(BF16)
    gp_out[...] = all_gp[size:, :]
    dots = jnp.zeros((1, q_ref.shape[1]), F32)
    for h in range(heads):
        at = h * size
        gp = all_gp[at : at + size, :].astype(F32)
        q = q_ref[head_rows(h), :].astype(F32) * HEAD_DIM**0.5
        k = kv_ref[head_rows(h), :].astype(F32)
        v = kv_ref[head_rows(heads + h), :].astype(F32)
        for j, held in enumerate((q, k, v)):
            dots = dots + jnp.sum(
                gp[j * HEAD_DIM : (j + 1) * HEAD_DIM] * held, axis=0, keepdims=True
            )
    dots = dots / width
    half = wq_ref.shape[0] // 2
    other_out[:half, :] = nn(wq_ref[half:, :], all_gp[...]).astype(BF16)
    high, low = split(dots)
    other_out[half:, :] = jnp.concatenate(
        [high, low, jnp.zeros((PAD - 2, dots.shape[1]), BF16)], axis=0
    )
    own_out[:half, :] = nn(wq_ref[:half, :], all_gp[...])
    own_out[half:, :] = jnp.broadcast_to(dots, (8, dots.shape[1]))


def grads_pair_body(own_ref, got_ref, *outs):
    chunk = outs[0].shape[0] - PAD
    half = SIDE * chunk
    got = got_ref[half:, :].astype(F32)
    dots = own_ref[half : half + 1, :] + got[0:1] + got[1:2]
    high, low = split(dots)
    tail = jnp.concatenate([high, low, jnp.zeros((PAD - 2, dots.shape[1]), BF16)], axis=0)
    for d in range(SIDE):
        at = slice(d * chunk, (d + 1) * chunk)
        outs[d][:chunk, :] = (own_ref[at, :] + got_ref[at, :].astype(F32)).astype(BF16)
        outs[d][chunk:, :] = tail


def later_weights_body(gp_ref, normed_ref, part_out):
    part_out[...] = nt(gp_ref[...], normed_ref[...]).astype(BF16)


def spread_body(in_ref, out_ref):
    members, rows, width = in_ref.shape
    total = sum(in_ref[i].astype(F32) for i in range(members)).astype(BF16)
    for i in range(members):
        out_ref[i] = total


def spread_small_body(in_ref, small_ref, out_ref):
    members, rows, width = in_ref.shape
    total = sum(in_ref[i].astype(F32) for i in range(members)).astype(BF16)
    small = small_ref[...]
    for i in range(members):
        out_ref[i, :, :width] = total
        out_ref[i, :, width:] = small


def finish_body(heads, first_ref, later_ref, qkv_out, small_out):
    members, each, _ = first_ref.shape
    width = qkv_out.shape[2]
    step = 8
    for h in range(heads):
        for j in range(3):
            for i in range(HEAD_DIM // step):
                if h == 0:
                    row = j * HEAD_DIM + i * step
                    src = first_ref
                else:
                    row = ((h - 1) * 3 + j) * HEAD_DIM + i * step
                    src = later_ref
                m, k = divmod(row, each)
                at = h * HEAD_DIM + i * step
                qkv_out[j, at : at + step, :] = src[m, k : k + step, :width].astype(F32)
    small_out[...] = sum(later_ref[m, :, width:].astype(F32) for m in range(members))


def tie(value, *others):
    return lax.optimization_barrier((value, *others))[0]


def shards(frames, norm_gain, w_qkv, w_out, conv_kernel, grad_out):
    own_width, rows = frames.shape
    head_cols, width = w_qkv.shape[1:]
    heads = head_cols // HEAD_DIM
    members = lax.axis_size("tm")
    taps = conv_kernel.shape[0]
    span = SIDE * rows
    y, core = lax.axis_index("mp") // 2, lax.axis_index("mp") % 2
    steps = jnp.arange(SIDE, dtype=jnp.int32)
    cores = jnp.stack([core, 1 - core]).astype(jnp.int32)
    came = ((((y - steps + SIDE) % SIDE) * 2)[None, :] + cores[:, None]).reshape(-1)
    goes = ((((y + steps) % SIDE) * 2)[None, :] + cores[:, None]).reshape(-1)

    def gather_mp(a):
        blocks = [a] + [shift_y(a, d) for d in range(1, SIDE)]
        return blocks + [swap_core(jnp.concatenate(blocks, axis=0))]

    in_blocks = gather_mp(frames)
    up_left, up_right = halos(grad_out)
    back_sum, back_cast = conv_back(up_left, grad_out, up_right, conv_kernel)
    wq_rel, wo_rel = call(
        prep_body, "prep",
        [((width, 3 * head_cols), BF16), ((width, head_cols), BF16)],
        [goes, w_qkv, w_out], [SM, VM, VM],
        [
            pltpu.VMEM((3 * head_cols, width), BF16),
            pltpu.VMEM((width, 3 * head_cols), BF16),
            pltpu.VMEM((width, head_cols), BF16),
        ],
    )
    normed, inverse, queries, keys_values = call(
        norm_body, "norm_qkv",
        [((width, rows), BF16), ((1, rows), F32), ((head_cols, rows), BF16), ((2 * head_cols, rows), BF16)],
        [came, *in_blocks, norm_gain[:, None], w_qkv], [SM] + [VM] * 7,
        flops=2 * 3 * head_cols * width * rows,
    )
    group_kv = [keys_values] + [shift_z(keys_values, s) for s in range(1, SIDE)]
    group_q = [queries] + [shift_x(queries, s) for s in range(1, SIDE)]

    back_blocks = gather_mp(tie(back_cast, *in_blocks[1:4]))
    back_full, grad_attn = call(
        back_arrange_body, "back_arrange",
        [((width, rows), BF16), ((head_cols, rows), BF16)],
        [came, *back_blocks, w_out], [SM] + [VM] * 6,
        flops=2 * head_cols * width * rows,
    )
    group_g = [grad_attn] + [shift_x(grad_attn, s) for s in range(1, SIDE)]

    part_out, part_lse = call(
        functools.partial(fwd_loop_body, heads), "attn_fwd",
        [((head_cols, span), F32), ((heads, span), F32)],
        [*group_q, *group_kv], None,
        [
            pltpu.VMEM((heads, span, HEAD_DIM), BF16),
            pltpu.VMEM((head_cols, span), BF16),
            pltpu.VMEM((head_cols, span), BF16),
        ],
        flops=16 * head_cols * span * span, exps=heads * span * span,
    )
    (stats,) = call(
        functools.partial(stats_body, heads), "stats",
        [((8, span), F32)], [part_out, part_lse, *group_g],
    )
    peers = [stats] + [shift_x(stats, s) for s in range(1, SIDE)]
    logsum, offset, *out_blocks = call(
        functools.partial(combine_body, heads), "combine",
        [((8, span), F32), ((8, span), F32)] + [((head_cols, rows), BF16)] * SIDE,
        [part_out, *peers],
    )

    def head_grads(h, logsum):
        outs = call(
            functools.partial(bwd_body, h, heads, min(1024, span), min(512, span)), f"attn_bwd{h}",
            [((HEAD_DIM, rows), BF16)] * SIDE + [((2 * HEAD_DIM, rows), BF16)] * SIDE,
            [*group_q, *group_kv, *group_g, logsum, offset], None,
            [pltpu.VMEM((span, HEAD_DIM), BF16)] * 2
            + [pltpu.VMEM((HEAD_DIM, span), BF16)] * 3
            + [pltpu.VMEM((8, span), F32)]
            + [pltpu.VMEM((HEAD_DIM, span), F32)] * 3,
            flops=40 * HEAD_DIM * span * span, exps=span * span,
        )
        return outs[:SIDE], outs[SIDE:]

    def ring_terms(grads):
        dq, dkv = grads
        return (
            [dq[0]] + [shift_x(dq[s], -s) for s in range(1, SIDE)]
            + [dkv[0]] + [shift_z(dkv[s], -s) for s in range(1, SIDE)]
        )

    def scatter_mp(blocks):
        return [blocks[0]] + [shift_y(blocks[d], d) for d in range(1, SIDE)]

    out_terms = [out_blocks[0]] + [shift_x(out_blocks[s], -s) for s in range(1, SIDE)]
    grads0 = head_grads(0, logsum)
    terms0 = ring_terms(grads0)

    half = SIDE * own_width
    attended, proj_own, proj_other = call(
        proj_body, "proj",
        [((head_cols, rows), BF16), ((half, rows), F32), ((half, rows), BF16)],
        [tie(out_terms[0], *grads0[0]), *out_terms[1:], wo_rel],
        flops=2 * head_cols * width * rows,
    )
    proj_blocks = call(
        pair_body, "proj_pair", [((own_width, rows), BF16)] * SIDE, [proj_own, swap_core(proj_other)]
    )
    proj_terms = scatter_mp(proj_blocks)

    grads1 = head_grads(1, tie(logsum, *proj_blocks))
    terms1 = ring_terms(grads1)

    gp0, first_part = call(
        first_weights_body, "first_weights",
        [((3 * HEAD_DIM, rows), BF16), ((3 * HEAD_DIM + head_cols, width), BF16)],
        [tie(terms0[0], *grads1[0]), *terms0[1:], normed, attended, back_full],
        flops=2 * (3 * HEAD_DIM + head_cols) * width * rows,
    )
    each = first_part.shape[0] // members
    first_got = lax.all_to_all(
        first_part.reshape(members, each, width), "tm", 0, 0, tiled=True
    )
    mixed = sum(t.astype(F32) for t in [tie(proj_terms[0], *grads1[0])] + proj_terms[1:])
    residual = (frames.astype(F32) + mixed).astype(BF16)
    res_left, res_right = halos(residual)

    grads2 = head_grads(2, tie(logsum, first_part, residual))
    terms2 = ring_terms(grads2)
    block_out, kernel_part = conv_forward(
        res_left, tie(residual, *grads2[0]), res_right, grad_out, conv_kernel
    )

    later_gp, gn_own, gn_other = call(
        functools.partial(grads_body, heads, width), "packed_grads",
        [
            ((3 * HEAD_DIM * (heads - 1), rows), BF16),
            ((half + 8, rows), F32),
            ((half + PAD, rows), BF16),
        ],
        [gp0, *terms1, *terms2, queries, keys_values, wq_rel], None,
        [pltpu.VMEM((3 * head_cols, rows), BF16)],
        flops=2 * 3 * head_cols * width * rows,
    )
    gn_blocks = call(
        grads_pair_body, "grads_pair", [((own_width + PAD, rows), BF16)] * SIDE,
        [gn_own, swap_core(gn_other)],
    )
    gn_terms = scatter_mp(gn_blocks)
    (later_part,) = call(
        later_weights_body, "later_weights", [((3 * HEAD_DIM * (heads - 1), width), BF16)],
        [later_gp, normed], flops=2 * 3 * HEAD_DIM * (heads - 1) * width * rows,
    )
    later_each = later_part.shape[0] // members
    later_got = lax.all_to_all(
        later_part.reshape(members, later_each, width), "tm", 0, 0, tiled=True
    )
    (first_spread,) = call(
        spread_body, "first_spread", [((members, each, width), BF16)], [first_got]
    )
    first_all = lax.all_to_all(first_spread, "tm", 0, 0, tiled=True)

    summed = sum(t.astype(F32) for t in gn_terms)
    grad_own = summed[:own_width]
    dots = summed[own_width : own_width + 1] + summed[own_width + 1 : own_width + 2]
    column_start = lax.axis_index("mp") * own_width
    gain_own = lax.dynamic_slice_in_dim(norm_gain, column_start, own_width, 0)[:, None]
    normed_own = frames.astype(F32) * inverse
    grad_frames = (
        back_sum + inverse * (grad_own * gain_own) - normed_own * inverse * dots
    ).astype(BF16)
    gain_part = jnp.sum(grad_own * normed_own, axis=1)
    small = jnp.concatenate([kernel_part.astype(BF16), gain_part.astype(BF16)[None]], axis=0)
    small_cols = small.size // later_each
    (later_spread,) = call(
        spread_small_body, "later_spread", [((members, later_each, width + small_cols), BF16)],
        [later_got, small.reshape(later_each, small_cols)],
    )
    later_all = lax.all_to_all(later_spread, "tm", 0, 0, tiled=True)
    out_grads = first_all.reshape(-1, width)[3 * HEAD_DIM :].astype(F32)
    qkv_grads, small_sum = call(
        functools.partial(finish_body, heads), "finish",
        [((3, head_cols, width), F32), ((later_each, small_cols), F32)], [first_all, later_all],
    )
    small_sum = small_sum.reshape(taps + 1, own_width)
    return block_out, grad_frames, small_sum[taps], qkv_grads, out_grads, small_sum[:taps]


def solution(mesh):
    return jax.shard_map(
        shards,
        mesh=mesh,
        in_specs=(
            P("mp", "tm"),
            P(),
            P(None, "mp", None),
            P("mp", None),
            P(None, "mp"),
            P("mp", "tm"),
        ),
        out_specs=(
            P("mp", "tm"),
            P("mp", "tm"),
            P("mp"),
            P(None, "mp", None),
            P("mp", None),
            P(None, "mp"),
        ),
        check_vma=False,
    )
```

```python
import functools

import jax
import jax.numpy as jnp
from jax import lax
from jax.experimental import pallas as pl
from jax.experimental.pallas import tpu as pltpu
from jax.sharding import PartitionSpec as P

HEAD_DIM = 64
SIDE = 4
PAD = 16
F32 = jnp.float32
BF16 = jnp.bfloat16


def nn(a, b):
    return jnp.dot(a, b, preferred_element_type=F32)


def nt(a, b):
    return lax.dot_general(a, b, (((1,), (1,)), ((), ())), preferred_element_type=F32)


def tn(a, b):
    return lax.dot_general(a, b, (((0,), (0,)), ((), ())), preferred_element_type=F32)


VM = pl.BlockSpec(memory_space=pltpu.VMEM)


STEP = 64


def fill(pad_ref, left_ref, own_ref, right_ref):
    count = own_ref.shape[1]
    slab = left_ref.shape[1]
    pad_ref[PAD : PAD + count, :] = own_ref[...].astype(F32).T
    pad_ref[:PAD, :] = left_ref[...].astype(F32).T[slab - PAD :, :]
    pad_ref[PAD + count :, :] = right_ref[...].astype(F32).T[:PAD, :]


def back_kernel(left_ref, own_ref, right_ref, taps_ref, sum_ref, cast_ref, pad_ref, acc_ref, near):
    count = own_ref.shape[1]
    fill(pad_ref, left_ref, own_ref, right_ref)
    taps = taps_ref.shape[0]
    half = taps // 2

    def step(i, carry):
        base = pl.multiple_of(i * STEP, STEP)
        near[...] = pad_ref[pl.ds(base, STEP + 2 * PAD), :]
        acc = near[PAD : PAD + STEP, :]
        for j in range(taps):
            start = PAD + half - j
            acc = acc + taps_ref[j : j + 1, :] * near[start : start + STEP, :]
        acc_ref[pl.ds(base, STEP), :] = acc
        return carry

    lax.fori_loop(0, count // STEP, step, 0)
    acc = acc_ref[...].T
    sum_ref[...] = acc
    cast_ref[...] = acc.astype(BF16)


def conv_body(left_ref, own_ref, right_ref, up_ref, taps_ref, out_ref, grad_ref, pad_ref, upt_ref, sums, near):
    count = own_ref.shape[1]
    fill(pad_ref, left_ref, own_ref, right_ref)
    upt_ref[...] = up_ref[...].astype(F32).T
    taps = taps_ref.shape[0]
    half = taps // 2
    sums[...] = jnp.zeros_like(sums)

    def step(i, carry):
        base = pl.multiple_of(i * STEP, STEP)
        near[...] = pad_ref[pl.ds(base, STEP + 2 * PAD), :]
        acc = near[PAD : PAD + STEP, :]
        up = upt_ref[pl.ds(base, STEP), :]
        for j in range(taps):
            start = PAD + j - half
            part = near[start : start + STEP, :]
            acc = acc + taps_ref[j : j + 1, :] * part
            prod = up * part
            sums[j] += sum(prod[8 * s : 8 * s + 8] for s in range(STEP // 8))
        upt_ref[pl.ds(base, STEP), :] = acc
        return carry

    lax.fori_loop(0, count // STEP, step, 0)
    for j in range(taps):
        grad_ref[j : j + 1, :] = jnp.sum(sums[j], axis=0, keepdims=True)
    out_ref[...] = upt_ref[...].T.astype(BF16)


def shift_x(a, by):
    pairs = [
        (z * SIDE + x, z * SIDE + (x + by) % SIDE) for z in range(SIDE) for x in range(SIDE)
    ]
    return lax.ppermute(a, "tm", pairs)


def shift_z(a, by):
    pairs = [
        (z * SIDE + x, ((z + by) % SIDE) * SIDE + x) for z in range(SIDE) for x in range(SIDE)
    ]
    return lax.ppermute(a, "tm", pairs)


def halos(a, slab=128):
    count = lax.axis_size("tm")
    ends = count - 1
    left = lax.ppermute(a[:, a.shape[1] - slab :], "tm", [(i, i + 1) for i in range(ends)])
    right = lax.ppermute(a[:, :slab], "tm", [(i + 1, i) for i in range(ends)])
    return left, right


SM = pl.BlockSpec(memory_space=pltpu.SMEM)


def shift_y(a, by):
    count = lax.axis_size("mp") // 2
    pairs = [(y * 2 + c, ((y + by) % count) * 2 + c) for y in range(count) for c in range(2)]
    return lax.ppermute(a, "mp", pairs)


def swap_core(a):
    count = lax.axis_size("mp")
    return lax.ppermute(a, "mp", [(i, i ^ 1) for i in range(count)])


def call(body, name, outs, args, specs=None, scratch=(), flops=0, exps=0):
    out_shape = tuple(jax.ShapeDtypeStruct(s, t) for s, t in outs)
    moved = sum(a.size * a.dtype.itemsize for a in args)
    moved += sum(o.size * o.dtype.itemsize for o in out_shape)
    return pl.pallas_call(
        body,
        out_shape=out_shape,
        in_specs=specs or [VM] * len(args),
        out_specs=[VM] * len(outs),
        scratch_shapes=list(scratch),
        cost_estimate=pl.CostEstimate(flops=flops, bytes_accessed=moved, transcendentals=exps),
        name=name,
    )(*args)


def head_rows(h):
    return slice(h * HEAD_DIM, (h + 1) * HEAD_DIM)


def prep_body(pos_ref, w_ref, wo_ref, wq_out, wo_out, mixed, turned, turned_out):
    head_cols, width = wo_ref.shape
    heads = head_cols // HEAD_DIM
    for h in range(heads):
        for j in range(3):
            at = (h * 3 + j) * HEAD_DIM
            mixed[at : at + HEAD_DIM, :] = w_ref[j, head_rows(h), :]
    turned[...] = mixed[...].T
    turned_out[...] = wo_ref[...].T
    chunk = width // 8
    for r in range(8):
        rows = pl.ds(pl.multiple_of(pos_ref[r] * chunk, chunk), chunk)
        wq_out[r * chunk : (r + 1) * chunk, :] = turned[rows, :]
        wo_out[r * chunk : (r + 1) * chunk, :] = turned_out[rows, :]


def norm_body(pos_ref, b0, b1, b2, b3, other, gain_ref, w_ref, normed_out, inv_out, q_out, kv_out):
    own = [b0, b1, b2, b3]
    chunk, rows = b0.shape
    width = normed_out.shape[0]

    def block(r):
        part = own[r][...] if r < 4 else other[(r - 4) * chunk : (r - 3) * chunk, :]
        return part.astype(F32)

    total = jnp.zeros((1, rows), F32)
    for r in range(8):
        x = block(r)
        total = total + jnp.sum(x * x, axis=0, keepdims=True)
    inverse = lax.rsqrt(total / width + 1e-06)
    inv_out[...] = inverse
    for r in range(8):
        at = pl.ds(pl.multiple_of(pos_ref[r] * chunk, chunk), chunk)
        normed_out[at, :] = (block(r) * inverse * gain_ref[at, :]).astype(BF16)
    normed = normed_out[...]
    q_out[...] = nn(w_ref[0], normed).astype(BF16) * jnp.asarray(HEAD_DIM ** (-0.5), BF16)
    head_cols = q_out.shape[0]
    for j in (1, 2):
        kv_out[(j - 1) * head_cols : j * head_cols, :] = nn(w_ref[j], normed).astype(BF16)


def back_arrange_body(pos_ref, b0, b1, b2, b3, other, wo_ref, full_out, grad_out):
    own = [b0, b1, b2, b3]
    chunk = b0.shape[0]
    for r in range(8):
        at = pl.ds(pl.multiple_of(pos_ref[r] * chunk, chunk), chunk)
        full_out[at, :] = own[r][...] if r < 4 else other[(r - 4) * chunk : (r - 3) * chunk, :]
    grad_out[...] = nn(wo_ref[...], full_out[...]).astype(BF16)


def fwd_loop_body(heads, *refs):
    q_refs, kv_refs = refs[:SIDE], refs[SIDE : 2 * SIDE]
    o_ref, lse_ref, keys, vals, queries = refs[2 * SIDE :]
    rows = q_refs[0].shape[1]
    width = heads * HEAD_DIM
    for r in range(SIDE):
        cols = slice(r * rows, (r + 1) * rows)
        vals[:, cols] = kv_refs[r][width:, :]
        queries[:, cols] = q_refs[r][...]
        for h in range(heads):
            keys[h, cols, :] = kv_refs[r][head_rows(h), :].T

    def step(r, carry):
        cols = pl.ds(pl.multiple_of(r * rows, rows), rows)
        for h in range(heads):
            at = head_rows(h)
            scores = nn(keys[h], queries[at, cols])
            top = jnp.max(scores, axis=0, keepdims=True)
            weights = jnp.exp(scores - top)
            total = jnp.sum(weights, axis=0, keepdims=True)
            o_ref[at, cols] = nn(vals[at, :], weights.astype(BF16)) / total
            lse_ref[h : h + 1, cols] = top + jnp.log(total)
        return carry

    lax.fori_loop(0, SIDE, step, 0)


def stats_body(heads, o_ref, lse_ref, *refs):
    g_refs, out_ref = refs[:SIDE], refs[SIDE]
    rows = g_refs[0].shape[1]
    out_ref[...] = jnp.zeros_like(out_ref)
    out_ref[:heads, :] = lse_ref[...]
    for r in range(SIDE):
        cols = slice(r * rows, (r + 1) * rows)
        for h in range(heads):
            at = head_rows(h)
            out_ref[heads + h : heads + h + 1, cols] = jnp.sum(
                o_ref[at, cols] * g_refs[r][at, :].astype(F32), axis=0, keepdims=True
            )


def combine_body(heads, o_ref, *refs):
    peers, outs = refs[:SIDE], refs[SIDE:]
    lse_out, off_out, blocks = outs[0], outs[1], outs[2:]
    rows = o_ref.shape[1] // SIDE
    for r in range(SIDE):
        cols = slice(r * rows, (r + 1) * rows)
        theirs = []
        for s in range(SIDE):
            at = (r - s) % SIDE
            theirs.append(peers[s][:, at * rows : (at + 1) * rows])
        lse = [t[:heads] for t in theirs]
        off = [t[heads : 2 * heads] for t in theirs]
        top = jnp.maximum(jnp.maximum(lse[0], lse[1]), jnp.maximum(lse[2], lse[3]))
        logsum = top + jnp.log(sum(jnp.exp(v - top) for v in lse))
        shares = [jnp.exp(v - logsum) for v in lse]
        lse_out[:heads, cols] = logsum
        off_out[:heads, cols] = sum(w * v for w, v in zip(shares, off))
        for h in range(heads):
            at = head_rows(h)
            blocks[r][at, :] = (o_ref[at, cols] * shares[0][h : h + 1]).astype(BF16)


def bwd_body(heads, q_block, k_block, *refs):
    q_refs, kv_refs, g_refs = refs[:SIDE], refs[SIDE : 2 * SIDE], refs[2 * SIDE : 3 * SIDE]
    lse_ref, off_ref = refs[3 * SIDE : 3 * SIDE + 2]
    dq_refs = refs[3 * SIDE + 2 : 4 * SIDE + 2]
    dkv_refs = refs[4 * SIDE + 2 : 5 * SIDE + 2]
    keys, vals, kt, qt, gt, dq, dk, dv = refs[5 * SIDE + 2 :]
    rows = q_refs[0].shape[1]
    span = SIDE * rows
    width = heads * HEAD_DIM
    for r in range(SIDE):
        cols = slice(r * rows, (r + 1) * rows)
        qt[:, cols] = q_refs[r][...]
        gt[:, cols] = g_refs[r][...]
        kt[:, cols] = kv_refs[r][:width, :]
        for h in range(heads):
            keys[h, cols, :] = kv_refs[r][head_rows(h), :].T
            vals[h, cols, :] = kv_refs[r][head_rows(heads + h), :].T
    dk[...] = jnp.zeros_like(dk)
    dv[...] = jnp.zeros_like(dv)
    dq[...] = jnp.zeros_like(dq)

    def q_step(qi, carry):
        q_cols = pl.ds(pl.multiple_of(qi * q_block, q_block), q_block)

        def k_step(ki, carry):
            k_rows = pl.ds(pl.multiple_of(ki * k_block, k_block), k_block)
            for h in range(heads):
                at = head_rows(h)
                one = slice(h, h + 1)
                q = qt[at, q_cols]
                g = gt[at, q_cols]
                scores = nn(keys[h, k_rows, :], q)
                prob = jnp.exp(scores - lse_ref[one, q_cols])
                grad_prob = nn(vals[h, k_rows, :], g)
                grad_score = (prob * (grad_prob - off_ref[one, q_cols])).astype(BF16)
                dq[at, q_cols] += nn(kt[at, k_rows], grad_score)
                dk[at, k_rows] += nt(q, grad_score)
                dv[at, k_rows] += nt(g, prob.astype(BF16))
            return carry

        lax.fori_loop(0, span // k_block, k_step, 0)
        return carry

    lax.fori_loop(0, span // q_block, q_step, 0)
    for r in range(SIDE):
        cols = slice(r * rows, (r + 1) * rows)
        dq_refs[r][...] = (dq[:, cols] * HEAD_DIM ** (-0.5)).astype(BF16)
        dkv_refs[r][:width, :] = dk[:, cols].astype(BF16)
        dkv_refs[r][width:, :] = dv[:, cols].astype(BF16)


def sum_terms(refs):
    return sum(t[...].astype(F32) for t in refs)


def proj_body(*refs):
    terms, wo_ref, full_ref = refs[:SIDE], refs[SIDE], refs[SIDE + 1]
    part_out, own_out, other_out = refs[SIDE + 2 :]
    attended = sum_terms(terms).astype(BF16)
    half = own_out.shape[0]
    other_out[...] = nn(wo_ref[half:, :], attended).astype(BF16)
    own_out[...] = nn(wo_ref[:half, :], attended)
    part_out[...] = nt(attended, full_ref[...]).astype(BF16)


def pair_body(own_ref, got_ref, *outs):
    chunk = outs[0].shape[0]
    for d in range(SIDE):
        at = slice(d * chunk, (d + 1) * chunk)
        outs[d][...] = (own_ref[at, :] + got_ref[at, :].astype(F32)).astype(BF16)


def weights_body(heads, *refs):
    dq, dkv = refs[:SIDE], refs[SIDE : 2 * SIDE]
    normed_ref, out_part_ref, gp_out, part_out = refs[2 * SIDE :]
    width = heads * HEAD_DIM
    grad_q = sum_terms(dq).astype(BF16)
    grad_kv = sum_terms(dkv).astype(BF16)
    for h in range(heads):
        at = h * 3 * HEAD_DIM
        gp_out[at : at + HEAD_DIM, :] = grad_q[head_rows(h)]
        gp_out[at + HEAD_DIM : at + 2 * HEAD_DIM, :] = grad_kv[head_rows(h)]
        gp_out[at + 2 * HEAD_DIM : at + 3 * HEAD_DIM, :] = grad_kv[head_rows(heads + h)]
    part_out[: 3 * width, :] = nt(gp_out[...], normed_ref[...]).astype(BF16)
    part_out[3 * width :, :] = out_part_ref[...]


def split(v):
    high = v.astype(BF16)
    return high, (v - high.astype(F32)).astype(BF16)


def grads_body(heads, width, all_gp, q_ref, kv_ref, wq_ref, own_out, other_out):
    size = 3 * HEAD_DIM
    dots = jnp.zeros((1, q_ref.shape[1]), F32)
    for h in range(heads):
        at = h * size
        gp = all_gp[at : at + size, :].astype(F32)
        q = q_ref[head_rows(h), :].astype(F32) * HEAD_DIM**0.5
        k = kv_ref[head_rows(h), :].astype(F32)
        v = kv_ref[head_rows(heads + h), :].astype(F32)
        for j, held in enumerate((q, k, v)):
            dots = dots + jnp.sum(
                gp[j * HEAD_DIM : (j + 1) * HEAD_DIM] * held, axis=0, keepdims=True
            )
    dots = dots / width
    half = wq_ref.shape[0] // 2
    other_out[:half, :] = nn(wq_ref[half:, :], all_gp[...]).astype(BF16)
    high, low = split(dots)
    other_out[half:, :] = jnp.concatenate(
        [high, low, jnp.zeros((PAD - 2, dots.shape[1]), BF16)], axis=0
    )
    own_out[:half, :] = nn(wq_ref[:half, :], all_gp[...])
    own_out[half:, :] = jnp.broadcast_to(dots, (8, dots.shape[1]))


def grads_pair_body(own_ref, got_ref, *outs):
    chunk = outs[0].shape[0] - PAD
    half = SIDE * chunk
    got = got_ref[half:, :].astype(F32)
    dots = own_ref[half : half + 1, :] + got[0:1] + got[1:2]
    high, low = split(dots)
    tail = jnp.concatenate([high, low, jnp.zeros((PAD - 2, dots.shape[1]), BF16)], axis=0)
    for d in range(SIDE):
        at = slice(d * chunk, (d + 1) * chunk)
        outs[d][:chunk, :] = (own_ref[at, :] + got_ref[at, :].astype(F32)).astype(BF16)
        outs[d][chunk:, :] = tail


def spread_small_body(in_ref, small_ref, out_ref):
    members, rows, width = in_ref.shape
    total = sum(in_ref[i].astype(F32) for i in range(members)).astype(BF16)
    small = small_ref[...]
    for i in range(members):
        out_ref[i, :, :width] = total
        out_ref[i, :, width:] = small


def finish_body(heads, all_ref, qkv_out, proj_out, small_out):
    members, each, _ = all_ref.shape
    width = qkv_out.shape[2]
    step = 8

    def rows_of(row):
        m, k = divmod(row, each)
        return all_ref[m, k : k + step, :width].astype(F32)

    for i in range(0, HEAD_DIM, step):
        for h in range(heads):
            for j in range(3):
                at = h * HEAD_DIM + i
                qkv_out[j, at : at + step, :] = rows_of((h * 3 + j) * HEAD_DIM + i)
    for i in range(0, heads * HEAD_DIM, step):
        proj_out[i : i + step, :] = rows_of(3 * heads * HEAD_DIM + i)
    small_out[...] = sum(all_ref[m, :, width:].astype(F32) for m in range(members))


def tie(value, *others):
    return lax.optimization_barrier((value, *others))[0]


def shards(frames, norm_gain, w_qkv, w_out, conv_kernel, grad_out):
    own_width, rows = frames.shape
    head_cols, width = w_qkv.shape[1:]
    heads = head_cols // HEAD_DIM
    members = lax.axis_size("tm")
    taps = conv_kernel.shape[0]
    span = SIDE * rows
    y, core = lax.axis_index("mp") // 2, lax.axis_index("mp") % 2
    steps = jnp.arange(SIDE, dtype=jnp.int32)
    cores = jnp.stack([core, 1 - core]).astype(jnp.int32)
    came = ((((y - steps + SIDE) % SIDE) * 2)[None, :] + cores[:, None]).reshape(-1)
    goes = ((((y + steps) % SIDE) * 2)[None, :] + cores[:, None]).reshape(-1)

    def with_swap(blocks):
        return blocks + [swap_core(jnp.concatenate(blocks, axis=0))]

    def scatter_mp(blocks):
        return [blocks[0]] + [shift_y(blocks[d], d) for d in range(1, SIDE)]

    up_left, up_right = halos(grad_out)
    in_blocks = [frames] + [shift_y(frames, d) for d in range(1, SIDE)]
    wq_rel, wo_rel = call(
        prep_body, "prep",
        [((width, 3 * head_cols), BF16), ((width, head_cols), BF16)],
        [goes, w_qkv, w_out], [SM, VM, VM],
        [
            pltpu.VMEM((3 * head_cols, width), BF16),
            pltpu.VMEM((width, 3 * head_cols), BF16),
            pltpu.VMEM((width, head_cols), BF16),
        ],
    )
    back_sum, back_cast = call(
        back_kernel, "conv_back",
        [((own_width, rows), F32), ((own_width, rows), BF16)],
        [tie(up_left, wq_rel), grad_out, up_right, conv_kernel], None,
        [
            pltpu.VMEM((rows + 2 * PAD, own_width), F32),
            pltpu.VMEM((rows, own_width), F32),
            pltpu.VMEM((STEP + 2 * PAD, own_width), F32),
        ],
        flops=8 * own_width * rows * taps,
    )
    in_blocks = list(lax.optimization_barrier((*in_blocks, back_cast)))
    back_cast = in_blocks.pop()
    back_blocks = [back_cast] + [shift_y(back_cast, d) for d in range(1, SIDE)]
    normed, inverse, queries, keys_values = call(
        norm_body, "norm_qkv",
        [((width, rows), BF16), ((1, rows), F32), ((head_cols, rows), BF16), ((2 * head_cols, rows), BF16)],
        [came, *with_swap(in_blocks), norm_gain[:, None], w_qkv], [SM] + [VM] * 7,
        flops=2 * 3 * head_cols * width * rows,
    )
    group_kv = [keys_values] + [shift_z(keys_values, s) for s in range(1, SIDE)]
    group_q = [queries] + [shift_x(queries, s) for s in range(1, SIDE)]

    back_blocks = list(lax.optimization_barrier((*back_blocks, group_q[1])))[:SIDE]
    back_full, grad_attn = call(
        back_arrange_body, "back_arrange",
        [((width, rows), BF16), ((head_cols, rows), BF16)],
        [came, *with_swap(back_blocks), w_out], [SM] + [VM] * 6,
        flops=2 * head_cols * width * rows,
    )
    group_g = [grad_attn] + [shift_x(grad_attn, s) for s in range(1, SIDE)]

    part_out, part_lse = call(
        functools.partial(fwd_loop_body, heads), "attn_fwd",
        [((head_cols, span), F32), ((heads, span), F32)],
        [tie(group_q[0], grad_attn), *group_q[1:], *group_kv], None,
        [
            pltpu.VMEM((heads, span, HEAD_DIM), BF16),
            pltpu.VMEM((head_cols, span), BF16),
            pltpu.VMEM((head_cols, span), BF16),
        ],
        flops=16 * head_cols * span * span, exps=heads * span * span,
    )
    (stats,) = call(
        functools.partial(stats_body, heads), "stats",
        [((8, span), F32)], [part_out, part_lse, *group_g],
    )
    peers = [stats] + [shift_x(stats, s) for s in range(1, SIDE)]
    logsum, offset, *out_blocks = call(
        functools.partial(combine_body, heads), "combine",
        [((8, span), F32), ((8, span), F32)] + [((head_cols, rows), BF16)] * SIDE,
        [part_out, *peers],
    )
    out_terms = [out_blocks[0]] + [shift_x(out_blocks[s], -s) for s in range(1, SIDE)]

    q_block, k_block = min(1024, span), min(512, span)
    grads = call(
        functools.partial(bwd_body, heads, q_block, k_block), "attn_bwd",
        [((head_cols, rows), BF16)] * SIDE + [((2 * head_cols, rows), BF16)] * SIDE,
        [*group_q, *group_kv, *group_g, logsum, offset], None,
        [pltpu.VMEM((heads, span, HEAD_DIM), BF16)] * 2
        + [pltpu.VMEM((head_cols, span), BF16)] * 3
        + [pltpu.VMEM((head_cols, span), F32)] * 3,
        flops=40 * head_cols * span * span, exps=heads * span * span,
    )
    dq, dkv = grads[:SIDE], grads[SIDE:]
    dkv_terms = [dkv[0]] + [shift_z(dkv[s], -s) for s in range(1, SIDE)]
    dq_terms = [dq[0]] + [shift_x(dq[s], -s) for s in range(1, SIDE)]

    half = SIDE * own_width
    out_part, proj_own, proj_other = call(
        proj_body, "proj",
        [((head_cols, width), BF16), ((half, rows), F32), ((half, rows), BF16)],
        [tie(out_terms[0], dq_terms[1]), *out_terms[1:], wo_rel, back_full],
        flops=4 * head_cols * width * rows,
    )
    proj_blocks = call(
        pair_body, "proj_pair", [((own_width, rows), BF16)] * SIDE, [proj_own, swap_core(proj_other)]
    )
    proj_terms = scatter_mp(proj_blocks)

    all_gp, part = call(
        functools.partial(weights_body, heads), "weights",
        [((3 * head_cols, rows), BF16), ((4 * head_cols, width), BF16)],
        [*dq_terms, *dkv_terms, normed, tie(out_part, *proj_blocks)],
        flops=2 * 3 * head_cols * width * rows,
    )
    each = part.shape[0] // members
    got = lax.all_to_all(part.reshape(members, each, width), "tm", 0, 0, tiled=True)

    gn_own, gn_other = call(
        functools.partial(grads_body, heads, width), "packed_grads",
        [((half + 8, rows), F32), ((half + PAD, rows), BF16)],
        [tie(all_gp, part), queries, keys_values, wq_rel],
        flops=2 * 3 * head_cols * width * rows,
    )
    gn_blocks = call(
        grads_pair_body, "grads_pair", [((own_width + PAD, rows), BF16)] * SIDE,
        [gn_own, swap_core(gn_other)],
    )
    gn_terms = scatter_mp(gn_blocks)

    mixed = sum(t.astype(F32) for t in [tie(proj_terms[0], part)] + proj_terms[1:])
    residual = (frames.astype(F32) + mixed).astype(BF16)
    res_left, res_right = halos(residual)
    block_out, kernel_part = call(
        conv_body, "conv_fwd",
        [((own_width, rows), BF16), ((taps, own_width), F32)],
        [tie(res_left, *gn_blocks), residual, res_right, grad_out, conv_kernel], None,
        [
            pltpu.VMEM((rows + 2 * PAD, own_width), F32),
            pltpu.VMEM((rows, own_width), F32),
            pltpu.VMEM((taps, 8, own_width), F32),
            pltpu.VMEM((STEP + 2 * PAD, own_width), F32),
        ],
        flops=16 * own_width * rows * taps,
    )

    summed = sum(t.astype(F32) for t in [tie(gn_terms[0], kernel_part)] + gn_terms[1:])
    grad_own = summed[:own_width]
    dots = summed[own_width : own_width + 1] + summed[own_width + 1 : own_width + 2]
    column_start = lax.axis_index("mp") * own_width
    gain_own = lax.dynamic_slice_in_dim(norm_gain, column_start, own_width, 0)[:, None]
    normed_own = frames.astype(F32) * inverse
    grad_frames = (
        back_sum + inverse * (grad_own * gain_own) - normed_own * inverse * dots
    ).astype(BF16)
    gain_part = jnp.sum(grad_own * normed_own, axis=1)
    small = jnp.concatenate([kernel_part.astype(BF16), gain_part.astype(BF16)[None]], axis=0)
    small_cols = small.size // each
    (spread,) = call(
        spread_small_body, "spread", [((members, each, width + small_cols), BF16)],
        [got, small.reshape(each, small_cols)],
    )
    everything = lax.all_to_all(spread, "tm", 0, 0, tiled=True)
    qkv_grads, out_grads, small_sum = call(
        functools.partial(finish_body, heads), "finish",
        [((3, head_cols, width), F32), ((head_cols, width), F32), ((each, small_cols), F32)],
        [everything],
    )
    small_sum = small_sum.reshape(taps + 1, own_width)
    return block_out, grad_frames, small_sum[taps], qkv_grads, out_grads, small_sum[:taps]


def solution(mesh):
    return jax.shard_map(
        shards,
        mesh=mesh,
        in_specs=(
            P("mp", "tm"),
            P(),
            P(None, "mp", None),
            P("mp", None),
            P(None, "mp"),
            P("mp", "tm"),
        ),
        out_specs=(
            P("mp", "tm"),
            P("mp", "tm"),
            P("mp"),
            P(None, "mp", None),
            P("mp", None),
            P(None, "mp"),
        ),
        check_vma=False,
    )
```

```python
import functools

import jax
import jax.numpy as jnp
from jax import lax
from jax.experimental import pallas as pl
from jax.experimental.pallas import tpu as pltpu
from jax.sharding import PartitionSpec as P


HEAD_DIM = 64
SIDE = 4
PAD = 16
F32 = jnp.float32
BF16 = jnp.bfloat16


def nn(a, b):
    return jnp.dot(a, b, preferred_element_type=F32)


def nt(a, b):
    return lax.dot_general(a, b, (((1,), (1,)), ((), ())), preferred_element_type=F32)


VM = pl.BlockSpec(memory_space=pltpu.VMEM)


STEP = 64


def fill(pad_ref, left_ref, own_ref, right_ref):
    count = own_ref.shape[1]
    slab = left_ref.shape[1]
    pad_ref[PAD : PAD + count, :] = own_ref[...].astype(F32).T
    pad_ref[:PAD, :] = left_ref[...].astype(F32).T[slab - PAD :, :]
    pad_ref[PAD + count :, :] = right_ref[...].astype(F32).T[:PAD, :]


def back_kernel(left_ref, own_ref, right_ref, taps_ref, sum_ref, cast_ref, pad_ref, acc_ref, near):
    count = own_ref.shape[1]
    fill(pad_ref, left_ref, own_ref, right_ref)
    taps = taps_ref.shape[0]
    half = taps // 2

    def step(i, carry):
        base = pl.multiple_of(i * STEP, STEP)
        near[...] = pad_ref[pl.ds(base, STEP + 2 * PAD), :]
        acc = near[PAD : PAD + STEP, :]
        for j in range(taps):
            start = PAD + half - j
            acc = acc + taps_ref[j : j + 1, :] * near[start : start + STEP, :]
        acc_ref[pl.ds(base, STEP), :] = acc
        return carry

    lax.fori_loop(0, count // STEP, step, 0)
    acc = acc_ref[...].T
    sum_ref[...] = acc
    cast_ref[...] = acc.astype(BF16)


def conv_body(left_ref, own_ref, right_ref, up_ref, taps_ref, out_ref, grad_ref, pad_ref, upt_ref, sums, near):
    count = own_ref.shape[1]
    fill(pad_ref, left_ref, own_ref, right_ref)
    upt_ref[...] = up_ref[...].astype(F32).T
    taps = taps_ref.shape[0]
    half = taps // 2
    sums[...] = jnp.zeros_like(sums)

    def step(i, carry):
        base = pl.multiple_of(i * STEP, STEP)
        near[...] = pad_ref[pl.ds(base, STEP + 2 * PAD), :]
        acc = near[PAD : PAD + STEP, :]
        up = upt_ref[pl.ds(base, STEP), :]
        for j in range(taps):
            start = PAD + j - half
            part = near[start : start + STEP, :]
            acc = acc + taps_ref[j : j + 1, :] * part
            prod = up * part
            sums[j] += sum(prod[8 * s : 8 * s + 8] for s in range(STEP // 8))
        upt_ref[pl.ds(base, STEP), :] = acc
        return carry

    lax.fori_loop(0, count // STEP, step, 0)
    for j in range(taps):
        grad_ref[j : j + 1, :] = jnp.sum(sums[j], axis=0, keepdims=True)
    out_ref[...] = upt_ref[...].T.astype(BF16)


def shift_x(a, by):
    pairs = [
        (z * SIDE + x, z * SIDE + (x + by) % SIDE) for z in range(SIDE) for x in range(SIDE)
    ]
    return lax.ppermute(a, "tm", pairs)


def shift_z(a, by):
    pairs = [
        (z * SIDE + x, ((z + by) % SIDE) * SIDE + x) for z in range(SIDE) for x in range(SIDE)
    ]
    return lax.ppermute(a, "tm", pairs)


def halos(a, slab=128):
    count = lax.axis_size("tm")
    ends = count - 1
    left = lax.ppermute(a[:, a.shape[1] - slab :], "tm", [(i, i + 1) for i in range(ends)])
    right = lax.ppermute(a[:, :slab], "tm", [(i + 1, i) for i in range(ends)])
    return left, right


SM = pl.BlockSpec(memory_space=pltpu.SMEM)


def shift_y(a, by):
    count = lax.axis_size("mp") // 2
    pairs = [(y * 2 + c, ((y + by) % count) * 2 + c) for y in range(count) for c in range(2)]
    return lax.ppermute(a, "mp", pairs)


def swap_core(a):
    count = lax.axis_size("mp")
    return lax.ppermute(a, "mp", [(i, i ^ 1) for i in range(count)])


def call(body, outs, args, specs=None, scratch=(), flops=0, exps=0):
    out_shape = tuple(jax.ShapeDtypeStruct(s, t) for s, t in outs)
    moved = sum(a.size * a.dtype.itemsize for a in args)
    moved += sum(o.size * o.dtype.itemsize for o in out_shape)
    return pl.pallas_call(
        body,
        out_shape=out_shape,
        in_specs=specs or [VM] * len(args),
        out_specs=[VM] * len(outs),
        scratch_shapes=list(scratch),
        cost_estimate=pl.CostEstimate(flops=flops, bytes_accessed=moved, transcendentals=exps),
    )(*args)


def ring(shift, blocks, sign):
    return [blocks[0]] + [shift(blocks[r], sign * r) for r in range(1, SIDE)]


def head_rows(h):
    return slice(h * HEAD_DIM, (h + 1) * HEAD_DIM)


def prep_body(pos_ref, w_ref, wo_ref, wq_out, wo_out, mixed, turned, turned_out):
    head_cols, width = wo_ref.shape
    heads = head_cols // HEAD_DIM
    for h in range(heads):
        for j in range(3):
            at = (h * 3 + j) * HEAD_DIM
            mixed[at : at + HEAD_DIM, :] = w_ref[j, head_rows(h), :]
    turned[...] = mixed[...].T
    turned_out[...] = wo_ref[...].T
    chunk = width // 8
    for r in range(8):
        rows = pl.ds(pl.multiple_of(pos_ref[r] * chunk, chunk), chunk)
        wq_out[r * chunk : (r + 1) * chunk, :] = turned[rows, :]
        wo_out[r * chunk : (r + 1) * chunk, :] = turned_out[rows, :]


def norm_body(pos_ref, b0, b1, b2, b3, other, gain_ref, w_ref, normed_out, inv_out, q_out, kv_out):
    own = [b0, b1, b2, b3]
    chunk, rows = b0.shape
    width = normed_out.shape[0]

    def block(r):
        part = own[r][...] if r < 4 else other[(r - 4) * chunk : (r - 3) * chunk, :]
        return part.astype(F32)

    total = jnp.zeros((1, rows), F32)
    for r in range(8):
        x = block(r)
        total = total + jnp.sum(x * x, axis=0, keepdims=True)
    inverse = lax.rsqrt(total / width + 1e-06)
    inv_out[...] = inverse
    for r in range(8):
        at = pl.ds(pl.multiple_of(pos_ref[r] * chunk, chunk), chunk)
        normed_out[at, :] = (block(r) * inverse * gain_ref[at, :]).astype(BF16)
    normed = normed_out[...]
    q_out[...] = nn(w_ref[0], normed).astype(BF16) * jnp.asarray(HEAD_DIM ** (-0.5), BF16)
    head_cols = q_out.shape[0]
    for j in (1, 2):
        kv_out[(j - 1) * head_cols : j * head_cols, :] = nn(w_ref[j], normed).astype(BF16)


def back_arrange_body(pos_ref, b0, b1, b2, b3, other, wo_ref, full_out, grad_out):
    own = [b0, b1, b2, b3]
    chunk = b0.shape[0]
    for r in range(8):
        at = pl.ds(pl.multiple_of(pos_ref[r] * chunk, chunk), chunk)
        full_out[at, :] = own[r][...] if r < 4 else other[(r - 4) * chunk : (r - 3) * chunk, :]
    grad_out[...] = nn(wo_ref[...], full_out[...]).astype(BF16)


def fwd_loop_body(heads, *refs):
    q_refs, kv_refs = refs[:SIDE], refs[SIDE : 2 * SIDE]
    o_ref, lse_ref, keys, vals, queries = refs[2 * SIDE :]
    rows = q_refs[0].shape[1]
    width = heads * HEAD_DIM
    for r in range(SIDE):
        cols = slice(r * rows, (r + 1) * rows)
        vals[:, cols] = kv_refs[r][width:, :]
        queries[:, cols] = q_refs[r][...]
        for h in range(heads):
            keys[h, cols, :] = kv_refs[r][head_rows(h), :].T

    def step(r, carry):
        cols = pl.ds(pl.multiple_of(r * rows, rows), rows)
        for h in range(heads):
            at = head_rows(h)
            scores = nn(keys[h], queries[at, cols])
            top = jnp.max(scores, axis=0, keepdims=True)
            weights = jnp.exp(scores - top)
            total = jnp.sum(weights, axis=0, keepdims=True)
            out = nn(vals[at, :], weights.astype(BF16)) / total
            o_ref[at, cols] = out.astype(BF16)
            lse_ref[h : h + 1, cols] = top + jnp.log(total)
        return carry

    lax.fori_loop(0, SIDE, step, 0)


def stats_body(heads, o_ref, lse_ref, *refs):
    g_refs, out_ref = refs[:SIDE], refs[SIDE]
    rows = g_refs[0].shape[1]
    out_ref[...] = jnp.zeros_like(out_ref)
    out_ref[:heads, :] = lse_ref[...]
    for r in range(SIDE):
        cols = slice(r * rows, (r + 1) * rows)
        for h in range(heads):
            at = head_rows(h)
            out_ref[heads + h : heads + h + 1, cols] = jnp.sum(
                o_ref[at, cols].astype(F32) * g_refs[r][at, :].astype(F32), axis=0, keepdims=True
            )


def combine_body(heads, o_ref, *refs):
    peers, outs = refs[:SIDE], refs[SIDE:]
    lse_out, off_out, blocks = outs[0], outs[1], outs[2:]
    rows = o_ref.shape[1] // SIDE
    for r in range(SIDE):
        cols = slice(r * rows, (r + 1) * rows)
        theirs = []
        for s in range(SIDE):
            at = (r - s) % SIDE
            theirs.append(peers[s][:, at * rows : (at + 1) * rows])
        lse = [t[:heads] for t in theirs]
        off = [t[heads : 2 * heads] for t in theirs]
        top = jnp.maximum(jnp.maximum(lse[0], lse[1]), jnp.maximum(lse[2], lse[3]))
        logsum = top + jnp.log(sum(jnp.exp(v - top) for v in lse))
        shares = [jnp.exp(v - logsum) for v in lse]
        lse_out[:heads, cols] = logsum
        off_out[:heads, cols] = sum(w * v for w, v in zip(shares, off))
        for h in range(heads):
            at = head_rows(h)
            blocks[r][at, :] = (o_ref[at, cols].astype(F32) * shares[0][h : h + 1]).astype(BF16)


def bwd_body(first, last, heads, q_block, k_block, *refs):
    q_refs, kv_refs, g_refs = refs[:SIDE], refs[SIDE : 2 * SIDE], refs[2 * SIDE : 3 * SIDE]
    lse_ref, off_ref = refs[3 * SIDE : 3 * SIDE + 2]
    refs = refs[3 * SIDE + 2 :]
    carried = refs[: 2 * SIDE] if first else ()
    refs = refs[len(carried) :]
    dq_refs, dkv_refs = refs[:SIDE], refs[SIDE : 2 * SIDE]
    keys, vals, kt, qt, gt, stat, dq, dk, dv = refs[2 * SIDE :]
    count = last - first
    rows = q_refs[0].shape[1]
    span = SIDE * rows
    mine = slice(first * HEAD_DIM, last * HEAD_DIM)
    for r in range(SIDE):
        cols = slice(r * rows, (r + 1) * rows)
        qt[:, cols] = q_refs[r][mine, :]
        gt[:, cols] = g_refs[r][mine, :]
        kt[:, cols] = kv_refs[r][mine, :]
        for h in range(count):
            keys[h, cols, :] = kv_refs[r][head_rows(first + h), :].T
            vals[h, cols, :] = kv_refs[r][head_rows(heads + first + h), :].T
    for h in range(count):
        stat[h : h + 1, :] = lse_ref[first + h : first + h + 1, :]
        stat[count + h : count + h + 1, :] = off_ref[first + h : first + h + 1, :]
    dk[...] = jnp.zeros_like(dk)
    dv[...] = jnp.zeros_like(dv)
    dq[...] = jnp.zeros_like(dq)

    def q_step(qi, carry):
        q_cols = pl.ds(pl.multiple_of(qi * q_block, q_block), q_block)

        def k_step(ki, carry):
            k_rows = pl.ds(pl.multiple_of(ki * k_block, k_block), k_block)
            for h in range(count):
                at = head_rows(h)
                q = qt[at, q_cols]
                g = gt[at, q_cols]
                scores = nn(keys[h, k_rows, :], q)
                prob = jnp.exp(scores - stat[h : h + 1, q_cols])
                grad_prob = nn(vals[h, k_rows, :], g)
                off = stat[count + h : count + h + 1, q_cols]
                grad_score = (prob * (grad_prob - off)).astype(BF16)
                dq[at, q_cols] += nn(kt[at, k_rows], grad_score)
                dk[at, k_rows] += nt(q, grad_score)
                dv[at, k_rows] += nt(g, prob.astype(BF16))
            return carry

        lax.fori_loop(0, span // k_block, k_step, 0)
        return carry

    lax.fori_loop(0, span // q_block, q_step, 0)
    done = first * HEAD_DIM
    for r in range(SIDE):
        cols = slice(r * rows, (r + 1) * rows)
        dq_refs[r][done:, :] = (dq[:, cols] * HEAD_DIM ** (-0.5)).astype(BF16)
        half = last * HEAD_DIM
        dkv_refs[r][done:half, :] = dk[:, cols].astype(BF16)
        dkv_refs[r][half + done :, :] = dv[:, cols].astype(BF16)
        if first:
            dq_refs[r][:done, :] = carried[r][...]
            dkv_refs[r][:done, :] = carried[SIDE + r][:done, :]
            dkv_refs[r][half : half + done, :] = carried[SIDE + r][done:, :]


def sum_terms(refs):
    return sum(t[...].astype(F32) for t in refs)


def proj_body(*refs):
    terms, wo_ref = refs[:SIDE], refs[SIDE]
    att_out, own_out, other_out = refs[SIDE + 1 :]
    attended = sum_terms(terms).astype(BF16)
    half = own_out.shape[0]
    other_out[...] = nn(wo_ref[half:, :], attended).astype(BF16)
    own_out[...] = nn(wo_ref[:half, :], attended)
    att_out[...] = attended


def out_weights_body(att_ref, full_ref, part_out):
    part_out[...] = nt(att_ref[...], full_ref[...]).astype(BF16)


def pair_body(own_ref, got_ref, *outs):
    chunk = outs[0].shape[0]
    for d in range(SIDE):
        at = slice(d * chunk, (d + 1) * chunk)
        outs[d][...] = (own_ref[at, :] + got_ref[at, :].astype(F32)).astype(BF16)


def weights_body(heads, *refs):
    dq, dkv = refs[:SIDE], refs[SIDE : 2 * SIDE]
    normed_ref, out_part_ref, gp_out, part_out = refs[2 * SIDE :]
    width = heads * HEAD_DIM
    grad_q = sum_terms(dq).astype(BF16)
    grad_kv = sum_terms(dkv).astype(BF16)
    for h in range(heads):
        at = h * 3 * HEAD_DIM
        gp_out[at : at + HEAD_DIM, :] = grad_q[head_rows(h)]
        gp_out[at + HEAD_DIM : at + 2 * HEAD_DIM, :] = grad_kv[head_rows(h)]
        gp_out[at + 2 * HEAD_DIM : at + 3 * HEAD_DIM, :] = grad_kv[head_rows(heads + h)]
    part_out[: 3 * width, :] = nt(gp_out[...], normed_ref[...]).astype(BF16)
    part_out[3 * width :, :] = out_part_ref[...]


def split(v):
    high = v.astype(BF16)
    return high, (v - high.astype(F32)).astype(BF16)


def grads_body(heads, width, all_gp, q_ref, kv_ref, wq_ref, own_out, other_out):
    size = 3 * HEAD_DIM
    dots = jnp.zeros((1, q_ref.shape[1]), F32)
    for h in range(heads):
        at = h * size
        gp = all_gp[at : at + size, :].astype(F32)
        q = q_ref[head_rows(h), :].astype(F32) * HEAD_DIM**0.5
        k = kv_ref[head_rows(h), :].astype(F32)
        v = kv_ref[head_rows(heads + h), :].astype(F32)
        for j, held in enumerate((q, k, v)):
            dots = dots + jnp.sum(
                gp[j * HEAD_DIM : (j + 1) * HEAD_DIM] * held, axis=0, keepdims=True
            )
    dots = dots / width
    half = wq_ref.shape[0] // 2
    other_out[:half, :] = nn(wq_ref[half:, :], all_gp[...]).astype(BF16)
    high, low = split(dots)
    other_out[half:, :] = jnp.concatenate(
        [high, low, jnp.zeros((PAD - 2, dots.shape[1]), BF16)], axis=0
    )
    own_out[:half, :] = nn(wq_ref[:half, :], all_gp[...])
    own_out[half:, :] = jnp.broadcast_to(dots, (8, dots.shape[1]))


def grads_pair_body(own_ref, got_ref, *outs):
    chunk = outs[0].shape[0] - PAD
    half = SIDE * chunk
    got = got_ref[half:, :].astype(F32)
    dots = own_ref[half : half + 1, :] + got[0:1] + got[1:2]
    high, low = split(dots)
    tail = jnp.concatenate([high, low, jnp.zeros((PAD - 2, dots.shape[1]), BF16)], axis=0)
    for d in range(SIDE):
        at = slice(d * chunk, (d + 1) * chunk)
        outs[d][:chunk, :] = (own_ref[at, :] + got_ref[at, :].astype(F32)).astype(BF16)
        outs[d][chunk:, :] = tail


def spread_small_body(in_ref, small_ref, out_ref):
    members, _, width = in_ref.shape
    total = sum(in_ref[i].astype(F32) for i in range(members)).astype(BF16)
    small = small_ref[...]
    for i in range(members):
        out_ref[i, :, :width] = total
        out_ref[i, :, width:] = small


def finish_body(heads, all_ref, qkv_out, proj_out, small_out):
    members, each, _ = all_ref.shape
    width = qkv_out.shape[2]
    step = 8

    def rows_of(row):
        m, k = divmod(row, each)
        return all_ref[m, k : k + step, :width].astype(F32)

    for i in range(0, HEAD_DIM, step):
        for h in range(heads):
            for j in range(3):
                at = h * HEAD_DIM + i
                qkv_out[j, at : at + step, :] = rows_of((h * 3 + j) * HEAD_DIM + i)
    for i in range(0, heads * HEAD_DIM, step):
        proj_out[i : i + step, :] = rows_of(3 * heads * HEAD_DIM + i)
    small_out[...] = sum(all_ref[m, :, width:].astype(F32) for m in range(members))


def tie(value, *others):
    return lax.optimization_barrier((value, *others))[0]


def shards(frames, norm_gain, w_qkv, w_out, conv_kernel, grad_out):
    own_width, rows = frames.shape
    head_cols, width = w_qkv.shape[1:]
    heads = head_cols // HEAD_DIM
    members = lax.axis_size("tm")
    taps = conv_kernel.shape[0]
    span = SIDE * rows
    y, core = lax.axis_index("mp") // 2, lax.axis_index("mp") % 2
    steps = jnp.arange(SIDE, dtype=jnp.int32)
    cores = jnp.stack([core, 1 - core]).astype(jnp.int32)
    came = ((((y - steps + SIDE) % SIDE) * 2)[None, :] + cores[:, None]).reshape(-1)
    goes = ((((y + steps) % SIDE) * 2)[None, :] + cores[:, None]).reshape(-1)

    def with_swap(blocks):
        return blocks + [swap_core(jnp.concatenate(blocks, axis=0))]

    up_left, up_right = halos(grad_out)
    in_blocks = ring(shift_y, [frames] * SIDE, 1)
    back_sum, back_cast = call(
        back_kernel,
        [((own_width, rows), F32), ((own_width, rows), BF16)],
        [up_left, grad_out, up_right, conv_kernel], None,
        [
            pltpu.VMEM((rows + 2 * PAD, own_width), F32),
            pltpu.VMEM((rows, own_width), F32),
            pltpu.VMEM((STEP + 2 * PAD, own_width), F32),
        ],
        flops=8 * own_width * rows * taps,
    )
    in_blocks = list(lax.optimization_barrier((*in_blocks, back_cast)))
    back_cast = in_blocks.pop()
    in_blocks = with_swap(in_blocks)
    back_blocks = ring(shift_y, [back_cast] * SIDE, 1)
    normed, inverse, queries, keys_values = call(
        norm_body,
        [((width, rows), BF16), ((1, rows), F32), ((head_cols, rows), BF16), ((2 * head_cols, rows), BF16)],
        [came, *in_blocks, norm_gain[:, None], w_qkv], [SM] + [VM] * 7,
        flops=2 * 3 * head_cols * width * rows,
    )
    group_kv = ring(shift_z, [keys_values] * SIDE, 1)
    group_q = ring(shift_x, [queries] * SIDE, 1)

    back_blocks = list(lax.optimization_barrier((*back_blocks, keys_values)))[:SIDE]
    back_blocks = with_swap(back_blocks)
    back_full, grad_attn = call(
        back_arrange_body,
        [((width, rows), BF16), ((head_cols, rows), BF16)],
        [came, *back_blocks, w_out], [SM] + [VM] * 6,
        flops=2 * head_cols * width * rows,
    )
    group_g = ring(shift_x, [grad_attn] * SIDE, 1)

    part_out, part_lse = call(
        functools.partial(fwd_loop_body, heads),
        [((head_cols, span), BF16), ((heads, span), F32)],
        [tie(group_q[0], grad_attn), *group_q[1:], *group_kv], None,
        [
            pltpu.VMEM((heads, span, HEAD_DIM), BF16),
            pltpu.VMEM((head_cols, span), BF16),
            pltpu.VMEM((head_cols, span), BF16),
        ],
        flops=16 * head_cols * span * span, exps=heads * span * span,
    )
    (stats,) = call(
        functools.partial(stats_body, heads),
        [((8, span), F32)], [part_out, part_lse, *group_g],
    )
    peers = ring(shift_x, [stats] * SIDE, 1)
    wq_rel, wo_rel = call(
        prep_body,
        [((width, 3 * head_cols), BF16), ((width, head_cols), BF16)],
        [tie(goes, stats), w_qkv, w_out], [SM, VM, VM],
        [
            pltpu.VMEM((3 * head_cols, width), BF16),
            pltpu.VMEM((width, 3 * head_cols), BF16),
            pltpu.VMEM((width, head_cols), BF16),
        ],
    )
    logsum, offset, *out_blocks = call(
        functools.partial(combine_body, heads),
        [((8, span), F32), ((8, span), F32)] + [((head_cols, rows), BF16)] * SIDE,
        [tie(part_out, wo_rel), *peers],
    )
    out_terms = ring(shift_x, out_blocks, -1)

    q_block, k_block = min(1024, span), min(512, span)

    def head_grads(first, last, logsum, carried):
        count = last - first
        size = count * HEAD_DIM
        return call(
            functools.partial(bwd_body, first, last, heads, q_block, k_block),
            [((last * HEAD_DIM, rows), BF16)] * SIDE + [((2 * last * HEAD_DIM, rows), BF16)] * SIDE,
            [*group_q, *group_kv, *group_g, logsum, offset, *carried], None,
            [pltpu.VMEM((count, span, HEAD_DIM), BF16)] * 2
            + [pltpu.VMEM((size, span), BF16)] * 3
            + [pltpu.VMEM((8, span), F32)]
            + [pltpu.VMEM((size, span), F32)] * 3,
            flops=40 * size * span * span, exps=count * span * span,
        )

    early = head_grads(0, 1, logsum, ())
    half = SIDE * own_width
    attended, proj_own, proj_other = call(
        proj_body,
        [((head_cols, rows), BF16), ((half, rows), F32), ((half, rows), BF16)],
        [tie(out_terms[0], early[0]), *out_terms[1:], wo_rel],
        flops=2 * head_cols * width * rows,
    )
    proj_got = swap_core(proj_other)
    proj_blocks = call(pair_body, [((own_width, rows), BF16)] * SIDE, [proj_own, proj_got])
    proj_terms = ring(shift_y, proj_blocks, 1)

    grads = head_grads(1, heads, tie(logsum, *proj_blocks), early)
    dq, dkv = grads[:SIDE], grads[SIDE:]
    dkv_terms = ring(shift_z, dkv, -1)
    dq_terms = ring(shift_x, dq, -1)

    mixed = sum(t.astype(F32) for t in [tie(proj_terms[0], dq[0])] + proj_terms[1:])
    residual = (frames.astype(F32) + mixed).astype(BF16)
    res_left, res_right = halos(residual)
    (out_part,) = call(
        out_weights_body, [((head_cols, width), BF16)],
        [tie(attended, dq[0]), back_full], flops=2 * head_cols * width * rows,
    )
    block_out, kernel_part = call(
        conv_body,
        [((own_width, rows), BF16), ((taps, own_width), F32)],
        [res_left, residual, res_right, grad_out, conv_kernel], None,
        [
            pltpu.VMEM((rows + 2 * PAD, own_width), F32),
            pltpu.VMEM((rows, own_width), F32),
            pltpu.VMEM((taps, 8, own_width), F32),
            pltpu.VMEM((STEP + 2 * PAD, own_width), F32),
        ],
        flops=16 * own_width * rows * taps,
    )

    all_gp, part = call(
        functools.partial(weights_body, heads),
        [((3 * head_cols, rows), BF16), ((4 * head_cols, width), BF16)],
        [*dq_terms, *dkv_terms, normed, tie(out_part, kernel_part)],
        flops=2 * 3 * head_cols * width * rows,
    )
    each = part.shape[0] // members
    got = lax.all_to_all(part.reshape(members, each, width), "tm", 0, 0, tiled=True)

    gn_own, gn_other = call(
        functools.partial(grads_body, heads, width),
        [((half + 8, rows), F32), ((half + PAD, rows), BF16)],
        [tie(all_gp, part), queries, keys_values, wq_rel],
        flops=2 * 3 * head_cols * width * rows,
    )
    gn_got = swap_core(gn_other)
    gn_blocks = call(grads_pair_body, [((own_width + PAD, rows), BF16)] * SIDE, [gn_own, gn_got])
    gn_terms = ring(shift_y, gn_blocks, 1)
    summed = sum(t.astype(F32) for t in gn_terms)
    grad_own = summed[:own_width]
    dots = summed[own_width : own_width + 1] + summed[own_width + 1 : own_width + 2]
    column_start = lax.axis_index("mp") * own_width
    gain_own = lax.dynamic_slice_in_dim(norm_gain, column_start, own_width, 0)[:, None]
    normed_own = frames.astype(F32) * inverse
    grad_frames = (
        back_sum + inverse * (grad_own * gain_own) - normed_own * inverse * dots
    ).astype(BF16)
    gain_part = jnp.sum(grad_own * normed_own, axis=1)
    small = jnp.concatenate([kernel_part.astype(BF16), gain_part.astype(BF16)[None]], axis=0)
    small_cols = small.size // each
    (spread,) = call(
        spread_small_body, [((members, each, width + small_cols), BF16)],
        [got, small.reshape(each, small_cols)],
    )
    everything = lax.all_to_all(spread, "tm", 0, 0, tiled=True)
    qkv_grads, out_grads, small_sum = call(
        functools.partial(finish_body, heads),
        [((3, head_cols, width), F32), ((head_cols, width), F32), ((each, small_cols), F32)],
        [everything],
    )
    small_sum = small_sum.reshape(taps + 1, own_width)
    return block_out, grad_frames, small_sum[taps], qkv_grads, out_grads, small_sum[:taps]


def solution(mesh):
    return jax.shard_map(
        shards,
        mesh=mesh,
        in_specs=(
            P("mp", "tm"),
            P(),
            P(None, "mp", None),
            P("mp", None),
            P(None, "mp"),
            P("mp", "tm"),
        ),
        out_specs=(
            P("mp", "tm"),
            P("mp", "tm"),
            P("mp"),
            P(None, "mp", None),
            P("mp", None),
            P(None, "mp"),
        ),
        check_vma=False,
    )
```

```python
import functools

import jax
import jax.numpy as jnp
from jax import lax
from jax.experimental import pallas as pl
from jax.experimental.pallas import tpu as pltpu
from jax.sharding import PartitionSpec as P


HEAD_DIM = 64
SIDE = 4
PAD = 16
F32 = jnp.float32
BF16 = jnp.bfloat16


def nn(a, b):
    return jnp.dot(a, b, preferred_element_type=F32)


def nt(a, b):
    return lax.dot_general(a, b, (((1,), (1,)), ((), ())), preferred_element_type=F32)


VM = pl.BlockSpec(memory_space=pltpu.VMEM)


STEP = 64


def fill(pad_ref, left_ref, own_ref, right_ref):
    count = own_ref.shape[1]
    slab = left_ref.shape[1]
    pad_ref[PAD : PAD + count, :] = own_ref[...].astype(F32).T
    pad_ref[:PAD, :] = left_ref[...].astype(F32).T[slab - PAD :, :]
    pad_ref[PAD + count :, :] = right_ref[...].astype(F32).T[:PAD, :]


def back_kernel(left_ref, own_ref, right_ref, taps_ref, sum_ref, cast_ref, pad_ref, acc_ref, near):
    count = own_ref.shape[1]
    fill(pad_ref, left_ref, own_ref, right_ref)
    taps = taps_ref.shape[0]
    half = taps // 2

    def step(i, carry):
        base = pl.multiple_of(i * STEP, STEP)
        near[...] = pad_ref[pl.ds(base, STEP + 2 * PAD), :]
        acc = near[PAD : PAD + STEP, :]
        for j in range(taps):
            start = PAD + half - j
            acc = acc + taps_ref[j : j + 1, :] * near[start : start + STEP, :]
        acc_ref[pl.ds(base, STEP), :] = acc
        return carry

    lax.fori_loop(0, count // STEP, step, 0)
    acc = acc_ref[...].T
    sum_ref[...] = acc
    cast_ref[...] = acc.astype(BF16)


def conv_body(left_ref, own_ref, right_ref, up_ref, taps_ref, out_ref, grad_ref, pad_ref, upt_ref, sums, near):
    count = own_ref.shape[1]
    fill(pad_ref, left_ref, own_ref, right_ref)
    upt_ref[...] = up_ref[...].astype(F32).T
    taps = taps_ref.shape[0]
    half = taps // 2
    sums[...] = jnp.zeros_like(sums)

    def step(i, carry):
        base = pl.multiple_of(i * STEP, STEP)
        near[...] = pad_ref[pl.ds(base, STEP + 2 * PAD), :]
        acc = near[PAD : PAD + STEP, :]
        up = upt_ref[pl.ds(base, STEP), :]
        for j in range(taps):
            start = PAD + j - half
            part = near[start : start + STEP, :]
            acc = acc + taps_ref[j : j + 1, :] * part
            prod = up * part
            sums[j] += sum(prod[8 * s : 8 * s + 8] for s in range(STEP // 8))
        upt_ref[pl.ds(base, STEP), :] = acc
        return carry

    lax.fori_loop(0, count // STEP, step, 0)
    for j in range(taps):
        grad_ref[j : j + 1, :] = jnp.sum(sums[j], axis=0, keepdims=True)
    out_ref[...] = upt_ref[...].T.astype(BF16)


def shift_x(a, by):
    pairs = [
        (z * SIDE + x, z * SIDE + (x + by) % SIDE) for z in range(SIDE) for x in range(SIDE)
    ]
    return lax.ppermute(a, "tm", pairs)


def shift_z(a, by):
    pairs = [
        (z * SIDE + x, ((z + by) % SIDE) * SIDE + x) for z in range(SIDE) for x in range(SIDE)
    ]
    return lax.ppermute(a, "tm", pairs)


def halos(a, slab=128):
    count = lax.axis_size("tm")
    ends = count - 1
    left = lax.ppermute(a[:, a.shape[1] - slab :], "tm", [(i, i + 1) for i in range(ends)])
    right = lax.ppermute(a[:, :slab], "tm", [(i + 1, i) for i in range(ends)])
    return left, right


SM = pl.BlockSpec(memory_space=pltpu.SMEM)


def shift_y(a, by):
    count = lax.axis_size("mp") // 2
    pairs = [(y * 2 + c, ((y + by) % count) * 2 + c) for y in range(count) for c in range(2)]
    return lax.ppermute(a, "mp", pairs)


def swap_core(a):
    count = lax.axis_size("mp")
    return lax.ppermute(a, "mp", [(i, i ^ 1) for i in range(count)])


def call(body, outs, args, specs=None, scratch=(), flops=0, exps=0):
    out_shape = tuple(jax.ShapeDtypeStruct(s, t) for s, t in outs)
    moved = sum(a.size * a.dtype.itemsize for a in args)
    moved += sum(o.size * o.dtype.itemsize for o in out_shape)
    return pl.pallas_call(
        body,
        out_shape=out_shape,
        in_specs=specs or [VM] * len(args),
        out_specs=[VM] * len(outs),
        scratch_shapes=list(scratch),
        cost_estimate=pl.CostEstimate(flops=flops, bytes_accessed=moved, transcendentals=exps),
    )(*args)


def ring(shift, blocks, sign):
    return [blocks[0]] + [shift(blocks[r], sign * r) for r in range(1, SIDE)]


def head_rows(h):
    return slice(h * HEAD_DIM, (h + 1) * HEAD_DIM)


def prep_body(pos_ref, w_ref, wo_ref, wq_out, wo_out, mixed, turned, turned_out):
    head_cols, width = wo_ref.shape
    heads = head_cols // HEAD_DIM
    for h in range(heads):
        for j in range(3):
            at = (h * 3 + j) * HEAD_DIM
            mixed[at : at + HEAD_DIM, :] = w_ref[j, head_rows(h), :]
    turned[...] = mixed[...].T
    turned_out[...] = wo_ref[...].T
    chunk = width // 8
    for r in range(8):
        rows = pl.ds(pl.multiple_of(pos_ref[r] * chunk, chunk), chunk)
        wq_out[r * chunk : (r + 1) * chunk, :] = turned[rows, :]
        wo_out[r * chunk : (r + 1) * chunk, :] = turned_out[rows, :]


def norm_body(pos_ref, b0, b1, b2, b3, other, gain_ref, w_ref, normed_out, inv_out, q_out, kv_out):
    own = [b0, b1, b2, b3]
    chunk, rows = b0.shape
    width = normed_out.shape[0]

    def block(r):
        part = own[r][...] if r < 4 else other[(r - 4) * chunk : (r - 3) * chunk, :]
        return part.astype(F32)

    total = jnp.zeros((1, rows), F32)
    for r in range(8):
        x = block(r)
        total = total + jnp.sum(x * x, axis=0, keepdims=True)
    inverse = lax.rsqrt(total / width + 1e-06)
    inv_out[...] = inverse
    for r in range(8):
        at = pl.ds(pl.multiple_of(pos_ref[r] * chunk, chunk), chunk)
        normed_out[at, :] = (block(r) * inverse * gain_ref[at, :]).astype(BF16)
    normed = normed_out[...]
    q_out[...] = nn(w_ref[0], normed).astype(BF16) * jnp.asarray(HEAD_DIM ** (-0.5), BF16)
    head_cols = q_out.shape[0]
    for j in (1, 2):
        kv_out[(j - 1) * head_cols : j * head_cols, :] = nn(w_ref[j], normed).astype(BF16)


def back_arrange_body(pos_ref, b0, b1, b2, b3, other, wo_ref, full_out, grad_out):
    own = [b0, b1, b2, b3]
    chunk = b0.shape[0]
    for r in range(8):
        at = pl.ds(pl.multiple_of(pos_ref[r] * chunk, chunk), chunk)
        full_out[at, :] = own[r][...] if r < 4 else other[(r - 4) * chunk : (r - 3) * chunk, :]
    grad_out[...] = nn(wo_ref[...], full_out[...]).astype(BF16)


def fwd_loop_body(heads, *refs):
    q_refs, kv_refs = refs[:SIDE], refs[SIDE : 2 * SIDE]
    o_ref, lse_ref, keys, vals, queries = refs[2 * SIDE :]
    rows = q_refs[0].shape[1]
    width = heads * HEAD_DIM
    for r in range(SIDE):
        cols = slice(r * rows, (r + 1) * rows)
        vals[:, cols] = kv_refs[r][width:, :]
        queries[:, cols] = q_refs[r][...]
        for h in range(heads):
            keys[h, cols, :] = kv_refs[r][head_rows(h), :].T

    def step(r, carry):
        cols = pl.ds(pl.multiple_of(r * rows, rows), rows)
        for h in range(heads):
            at = head_rows(h)
            scores = nn(keys[h], queries[at, cols])
            top = jnp.max(scores, axis=0, keepdims=True)
            weights = jnp.exp(scores - top)
            total = jnp.sum(weights, axis=0, keepdims=True)
            out = nn(vals[at, :], weights.astype(BF16)) / total
            o_ref[at, cols] = out.astype(BF16)
            lse_ref[h : h + 1, cols] = top + jnp.log(total)
        return carry

    lax.fori_loop(0, SIDE, step, 0)


def stats_body(heads, o_ref, lse_ref, *refs):
    g_refs, out_ref = refs[:SIDE], refs[SIDE]
    rows = g_refs[0].shape[1]
    out_ref[...] = jnp.zeros_like(out_ref)
    out_ref[:heads, :] = lse_ref[...]
    for r in range(SIDE):
        cols = slice(r * rows, (r + 1) * rows)
        for h in range(heads):
            at = head_rows(h)
            out_ref[heads + h : heads + h + 1, cols] = jnp.sum(
                o_ref[at, cols].astype(F32) * g_refs[r][at, :].astype(F32), axis=0, keepdims=True
            )


def combine_body(heads, o_ref, *refs):
    peers, outs = refs[:SIDE], refs[SIDE:]
    lse_out, off_out, blocks = outs[0], outs[1], outs[2:]
    rows = o_ref.shape[1] // SIDE
    for r in range(SIDE):
        cols = slice(r * rows, (r + 1) * rows)
        theirs = []
        for s in range(SIDE):
            at = (r - s) % SIDE
            theirs.append(peers[s][:, at * rows : (at + 1) * rows])
        lse = [t[:heads] for t in theirs]
        off = [t[heads : 2 * heads] for t in theirs]
        top = jnp.maximum(jnp.maximum(lse[0], lse[1]), jnp.maximum(lse[2], lse[3]))
        logsum = top + jnp.log(sum(jnp.exp(v - top) for v in lse))
        shares = [jnp.exp(v - logsum) for v in lse]
        lse_out[:heads, cols] = logsum
        off_out[:heads, cols] = sum(w * v for w, v in zip(shares, off))
        for h in range(heads):
            at = head_rows(h)
            blocks[r][at, :] = (o_ref[at, cols].astype(F32) * shares[0][h : h + 1]).astype(BF16)


def bwd_body(first, last, heads, q_block, k_block, *refs):
    q_refs, kv_refs, g_refs = refs[:SIDE], refs[SIDE : 2 * SIDE], refs[2 * SIDE : 3 * SIDE]
    lse_ref, off_ref = refs[3 * SIDE : 3 * SIDE + 2]
    refs = refs[3 * SIDE + 2 :]
    carried = refs[: 2 * SIDE] if first else ()
    refs = refs[len(carried) :]
    dq_refs, dkv_refs = refs[:SIDE], refs[SIDE : 2 * SIDE]
    keys, vals, kt, qt, gt, stat, dq, dk, dv = refs[2 * SIDE :]
    count = last - first
    rows = q_refs[0].shape[1]
    span = SIDE * rows
    mine = slice(first * HEAD_DIM, last * HEAD_DIM)
    for r in range(SIDE):
        cols = slice(r * rows, (r + 1) * rows)
        qt[:, cols] = q_refs[r][mine, :]
        gt[:, cols] = g_refs[r][mine, :]
        kt[:, cols] = kv_refs[r][mine, :]
        for h in range(count):
            keys[h, cols, :] = kv_refs[r][head_rows(first + h), :].T
            vals[h, cols, :] = kv_refs[r][head_rows(heads + first + h), :].T
    for h in range(count):
        stat[h : h + 1, :] = lse_ref[first + h : first + h + 1, :]
        stat[count + h : count + h + 1, :] = off_ref[first + h : first + h + 1, :]
    dk[...] = jnp.zeros_like(dk)
    dv[...] = jnp.zeros_like(dv)
    dq[...] = jnp.zeros_like(dq)

    def q_step(qi, carry):
        q_cols = pl.ds(pl.multiple_of(qi * q_block, q_block), q_block)

        def k_step(ki, carry):
            k_rows = pl.ds(pl.multiple_of(ki * k_block, k_block), k_block)
            for h in range(count):
                at = head_rows(h)
                q = qt[at, q_cols]
                g = gt[at, q_cols]
                scores = nn(keys[h, k_rows, :], q)
                prob = jnp.exp(scores - stat[h : h + 1, q_cols])
                grad_prob = nn(vals[h, k_rows, :], g)
                off = stat[count + h : count + h + 1, q_cols]
                grad_score = (prob * (grad_prob - off)).astype(BF16)
                dq[at, q_cols] += nn(kt[at, k_rows], grad_score)
                dk[at, k_rows] += nt(q, grad_score)
                dv[at, k_rows] += nt(g, prob.astype(BF16))
            return carry

        lax.fori_loop(0, span // k_block, k_step, 0)
        return carry

    lax.fori_loop(0, span // q_block, q_step, 0)
    done = first * HEAD_DIM
    for r in range(SIDE):
        cols = slice(r * rows, (r + 1) * rows)
        dq_refs[r][done:, :] = (dq[:, cols] * HEAD_DIM ** (-0.5)).astype(BF16)
        half = last * HEAD_DIM
        dkv_refs[r][done:half, :] = dk[:, cols].astype(BF16)
        dkv_refs[r][half + done :, :] = dv[:, cols].astype(BF16)
        if first:
            dq_refs[r][:done, :] = carried[r][...]
            dkv_refs[r][:done, :] = carried[SIDE + r][:done, :]
            dkv_refs[r][half : half + done, :] = carried[SIDE + r][done:, :]


def sum_terms(refs):
    return sum(t[...].astype(F32) for t in refs)


def proj_body(*refs):
    terms, wo_ref = refs[:SIDE], refs[SIDE]
    att_out, own_out, other_out = refs[SIDE + 1 :]
    attended = sum_terms(terms).astype(BF16)
    half = own_out.shape[0]
    other_out[...] = nn(wo_ref[half:, :], attended).astype(BF16)
    own_out[...] = nn(wo_ref[:half, :], attended)
    att_out[...] = attended


def out_weights_body(att_ref, full_ref, part_out):
    part_out[...] = nt(att_ref[...], full_ref[...]).astype(BF16)


def pair_body(own_ref, got_ref, *outs):
    chunk = outs[0].shape[0]
    for d in range(SIDE):
        at = slice(d * chunk, (d + 1) * chunk)
        outs[d][...] = (own_ref[at, :] + got_ref[at, :].astype(F32)).astype(BF16)


def weights_body(heads, *refs):
    dq, dkv = refs[:SIDE], refs[SIDE : 2 * SIDE]
    normed_ref, out_part_ref, gp_out, part_out = refs[2 * SIDE :]
    width = heads * HEAD_DIM
    grad_q = sum_terms(dq).astype(BF16)
    grad_kv = sum_terms(dkv).astype(BF16)
    for h in range(heads):
        at = h * 3 * HEAD_DIM
        gp_out[at : at + HEAD_DIM, :] = grad_q[head_rows(h)]
        gp_out[at + HEAD_DIM : at + 2 * HEAD_DIM, :] = grad_kv[head_rows(h)]
        gp_out[at + 2 * HEAD_DIM : at + 3 * HEAD_DIM, :] = grad_kv[head_rows(heads + h)]
    part_out[: 3 * width, :] = nt(gp_out[...], normed_ref[...]).astype(BF16)
    part_out[3 * width :, :] = out_part_ref[...]


def split(v):
    high = v.astype(BF16)
    return high, (v - high.astype(F32)).astype(BF16)


def grads_body(heads, width, all_gp, q_ref, kv_ref, wq_ref, own_out, other_out):
    size = 3 * HEAD_DIM
    dots = jnp.zeros((1, q_ref.shape[1]), F32)
    for h in range(heads):
        at = h * size
        gp = all_gp[at : at + size, :].astype(F32)
        q = q_ref[head_rows(h), :].astype(F32) * HEAD_DIM**0.5
        k = kv_ref[head_rows(h), :].astype(F32)
        v = kv_ref[head_rows(heads + h), :].astype(F32)
        for j, held in enumerate((q, k, v)):
            dots = dots + jnp.sum(
                gp[j * HEAD_DIM : (j + 1) * HEAD_DIM] * held, axis=0, keepdims=True
            )
    dots = dots / width
    half = wq_ref.shape[0] // 2
    other_out[:half, :] = nn(wq_ref[half:, :], all_gp[...]).astype(BF16)
    high, low = split(dots)
    other_out[half:, :] = jnp.concatenate(
        [high, low, jnp.zeros((PAD - 2, dots.shape[1]), BF16)], axis=0
    )
    own_out[:half, :] = nn(wq_ref[:half, :], all_gp[...])
    own_out[half:, :] = jnp.broadcast_to(dots, (8, dots.shape[1]))


def grads_pair_body(own_ref, got_ref, *outs):
    chunk = outs[0].shape[0] - PAD
    half = SIDE * chunk
    got = got_ref[half:, :].astype(F32)
    dots = own_ref[half : half + 1, :] + got[0:1] + got[1:2]
    high, low = split(dots)
    tail = jnp.concatenate([high, low, jnp.zeros((PAD - 2, dots.shape[1]), BF16)], axis=0)
    for d in range(SIDE):
        at = slice(d * chunk, (d + 1) * chunk)
        outs[d][:chunk, :] = (own_ref[at, :] + got_ref[at, :].astype(F32)).astype(BF16)
        outs[d][chunk:, :] = tail


def spread_body(in_ref, out_ref):
    members = in_ref.shape[0]
    total = sum(in_ref[i].astype(F32) for i in range(members)).astype(BF16)
    for i in range(members):
        out_ref[i] = total


def finish_body(heads, all_ref, qkv_out, proj_out):
    _, each, _ = all_ref.shape
    width = qkv_out.shape[2]
    step = 8

    def rows_of(row):
        m, k = divmod(row, each)
        return all_ref[m, k : k + step, :width].astype(F32)

    for i in range(0, HEAD_DIM, step):
        for h in range(heads):
            for j in range(3):
                at = h * HEAD_DIM + i
                qkv_out[j, at : at + step, :] = rows_of((h * 3 + j) * HEAD_DIM + i)
    for i in range(0, heads * HEAD_DIM, step):
        proj_out[i : i + step, :] = rows_of(3 * heads * HEAD_DIM + i)


def tie(value, *others):
    return lax.optimization_barrier((value, *others))[0]


def shards(frames, norm_gain, w_qkv, w_out, conv_kernel, grad_out):
    own_width, rows = frames.shape
    head_cols, width = w_qkv.shape[1:]
    heads = head_cols // HEAD_DIM
    members = lax.axis_size("tm")
    taps = conv_kernel.shape[0]
    span = SIDE * rows
    y, core = lax.axis_index("mp") // 2, lax.axis_index("mp") % 2
    steps = jnp.arange(SIDE, dtype=jnp.int32)
    cores = jnp.stack([core, 1 - core]).astype(jnp.int32)
    came = ((((y - steps + SIDE) % SIDE) * 2)[None, :] + cores[:, None]).reshape(-1)
    goes = ((((y + steps) % SIDE) * 2)[None, :] + cores[:, None]).reshape(-1)

    def with_swap(blocks):
        return blocks + [swap_core(jnp.concatenate(blocks, axis=0))]

    up_left, up_right = halos(grad_out)
    in_blocks = ring(shift_y, [frames] * SIDE, 1)
    back_sum, back_cast = call(
        back_kernel,
        [((own_width, rows), F32), ((own_width, rows), BF16)],
        [up_left, grad_out, up_right, conv_kernel], None,
        [
            pltpu.VMEM((rows + 2 * PAD, own_width), F32),
            pltpu.VMEM((rows, own_width), F32),
            pltpu.VMEM((STEP + 2 * PAD, own_width), F32),
        ],
        flops=8 * own_width * rows * taps,
    )
    in_blocks = list(lax.optimization_barrier((*in_blocks, back_cast)))
    back_cast = in_blocks.pop()
    in_blocks = with_swap(in_blocks)
    back_blocks = ring(shift_y, [back_cast] * SIDE, 1)
    normed, inverse, queries, keys_values = call(
        norm_body,
        [((width, rows), BF16), ((1, rows), F32), ((head_cols, rows), BF16), ((2 * head_cols, rows), BF16)],
        [came, *in_blocks, norm_gain[:, None], w_qkv], [SM] + [VM] * 7,
        flops=2 * 3 * head_cols * width * rows,
    )
    group_kv = ring(shift_z, [keys_values] * SIDE, 1)
    group_q = ring(shift_x, [queries] * SIDE, 1)

    back_blocks = list(lax.optimization_barrier((*back_blocks, keys_values)))[:SIDE]
    back_blocks = with_swap(back_blocks)
    back_full, grad_attn = call(
        back_arrange_body,
        [((width, rows), BF16), ((head_cols, rows), BF16)],
        [came, *back_blocks, w_out], [SM] + [VM] * 6,
        flops=2 * head_cols * width * rows,
    )
    group_g = ring(shift_x, [grad_attn] * SIDE, 1)

    part_out, part_lse = call(
        functools.partial(fwd_loop_body, heads),
        [((head_cols, span), BF16), ((heads, span), F32)],
        [tie(group_q[0], grad_attn), *group_q[1:], *group_kv], None,
        [
            pltpu.VMEM((heads, span, HEAD_DIM), BF16),
            pltpu.VMEM((head_cols, span), BF16),
            pltpu.VMEM((head_cols, span), BF16),
        ],
        flops=16 * head_cols * span * span, exps=heads * span * span,
    )
    (stats,) = call(
        functools.partial(stats_body, heads),
        [((8, span), F32)], [part_out, part_lse, *group_g],
    )
    peers = ring(shift_x, [stats] * SIDE, 1)
    wq_rel, wo_rel = call(
        prep_body,
        [((width, 3 * head_cols), BF16), ((width, head_cols), BF16)],
        [tie(goes, stats), w_qkv, w_out], [SM, VM, VM],
        [
            pltpu.VMEM((3 * head_cols, width), BF16),
            pltpu.VMEM((width, 3 * head_cols), BF16),
            pltpu.VMEM((width, head_cols), BF16),
        ],
    )
    logsum, offset, *out_blocks = call(
        functools.partial(combine_body, heads),
        [((8, span), F32), ((8, span), F32)] + [((head_cols, rows), BF16)] * SIDE,
        [tie(part_out, wo_rel), *peers],
    )
    out_terms = ring(shift_x, out_blocks, -1)

    q_block, k_block = min(1024, span), min(512, span)

    def head_grads(first, last, logsum, carried):
        count = last - first
        size = count * HEAD_DIM
        return call(
            functools.partial(bwd_body, first, last, heads, q_block, k_block),
            [((last * HEAD_DIM, rows), BF16)] * SIDE + [((2 * last * HEAD_DIM, rows), BF16)] * SIDE,
            [*group_q, *group_kv, *group_g, logsum, offset, *carried], None,
            [pltpu.VMEM((count, span, HEAD_DIM), BF16)] * 2
            + [pltpu.VMEM((size, span), BF16)] * 3
            + [pltpu.VMEM((8, span), F32)]
            + [pltpu.VMEM((size, span), F32)] * 3,
            flops=40 * size * span * span, exps=count * span * span,
        )

    early = head_grads(0, 1, logsum, ())
    half = SIDE * own_width
    attended, proj_own, proj_other = call(
        proj_body,
        [((head_cols, rows), BF16), ((half, rows), F32), ((half, rows), BF16)],
        [tie(out_terms[0], early[0]), *out_terms[1:], wo_rel],
        flops=2 * head_cols * width * rows,
    )
    proj_got = swap_core(proj_other)
    proj_blocks = call(pair_body, [((own_width, rows), BF16)] * SIDE, [proj_own, proj_got])
    proj_terms = ring(shift_y, proj_blocks, 1)

    grads = head_grads(1, heads, tie(logsum, *proj_blocks), early)
    dq, dkv = grads[:SIDE], grads[SIDE:]
    dkv_terms = ring(shift_z, dkv, -1)
    dq_terms = ring(shift_x, dq, -1)

    (out_part,) = call(
        out_weights_body, [((head_cols, width), BF16)],
        [tie(attended, dq[0]), back_full], flops=2 * head_cols * width * rows,
    )
    all_gp, part = call(
        functools.partial(weights_body, heads),
        [((3 * head_cols, rows), BF16), ((4 * head_cols, width), BF16)],
        [*dq_terms, *dkv_terms, normed, out_part],
        flops=2 * 3 * head_cols * width * rows,
    )
    each = part.shape[0] // members
    got = lax.all_to_all(part.reshape(members, each, width), "tm", 0, 0, tiled=True)

    gn_own, gn_other = call(
        functools.partial(grads_body, heads, width),
        [((half + 8, rows), F32), ((half + PAD, rows), BF16)],
        [tie(all_gp, part), queries, keys_values, wq_rel],
        flops=2 * 3 * head_cols * width * rows,
    )
    gn_got = swap_core(gn_other)
    gn_blocks = call(grads_pair_body, [((own_width + PAD, rows), BF16)] * SIDE, [gn_own, gn_got])
    gn_terms = ring(shift_y, gn_blocks, 1)

    mixed = sum(t.astype(F32) for t in [tie(proj_terms[0], *gn_blocks)] + proj_terms[1:])
    residual = (frames.astype(F32) + mixed).astype(BF16)
    res_left, res_right = halos(residual)
    (spread,) = call(spread_body, [((members, each, width), BF16)], [tie(got, res_left, res_right)])
    everything = lax.all_to_all(spread, "tm", 0, 0, tiled=True)
    block_out, kernel_part = call(
        conv_body,
        [((own_width, rows), BF16), ((taps, own_width), F32)],
        [tie(res_left, spread), residual, res_right, grad_out, conv_kernel], None,
        [
            pltpu.VMEM((rows + 2 * PAD, own_width), F32),
            pltpu.VMEM((rows, own_width), F32),
            pltpu.VMEM((taps, 8, own_width), F32),
            pltpu.VMEM((STEP + 2 * PAD, own_width), F32),
        ],
        flops=16 * own_width * rows * taps,
    )

    summed = sum(t.astype(F32) for t in [tie(gn_terms[0], spread)] + gn_terms[1:])
    grad_own = summed[:own_width]
    dots = summed[own_width : own_width + 1] + summed[own_width + 1 : own_width + 2]
    column_start = lax.axis_index("mp") * own_width
    gain_own = lax.dynamic_slice_in_dim(norm_gain, column_start, own_width, 0)[:, None]
    normed_own = frames.astype(F32) * inverse
    grad_frames = (
        back_sum + inverse * (grad_own * gain_own) - normed_own * inverse * dots
    ).astype(BF16)
    gain_part = jnp.sum(grad_own * normed_own, axis=1)
    small = jnp.concatenate([kernel_part.astype(BF16), gain_part.astype(BF16)[None]], axis=0)
    for shift in (shift_x, shift_z):
        small = sum(t.astype(F32) for t in ring(shift, [small] * SIDE, 1)).astype(BF16)
    small_sum = small.astype(F32)
    qkv_grads, out_grads = call(
        functools.partial(finish_body, heads),
        [((3, head_cols, width), F32), ((head_cols, width), F32)], [everything],
    )
    return block_out, grad_frames, small_sum[taps], qkv_grads, out_grads, small_sum[:taps]


def solution(mesh):
    return jax.shard_map(
        shards,
        mesh=mesh,
        in_specs=(
            P("mp", "tm"),
            P(),
            P(None, "mp", None),
            P("mp", None),
            P(None, "mp"),
            P("mp", "tm"),
        ),
        out_specs=(
            P("mp", "tm"),
            P("mp", "tm"),
            P("mp"),
            P(None, "mp", None),
            P("mp", None),
            P(None, "mp"),
        ),
        check_vma=False,
    )
```

```python
import functools

import jax
import jax.numpy as jnp
from jax import lax
from jax.experimental import pallas as pl
from jax.experimental.pallas import tpu as pltpu
from jax.sharding import PartitionSpec as P


HEAD_DIM = 64
SIDE = 4
PAD = 16
F32 = jnp.float32
BF16 = jnp.bfloat16


def nn(a, b):
    return jnp.dot(a, b, preferred_element_type=F32)


def nt(a, b):
    return lax.dot_general(a, b, (((1,), (1,)), ((), ())), preferred_element_type=F32)


VM = pl.BlockSpec(memory_space=pltpu.VMEM)


STEP = 64


def fill(pad_ref, left_ref, own_ref, right_ref):
    count = own_ref.shape[1]
    slab = left_ref.shape[1]
    pad_ref[PAD : PAD + count, :] = own_ref[...].astype(F32).T
    pad_ref[:PAD, :] = left_ref[...].astype(F32).T[slab - PAD :, :]
    pad_ref[PAD + count :, :] = right_ref[...].astype(F32).T[:PAD, :]


def back_kernel(left_ref, own_ref, right_ref, taps_ref, sum_ref, cast_ref, pad_ref, acc_ref, near):
    count = own_ref.shape[1]
    fill(pad_ref, left_ref, own_ref, right_ref)
    taps = taps_ref.shape[0]
    half = taps // 2

    def step(i, carry):
        base = pl.multiple_of(i * STEP, STEP)
        near[...] = pad_ref[pl.ds(base, STEP + 2 * PAD), :]
        acc = near[PAD : PAD + STEP, :]
        for j in range(taps):
            start = PAD + half - j
            acc = acc + taps_ref[j : j + 1, :] * near[start : start + STEP, :]
        acc_ref[pl.ds(base, STEP), :] = acc
        return carry

    lax.fori_loop(0, count // STEP, step, 0)
    acc = acc_ref[...].T
    sum_ref[...] = acc
    cast_ref[...] = acc.astype(BF16)


def conv_body(left_ref, own_ref, right_ref, up_ref, taps_ref, out_ref, grad_ref, pad_ref, upt_ref, sums, near):
    count = own_ref.shape[1]
    fill(pad_ref, left_ref, own_ref, right_ref)
    upt_ref[...] = up_ref[...].astype(F32).T
    taps = taps_ref.shape[0]
    half = taps // 2
    sums[...] = jnp.zeros_like(sums)

    def step(i, carry):
        base = pl.multiple_of(i * STEP, STEP)
        near[...] = pad_ref[pl.ds(base, STEP + 2 * PAD), :]
        acc = near[PAD : PAD + STEP, :]
        up = upt_ref[pl.ds(base, STEP), :]
        for j in range(taps):
            start = PAD + j - half
            part = near[start : start + STEP, :]
            acc = acc + taps_ref[j : j + 1, :] * part
            prod = up * part
            sums[j] += sum(prod[8 * s : 8 * s + 8] for s in range(STEP // 8))
        upt_ref[pl.ds(base, STEP), :] = acc
        return carry

    lax.fori_loop(0, count // STEP, step, 0)
    for j in range(taps):
        grad_ref[j : j + 1, :] = jnp.sum(sums[j], axis=0, keepdims=True)
    out_ref[...] = upt_ref[...].T.astype(BF16)


def shift_x(a, by):
    pairs = [
        (z * SIDE + x, z * SIDE + (x + by) % SIDE) for z in range(SIDE) for x in range(SIDE)
    ]
    return lax.ppermute(a, "tm", pairs)


def shift_z(a, by):
    pairs = [
        (z * SIDE + x, ((z + by) % SIDE) * SIDE + x) for z in range(SIDE) for x in range(SIDE)
    ]
    return lax.ppermute(a, "tm", pairs)


def halos(a, slab=128):
    count = lax.axis_size("tm")
    ends = count - 1
    left = lax.ppermute(a[:, a.shape[1] - slab :], "tm", [(i, i + 1) for i in range(ends)])
    right = lax.ppermute(a[:, :slab], "tm", [(i + 1, i) for i in range(ends)])
    return left, right


SM = pl.BlockSpec(memory_space=pltpu.SMEM)


def shift_y(a, by):
    count = lax.axis_size("mp") // 2
    pairs = [(y * 2 + c, ((y + by) % count) * 2 + c) for y in range(count) for c in range(2)]
    return lax.ppermute(a, "mp", pairs)


def swap_core(a):
    count = lax.axis_size("mp")
    return lax.ppermute(a, "mp", [(i, i ^ 1) for i in range(count)])


def call(body, outs, args, specs=None, scratch=(), flops=0, exps=0):
    out_shape = tuple(jax.ShapeDtypeStruct(s, t) for s, t in outs)
    moved = sum(a.size * a.dtype.itemsize for a in args)
    moved += sum(o.size * o.dtype.itemsize for o in out_shape)
    return pl.pallas_call(
        body,
        out_shape=out_shape,
        in_specs=specs or [VM] * len(args),
        out_specs=[VM] * len(outs),
        scratch_shapes=list(scratch),
        cost_estimate=pl.CostEstimate(flops=flops, bytes_accessed=moved, transcendentals=exps),
    )(*args)


def ring(shift, blocks, sign):
    return [blocks[0]] + [shift(blocks[r], sign * r) for r in range(1, SIDE)]


def head_rows(h):
    return slice(h * HEAD_DIM, (h + 1) * HEAD_DIM)


def prep_body(pos_ref, w_ref, wo_ref, wq_out, wo_out, mixed, turned, turned_out):
    head_cols, width = wo_ref.shape
    heads = head_cols // HEAD_DIM
    for h in range(heads):
        for j in range(3):
            at = (h * 3 + j) * HEAD_DIM
            mixed[at : at + HEAD_DIM, :] = w_ref[j, head_rows(h), :]
    lanes = 128

    def turn(i, carry):
        cols = pl.ds(pl.multiple_of(i * lanes, lanes), lanes)
        turned[cols, :] = mixed[:, cols].T
        turned_out[cols, :] = wo_ref[:, cols].T
        return carry

    lax.fori_loop(0, width // lanes, turn, 0)
    chunk = width // 8
    for r in range(8):
        rows = pl.ds(pl.multiple_of(pos_ref[r] * chunk, chunk), chunk)
        wq_out[r * chunk : (r + 1) * chunk, :] = turned[rows, :]
        wo_out[r * chunk : (r + 1) * chunk, :] = turned_out[rows, :]


def norm_body(pos_ref, b0, b1, b2, b3, other, gain_ref, w_ref, normed_out, inv_out, q_out, kv_out):
    own = [b0, b1, b2, b3]
    chunk, rows = b0.shape
    width = normed_out.shape[0]

    def block(r):
        part = own[r][...] if r < 4 else other[(r - 4) * chunk : (r - 3) * chunk, :]
        return part.astype(F32)

    total = jnp.zeros((1, rows), F32)
    for r in range(8):
        x = block(r)
        total = total + jnp.sum(x * x, axis=0, keepdims=True)
    inverse = lax.rsqrt(total / width + 1e-06)
    inv_out[...] = inverse
    for r in range(8):
        at = pl.ds(pl.multiple_of(pos_ref[r] * chunk, chunk), chunk)
        normed_out[at, :] = (block(r) * inverse * gain_ref[at, :]).astype(BF16)
    normed = normed_out[...]
    q_out[...] = nn(w_ref[0], normed).astype(BF16) * jnp.asarray(HEAD_DIM ** (-0.5), BF16)
    head_cols = q_out.shape[0]
    for j in (1, 2):
        kv_out[(j - 1) * head_cols : j * head_cols, :] = nn(w_ref[j], normed).astype(BF16)


def back_arrange_body(pos_ref, b0, b1, b2, b3, other, wo_ref, full_out, grad_out):
    own = [b0, b1, b2, b3]
    chunk = b0.shape[0]
    for r in range(8):
        at = pl.ds(pl.multiple_of(pos_ref[r] * chunk, chunk), chunk)
        full_out[at, :] = own[r][...] if r < 4 else other[(r - 4) * chunk : (r - 3) * chunk, :]
    grad_out[...] = nn(wo_ref[...], full_out[...]).astype(BF16)


def fwd_loop_body(heads, *refs):
    q_refs, kv_refs = refs[:SIDE], refs[SIDE : 2 * SIDE]
    o_ref, lse_ref, keys, vals, queries = refs[2 * SIDE :]
    rows = q_refs[0].shape[1]
    width = heads * HEAD_DIM
    for r in range(SIDE):
        cols = slice(r * rows, (r + 1) * rows)
        vals[:, cols] = kv_refs[r][width:, :]
        queries[:, cols] = q_refs[r][...]
        for h in range(heads):
            keys[h, cols, :] = kv_refs[r][head_rows(h), :].T

    def step(r, carry):
        cols = pl.ds(pl.multiple_of(r * rows, rows), rows)
        for h in range(heads):
            at = head_rows(h)
            scores = nn(keys[h], queries[at, cols])
            top = jnp.max(scores, axis=0, keepdims=True)
            weights = jnp.exp(scores - top)
            total = jnp.sum(weights, axis=0, keepdims=True)
            out = nn(vals[at, :], weights.astype(BF16)) / total
            o_ref[at, cols] = out.astype(BF16)
            lse_ref[h : h + 1, cols] = top + jnp.log(total)
        return carry

    lax.fori_loop(0, SIDE, step, 0)


def stats_body(heads, o_ref, lse_ref, *refs):
    g_refs, out_ref = refs[:SIDE], refs[SIDE]
    rows = g_refs[0].shape[1]
    out_ref[...] = jnp.zeros_like(out_ref)
    out_ref[:heads, :] = lse_ref[...]
    for r in range(SIDE):
        cols = slice(r * rows, (r + 1) * rows)
        for h in range(heads):
            at = head_rows(h)
            out_ref[heads + h : heads + h + 1, cols] = jnp.sum(
                o_ref[at, cols].astype(F32) * g_refs[r][at, :].astype(F32), axis=0, keepdims=True
            )


def combine_body(heads, o_ref, *refs):
    peers, outs = refs[:SIDE], refs[SIDE:]
    lse_out, off_out, blocks = outs[0], outs[1], outs[2:]
    rows = o_ref.shape[1] // SIDE
    for r in range(SIDE):
        cols = slice(r * rows, (r + 1) * rows)
        theirs = []
        for s in range(SIDE):
            at = (r - s) % SIDE
            theirs.append(peers[s][:, at * rows : (at + 1) * rows])
        lse = [t[:heads] for t in theirs]
        off = [t[heads : 2 * heads] for t in theirs]
        top = jnp.maximum(jnp.maximum(lse[0], lse[1]), jnp.maximum(lse[2], lse[3]))
        logsum = top + jnp.log(sum(jnp.exp(v - top) for v in lse))
        shares = [jnp.exp(v - logsum) for v in lse]
        lse_out[:heads, cols] = logsum
        off_out[:heads, cols] = sum(w * v for w, v in zip(shares, off))
        for h in range(heads):
            at = head_rows(h)
            blocks[r][at, :] = (o_ref[at, cols].astype(F32) * shares[0][h : h + 1]).astype(BF16)


def bwd_body(first, last, heads, q_block, k_block, *refs):
    q_refs, kv_refs, g_refs = refs[:SIDE], refs[SIDE : 2 * SIDE], refs[2 * SIDE : 3 * SIDE]
    lse_ref, off_ref = refs[3 * SIDE : 3 * SIDE + 2]
    refs = refs[3 * SIDE + 2 :]
    carried = refs[: 2 * SIDE] if first else ()
    refs = refs[len(carried) :]
    dq_refs, dkv_refs = refs[:SIDE], refs[SIDE : 2 * SIDE]
    keys, vals, kt, qt, gt, stat, dq, dk, dv = refs[2 * SIDE :]
    count = last - first
    rows = q_refs[0].shape[1]
    span = SIDE * rows
    mine = slice(first * HEAD_DIM, last * HEAD_DIM)
    for r in range(SIDE):
        cols = slice(r * rows, (r + 1) * rows)
        qt[:, cols] = q_refs[r][mine, :]
        gt[:, cols] = g_refs[r][mine, :]
        kt[:, cols] = kv_refs[r][mine, :]
        for h in range(count):
            keys[h, cols, :] = kv_refs[r][head_rows(first + h), :].T
            vals[h, cols, :] = kv_refs[r][head_rows(heads + first + h), :].T
    for h in range(count):
        stat[h : h + 1, :] = lse_ref[first + h : first + h + 1, :]
        stat[count + h : count + h + 1, :] = off_ref[first + h : first + h + 1, :]
    dk[...] = jnp.zeros_like(dk)
    dv[...] = jnp.zeros_like(dv)
    dq[...] = jnp.zeros_like(dq)

    def q_step(qi, carry):
        q_cols = pl.ds(pl.multiple_of(qi * q_block, q_block), q_block)

        def k_step(ki, carry):
            k_rows = pl.ds(pl.multiple_of(ki * k_block, k_block), k_block)
            for h in range(count):
                at = head_rows(h)
                q = qt[at, q_cols]
                g = gt[at, q_cols]
                scores = nn(keys[h, k_rows, :], q)
                prob = jnp.exp(scores - stat[h : h + 1, q_cols])
                grad_prob = nn(vals[h, k_rows, :], g)
                off = stat[count + h : count + h + 1, q_cols]
                grad_score = (prob * (grad_prob - off)).astype(BF16)
                dq[at, q_cols] += nn(kt[at, k_rows], grad_score)
                dk[at, k_rows] += nt(q, grad_score)
                dv[at, k_rows] += nt(g, prob.astype(BF16))
            return carry

        lax.fori_loop(0, span // k_block, k_step, 0)
        return carry

    lax.fori_loop(0, span // q_block, q_step, 0)
    done = first * HEAD_DIM
    for r in range(SIDE):
        cols = slice(r * rows, (r + 1) * rows)
        dq_refs[r][done:, :] = (dq[:, cols] * HEAD_DIM ** (-0.5)).astype(BF16)
        half = last * HEAD_DIM
        dkv_refs[r][done:half, :] = dk[:, cols].astype(BF16)
        dkv_refs[r][half + done :, :] = dv[:, cols].astype(BF16)
        if first:
            dq_refs[r][:done, :] = carried[r][...]
            dkv_refs[r][:done, :] = carried[SIDE + r][:done, :]
            dkv_refs[r][half : half + done, :] = carried[SIDE + r][done:, :]


def sum_terms(refs):
    return sum(t[...].astype(F32) for t in refs)


def proj_body(*refs):
    terms, wo_ref = refs[:SIDE], refs[SIDE]
    att_out, own_out, other_out = refs[SIDE + 1 :]
    attended = sum_terms(terms).astype(BF16)
    half = own_out.shape[0]
    chunk = half // SIDE

    def step(d, carry):
        at = pl.multiple_of(d * chunk, chunk)
        rows = pl.ds(at, chunk)
        other_out[rows, :] = nn(wo_ref[pl.ds(half + at, chunk), :], attended).astype(BF16)
        own_out[rows, :] = nn(wo_ref[rows, :], attended)
        return carry

    lax.fori_loop(0, SIDE, step, 0)
    att_out[...] = attended


def out_weights_body(att_ref, full_ref, part_out):
    part_out[...] = nt(att_ref[...], full_ref[...]).astype(BF16)


def pair_body(own_ref, got_ref, *outs):
    chunk = outs[0].shape[0]
    for d in range(SIDE):
        at = slice(d * chunk, (d + 1) * chunk)
        outs[d][...] = (own_ref[at, :] + got_ref[at, :].astype(F32)).astype(BF16)


def weights_body(heads, *refs):
    dq, dkv = refs[:SIDE], refs[SIDE : 2 * SIDE]
    normed_ref, out_part_ref, gp_out, part_out = refs[2 * SIDE :]
    width = heads * HEAD_DIM
    grad_q = sum_terms(dq).astype(BF16)
    grad_kv = sum_terms(dkv).astype(BF16)
    for h in range(heads):
        at = h * 3 * HEAD_DIM
        gp_out[at : at + HEAD_DIM, :] = grad_q[head_rows(h)]
        gp_out[at + HEAD_DIM : at + 2 * HEAD_DIM, :] = grad_kv[head_rows(h)]
        gp_out[at + 2 * HEAD_DIM : at + 3 * HEAD_DIM, :] = grad_kv[head_rows(heads + h)]

    def step(h, carry):
        rows = pl.ds(pl.multiple_of(h * 3 * HEAD_DIM, 3 * HEAD_DIM), 3 * HEAD_DIM)
        part_out[rows, :] = nt(gp_out[rows, :], normed_ref[...]).astype(BF16)
        return carry

    lax.fori_loop(0, heads, step, 0)
    part_out[3 * width :, :] = out_part_ref[...]


def split(v):
    high = v.astype(BF16)
    return high, (v - high.astype(F32)).astype(BF16)


def grads_body(heads, width, all_gp, q_ref, kv_ref, wq_ref, own_out, other_out):
    size = 3 * HEAD_DIM
    dots = jnp.zeros((1, q_ref.shape[1]), F32)
    for h in range(heads):
        at = h * size
        gp = all_gp[at : at + size, :].astype(F32)
        q = q_ref[head_rows(h), :].astype(F32) * HEAD_DIM**0.5
        k = kv_ref[head_rows(h), :].astype(F32)
        v = kv_ref[head_rows(heads + h), :].astype(F32)
        for j, held in enumerate((q, k, v)):
            dots = dots + jnp.sum(
                gp[j * HEAD_DIM : (j + 1) * HEAD_DIM] * held, axis=0, keepdims=True
            )
    dots = dots / width
    half = wq_ref.shape[0] // 2
    chunk = half // SIDE

    def step(d, carry):
        at = pl.multiple_of(d * chunk, chunk)
        rows = pl.ds(at, chunk)
        other_out[rows, :] = nn(wq_ref[pl.ds(half + at, chunk), :], all_gp[...]).astype(BF16)
        own_out[rows, :] = nn(wq_ref[rows, :], all_gp[...])
        return carry

    lax.fori_loop(0, SIDE, step, 0)
    high, low = split(dots)
    other_out[half:, :] = jnp.concatenate(
        [high, low, jnp.zeros((PAD - 2, dots.shape[1]), BF16)], axis=0
    )
    own_out[half:, :] = jnp.broadcast_to(dots, (8, dots.shape[1]))


def grads_pair_body(own_ref, got_ref, *outs):
    chunk = outs[0].shape[0] - PAD
    half = SIDE * chunk
    got = got_ref[half:, :].astype(F32)
    dots = own_ref[half : half + 1, :] + got[0:1] + got[1:2]
    high, low = split(dots)
    tail = jnp.concatenate([high, low, jnp.zeros((PAD - 2, dots.shape[1]), BF16)], axis=0)
    for d in range(SIDE):
        at = slice(d * chunk, (d + 1) * chunk)
        outs[d][:chunk, :] = (own_ref[at, :] + got_ref[at, :].astype(F32)).astype(BF16)
        outs[d][chunk:, :] = tail


def reduce_body(in_ref, small_ref, first_out, second_out):
    members, rows, width = in_ref.shape
    half = rows // 2
    lanes = 256

    def step(i, carry):
        cols = pl.ds(pl.multiple_of(i * lanes, lanes), lanes)
        total = sum(in_ref[m, :, cols].astype(F32) for m in range(members)).astype(BF16)
        first_out[:, cols] = total[:half]
        second_out[:, cols] = total[half:]
        return carry

    lax.fori_loop(0, width // lanes, step, 0)
    first_out[:, width:] = small_ref[:half, :]
    second_out[:, width:] = small_ref[half:, :]


def finish_body(heads, pos_ref, *refs):
    firsts, seconds = refs[:SIDE], refs[SIDE : 2 * SIDE]
    qkv_out, proj_out, small_out, held = refs[2 * SIDE :]
    half = firsts[0].shape[1]
    each = 2 * half
    width = qkv_out.shape[2]
    step = 8
    small_out[...] = jnp.zeros_like(small_out)
    for d in range(SIDE):

        def place(e, carry):
            held[pos_ref[d * SIDE + e], :half, :] = firsts[d][e, :, :width].astype(F32)
            held[pos_ref[e * SIDE + d], half:, :] = seconds[d][e, :, :width].astype(F32)
            small_out[:half, :] += firsts[d][e, :, width:].astype(F32)
            small_out[half:, :] += seconds[d][e, :, width:].astype(F32)
            return carry

        lax.fori_loop(0, SIDE, place, 0)

    def rows_of(row):
        return held[lax.div(row, each), pl.ds(pl.multiple_of(lax.rem(row, each), step), step), :]

    def write_qkv(g, carry):
        row = g * step
        block = lax.div(row, HEAD_DIM)
        at = lax.div(block, 3) * HEAD_DIM + lax.rem(row, HEAD_DIM)
        qkv_out[lax.rem(block, 3), pl.ds(pl.multiple_of(at, step), step), :] = rows_of(row)
        return carry

    def write_proj(g, carry):
        row = g * step
        proj_out[pl.ds(pl.multiple_of(row, step), step), :] = rows_of(row + 3 * heads * HEAD_DIM)
        return carry

    lax.fori_loop(0, 3 * heads * HEAD_DIM // step, write_qkv, 0)
    lax.fori_loop(0, heads * HEAD_DIM // step, write_proj, 0)


def tie(value, *others):
    return lax.optimization_barrier((value, *others))[0]


def shards(frames, norm_gain, w_qkv, w_out, conv_kernel, grad_out):
    own_width, rows = frames.shape
    head_cols, width = w_qkv.shape[1:]
    heads = head_cols // HEAD_DIM
    members = lax.axis_size("tm")
    taps = conv_kernel.shape[0]
    span = SIDE * rows
    y, core = lax.axis_index("mp") // 2, lax.axis_index("mp") % 2
    steps = jnp.arange(SIDE, dtype=jnp.int32)
    cores = jnp.stack([core, 1 - core]).astype(jnp.int32)
    came = ((((y - steps + SIDE) % SIDE) * 2)[None, :] + cores[:, None]).reshape(-1)
    goes = ((((y + steps) % SIDE) * 2)[None, :] + cores[:, None]).reshape(-1)

    def with_swap(blocks):
        return blocks + [swap_core(jnp.concatenate(blocks, axis=0))]

    up_left, up_right = halos(grad_out)
    in_blocks = ring(shift_y, [frames] * SIDE, 1)
    back_sum, back_cast = call(
        back_kernel,
        [((own_width, rows), F32), ((own_width, rows), BF16)],
        [up_left, grad_out, up_right, conv_kernel], None,
        [
            pltpu.VMEM((rows + 2 * PAD, own_width), F32),
            pltpu.VMEM((rows, own_width), F32),
            pltpu.VMEM((STEP + 2 * PAD, own_width), F32),
        ],
        flops=8 * own_width * rows * taps,
    )
    in_blocks = list(lax.optimization_barrier((*in_blocks, back_cast)))
    back_cast = in_blocks.pop()
    in_blocks = with_swap(in_blocks)
    back_blocks = ring(shift_y, [back_cast] * SIDE, 1)
    normed, inverse, queries, keys_values = call(
        norm_body,
        [((width, rows), BF16), ((1, rows), F32), ((head_cols, rows), BF16), ((2 * head_cols, rows), BF16)],
        [came, *in_blocks, norm_gain[:, None], w_qkv], [SM] + [VM] * 7,
        flops=2 * 3 * head_cols * width * rows,
    )
    group_kv = ring(shift_z, [keys_values] * SIDE, 1)
    group_q = ring(shift_x, [queries] * SIDE, 1)

    back_blocks = list(lax.optimization_barrier((*back_blocks, keys_values)))[:SIDE]
    back_blocks = with_swap(back_blocks)
    back_full, grad_attn = call(
        back_arrange_body,
        [((width, rows), BF16), ((head_cols, rows), BF16)],
        [came, *back_blocks, w_out], [SM] + [VM] * 6,
        flops=2 * head_cols * width * rows,
    )
    group_g = ring(shift_x, [grad_attn] * SIDE, 1)

    part_out, part_lse = call(
        functools.partial(fwd_loop_body, heads),
        [((head_cols, span), BF16), ((heads, span), F32)],
        [tie(group_q[0], grad_attn), *group_q[1:], *group_kv], None,
        [
            pltpu.VMEM((heads, span, HEAD_DIM), BF16),
            pltpu.VMEM((head_cols, span), BF16),
            pltpu.VMEM((head_cols, span), BF16),
        ],
        flops=16 * head_cols * span * span, exps=heads * span * span,
    )
    (stats,) = call(
        functools.partial(stats_body, heads),
        [((8, span), F32)], [part_out, part_lse, *group_g],
    )
    peers = ring(shift_x, [stats] * SIDE, 1)
    wq_rel, wo_rel = call(
        prep_body,
        [((width, 3 * head_cols), BF16), ((width, head_cols), BF16)],
        [tie(goes, stats), w_qkv, w_out], [SM, VM, VM],
        [
            pltpu.VMEM((3 * head_cols, width), BF16),
            pltpu.VMEM((width, 3 * head_cols), BF16),
            pltpu.VMEM((width, head_cols), BF16),
        ],
    )
    logsum, offset, *out_blocks = call(
        functools.partial(combine_body, heads),
        [((8, span), F32), ((8, span), F32)] + [((head_cols, rows), BF16)] * SIDE,
        [tie(part_out, wo_rel), *peers],
    )
    out_terms = ring(shift_x, out_blocks, -1)

    q_block, k_block = min(256, span), min(2048, span)

    def head_grads(first, last, logsum, carried):
        count = last - first
        size = count * HEAD_DIM
        return call(
            functools.partial(bwd_body, first, last, heads, q_block, k_block),
            [((last * HEAD_DIM, rows), BF16)] * SIDE + [((2 * last * HEAD_DIM, rows), BF16)] * SIDE,
            [*group_q, *group_kv, *group_g, logsum, offset, *carried], None,
            [pltpu.VMEM((count, span, HEAD_DIM), BF16)] * 2
            + [pltpu.VMEM((size, span), BF16)] * 3
            + [pltpu.VMEM((8, span), F32)]
            + [pltpu.VMEM((size, span), F32)] * 3,
            flops=40 * size * span * span, exps=count * span * span,
        )

    early = head_grads(0, 1, logsum, ())
    half = SIDE * own_width
    attended, proj_own, proj_other = call(
        proj_body,
        [((head_cols, rows), BF16), ((half, rows), F32), ((half, rows), BF16)],
        [tie(out_terms[0], early[0]), *out_terms[1:], wo_rel],
        flops=2 * head_cols * width * rows,
    )
    proj_got = swap_core(proj_other)
    proj_blocks = call(pair_body, [((own_width, rows), BF16)] * SIDE, [proj_own, proj_got])
    proj_terms = ring(shift_y, proj_blocks, 1)

    grads = head_grads(1, heads, tie(logsum, *proj_blocks), early)
    dq, dkv = grads[:SIDE], grads[SIDE:]
    dkv_terms = ring(shift_z, dkv, -1)
    dq_terms = ring(shift_x, dq, -1)

    mixed = sum(t.astype(F32) for t in [tie(proj_terms[0], dq[0])] + proj_terms[1:])
    residual = (frames.astype(F32) + mixed).astype(BF16)
    res_left, res_right = halos(residual)
    (out_part,) = call(
        out_weights_body, [((head_cols, width), BF16)],
        [tie(attended, dq[0]), back_full], flops=2 * head_cols * width * rows,
    )
    all_gp, part = call(
        functools.partial(weights_body, heads),
        [((3 * head_cols, rows), BF16), ((4 * head_cols, width), BF16)],
        [*dq_terms, *dkv_terms, normed, tie(out_part, res_left, res_right)],
        flops=2 * 3 * head_cols * width * rows,
    )
    each = part.shape[0] // members
    got = lax.all_to_all(part.reshape(members, each, width), "tm", 0, 0, tiled=True)

    gn_own, gn_other = call(
        functools.partial(grads_body, heads, width),
        [((half + 8, rows), F32), ((half + PAD, rows), BF16)],
        [tie(all_gp, part), queries, keys_values, wq_rel],
        flops=2 * 3 * head_cols * width * rows,
    )
    gn_got = swap_core(gn_other)
    gn_blocks = call(grads_pair_body, [((own_width + PAD, rows), BF16)] * SIDE, [gn_own, gn_got])
    gn_terms = ring(shift_y, gn_blocks, 1)
    block_out, kernel_part = call(
        conv_body,
        [((own_width, rows), BF16), ((taps, own_width), F32)],
        [tie(res_left, *gn_blocks), residual, res_right, grad_out, conv_kernel], None,
        [
            pltpu.VMEM((rows + 2 * PAD, own_width), F32),
            pltpu.VMEM((rows, own_width), F32),
            pltpu.VMEM((taps, 8, own_width), F32),
            pltpu.VMEM((STEP + 2 * PAD, own_width), F32),
        ],
        flops=16 * own_width * rows * taps,
    )

    summed = sum(t.astype(F32) for t in [tie(gn_terms[0], kernel_part)] + gn_terms[1:])
    grad_own = summed[:own_width]
    dots = summed[own_width : own_width + 1] + summed[own_width + 1 : own_width + 2]
    column_start = lax.axis_index("mp") * own_width
    gain_own = lax.dynamic_slice_in_dim(norm_gain, column_start, own_width, 0)[:, None]
    normed_own = frames.astype(F32) * inverse
    grad_frames = (
        back_sum + inverse * (grad_own * gain_own) - normed_own * inverse * dots
    ).astype(BF16)
    gain_part = jnp.sum(grad_own * normed_own, axis=1)
    small = jnp.concatenate([kernel_part.astype(BF16), gain_part.astype(BF16)[None]], axis=0)
    small_cols = small.size // each
    first, second = call(
        reduce_body, [((each // 2, width + small_cols), BF16)] * 2,
        [got, small.reshape(each, small_cols)],
    )
    first_row = jnp.stack(ring(shift_x, [first] * SIDE, 1))
    second_row = jnp.stack(ring(shift_z, [second] * SIDE, 1))
    first_all = ring(shift_z, [first_row] * SIDE, 1)
    second_all = ring(shift_x, [second_row] * SIDE, 1)
    z, x = lax.axis_index("tm") // SIDE, lax.axis_index("tm") % SIDE
    held_at = ((z - steps + SIDE) % SIDE * SIDE)[:, None] + ((x - steps + SIDE) % SIDE)[None, :]
    qkv_grads, out_grads, small_sum = call(
        functools.partial(finish_body, heads),
        [((3, head_cols, width), F32), ((head_cols, width), F32), ((each, small_cols), F32)],
        [held_at.reshape(-1).astype(jnp.int32), *first_all, *second_all], [SM] + [VM] * 2 * SIDE,
        [pltpu.VMEM((members, each, width), F32)],
    )
    small_sum = small_sum.reshape(taps + 1, own_width)
    return block_out, grad_frames, small_sum[taps], qkv_grads, out_grads, small_sum[:taps]


def solution(mesh):
    return jax.shard_map(
        shards,
        mesh=mesh,
        in_specs=(
            P("mp", "tm"),
            P(),
            P(None, "mp", None),
            P("mp", None),
            P(None, "mp"),
            P("mp", "tm"),
        ),
        out_specs=(
            P("mp", "tm"),
            P("mp", "tm"),
            P("mp"),
            P(None, "mp", None),
            P("mp", None),
            P(None, "mp"),
        ),
        check_vma=False,
    )
```

```python
import functools

import jax
import jax.numpy as jnp
from jax import lax
from jax.experimental import pallas as pl
from jax.experimental.pallas import tpu as pltpu
from jax.sharding import PartitionSpec as P


HEAD_DIM = 64
SIDE = 4
PAD = 16
F32 = jnp.float32
BF16 = jnp.bfloat16


def nn(a, b):
    return jnp.dot(a, b, preferred_element_type=F32)


def nt(a, b):
    return lax.dot_general(a, b, (((1,), (1,)), ((), ())), preferred_element_type=F32)


VM = pl.BlockSpec(memory_space=pltpu.VMEM)


STEP = 64


def fill(pad_ref, left_ref, own_ref, right_ref):
    count = own_ref.shape[1]
    slab = left_ref.shape[1]
    pad_ref[PAD : PAD + count, :] = own_ref[...].astype(F32).T
    pad_ref[:PAD, :] = left_ref[...].astype(F32).T[slab - PAD :, :]
    pad_ref[PAD + count :, :] = right_ref[...].astype(F32).T[:PAD, :]


def back_kernel(left_ref, own_ref, right_ref, taps_ref, sum_ref, cast_ref, pad_ref, acc_ref, near):
    count = own_ref.shape[1]
    fill(pad_ref, left_ref, own_ref, right_ref)
    taps = taps_ref.shape[0]
    half = taps // 2

    def step(i, carry):
        base = pl.multiple_of(i * STEP, STEP)
        near[...] = pad_ref[pl.ds(base, STEP + 2 * PAD), :]
        acc = near[PAD : PAD + STEP, :]
        for j in range(taps):
            start = PAD + half - j
            acc = acc + taps_ref[j : j + 1, :] * near[start : start + STEP, :]
        acc_ref[pl.ds(base, STEP), :] = acc
        return carry

    lax.fori_loop(0, count // STEP, step, 0)
    acc = acc_ref[...].T
    sum_ref[...] = acc
    cast_ref[...] = acc.astype(BF16)


def conv_body(left_ref, own_ref, right_ref, up_ref, taps_ref, out_ref, grad_ref, pad_ref, upt_ref, sums, near):
    count = own_ref.shape[1]
    fill(pad_ref, left_ref, own_ref, right_ref)
    upt_ref[...] = up_ref[...].astype(F32).T
    taps = taps_ref.shape[0]
    half = taps // 2
    sums[...] = jnp.zeros_like(sums)

    def step(i, carry):
        base = pl.multiple_of(i * STEP, STEP)
        near[...] = pad_ref[pl.ds(base, STEP + 2 * PAD), :]
        acc = near[PAD : PAD + STEP, :]
        up = upt_ref[pl.ds(base, STEP), :]
        for j in range(taps):
            start = PAD + j - half
            part = near[start : start + STEP, :]
            acc = acc + taps_ref[j : j + 1, :] * part
            prod = up * part
            sums[j] += sum(prod[8 * s : 8 * s + 8] for s in range(STEP // 8))
        upt_ref[pl.ds(base, STEP), :] = acc
        return carry

    lax.fori_loop(0, count // STEP, step, 0)
    for j in range(taps):
        grad_ref[j : j + 1, :] = jnp.sum(sums[j], axis=0, keepdims=True)
    out_ref[...] = upt_ref[...].T.astype(BF16)


def shift_x(a, by):
    pairs = [
        (z * SIDE + x, z * SIDE + (x + by) % SIDE) for z in range(SIDE) for x in range(SIDE)
    ]
    return lax.ppermute(a, "tm", pairs)


def shift_z(a, by):
    pairs = [
        (z * SIDE + x, ((z + by) % SIDE) * SIDE + x) for z in range(SIDE) for x in range(SIDE)
    ]
    return lax.ppermute(a, "tm", pairs)


def halos(a, slab=128):
    count = lax.axis_size("tm")
    ends = count - 1
    left = lax.ppermute(a[:, a.shape[1] - slab :], "tm", [(i, i + 1) for i in range(ends)])
    right = lax.ppermute(a[:, :slab], "tm", [(i + 1, i) for i in range(ends)])
    return left, right


def place_mp(step, core_step):
    index = lax.axis_index("mp")
    y, core = lax.div(index, 2), lax.rem(index, 2)
    core = 1 - core if core_step else core
    return lax.rem(y + step + SIDE, SIDE) * 2 + core


def place_tm(dz, dx):
    index = lax.axis_index("tm")
    z, x = lax.div(index, SIDE), lax.rem(index, SIDE)
    return lax.rem(z - dz + SIDE, SIDE) * SIDE + lax.rem(x - dx + SIDE, SIDE)


def shift_y(a, by):
    count = lax.axis_size("mp") // 2
    pairs = [(y * 2 + c, ((y + by) % count) * 2 + c) for y in range(count) for c in range(2)]
    return lax.ppermute(a, "mp", pairs)


def swap_core(a):
    count = lax.axis_size("mp")
    return lax.ppermute(a, "mp", [(i, i ^ 1) for i in range(count)])


def call(body, outs, args, specs=None, scratch=(), flops=0, exps=0):
    out_shape = tuple(jax.ShapeDtypeStruct(s, t) for s, t in outs)
    moved = sum(a.size * a.dtype.itemsize for a in args)
    moved += sum(o.size * o.dtype.itemsize for o in out_shape)
    return pl.pallas_call(
        body,
        out_shape=out_shape,
        in_specs=specs or [VM] * len(args),
        out_specs=[VM] * len(outs),
        scratch_shapes=list(scratch),
        cost_estimate=pl.CostEstimate(flops=flops, bytes_accessed=moved, transcendentals=exps),
    )(*args)


def ring(shift, blocks, sign):
    return [blocks[0]] + [shift(blocks[r], sign * r) for r in range(1, SIDE)]


def head_rows(h):
    return slice(h * HEAD_DIM, (h + 1) * HEAD_DIM)


def prep_body(after_ref, w_ref, wo_ref, wq_out, wo_out, mixed, turned, turned_out):
    head_cols, width = wo_ref.shape
    heads = head_cols // HEAD_DIM
    for h in range(heads):
        for j in range(3):
            at = (h * 3 + j) * HEAD_DIM
            mixed[at : at + HEAD_DIM, :] = w_ref[j, head_rows(h), :]
    lanes = 128

    def turn(i, carry):
        cols = pl.ds(pl.multiple_of(i * lanes, lanes), lanes)
        turned[cols, :] = mixed[:, cols].T
        turned_out[cols, :] = wo_ref[:, cols].T
        return carry

    lax.fori_loop(0, width // lanes, turn, 0)
    chunk = width // 8
    for r in range(8):
        at = place_mp(r % SIDE, r // SIDE)
        rows = pl.ds(pl.multiple_of(at * chunk, chunk), chunk)
        wq_out[r * chunk : (r + 1) * chunk, :] = turned[rows, :]
        wo_out[r * chunk : (r + 1) * chunk, :] = turned_out[rows, :]


def norm_body(b0, b1, b2, b3, other, gain_ref, w_ref, normed_out, inv_out, q_out, kv_out, gain):
    own = [b0, b1, b2, b3]
    chunk, rows = b0.shape
    width = normed_out.shape[0]

    def block(r):
        part = own[r][...] if r < 4 else other[(r - 4) * chunk : (r - 3) * chunk, :]
        return part.astype(F32)

    gain[...] = jnp.broadcast_to(gain_ref[...], (8, width)).T
    total = jnp.zeros((1, rows), F32)
    for r in range(8):
        x = block(r)
        total = total + jnp.sum(x * x, axis=0, keepdims=True)
    inverse = lax.rsqrt(total / width + 1e-06)
    inv_out[...] = inverse
    for r in range(8):
        at = pl.ds(pl.multiple_of(place_mp(-(r % SIDE), r // SIDE) * chunk, chunk), chunk)
        normed_out[at, :] = (block(r) * inverse * gain[at, :1]).astype(BF16)
    normed = normed_out[...]
    q_out[...] = nn(w_ref[0], normed).astype(BF16) * jnp.asarray(HEAD_DIM ** (-0.5), BF16)
    head_cols = q_out.shape[0]

    def step(j, carry):
        at = pl.ds(pl.multiple_of((j - 1) * head_cols, head_cols), head_cols)
        kv_out[at, :] = nn(w_ref[j], normed_out[...]).astype(BF16)
        return carry

    lax.fori_loop(1, 3, step, 0)


def back_arrange_body(b0, b1, b2, b3, other, wo_ref, full_out, grad_out):
    own = [b0, b1, b2, b3]
    chunk = b0.shape[0]
    for r in range(8):
        at = pl.ds(pl.multiple_of(place_mp(-(r % SIDE), r // SIDE) * chunk, chunk), chunk)
        full_out[at, :] = own[r][...] if r < 4 else other[(r - 4) * chunk : (r - 3) * chunk, :]
    grad_out[...] = nn(wo_ref[...], full_out[...]).astype(BF16)


def fwd_loop_body(heads, *refs):
    q_refs, kv_refs = refs[:SIDE], refs[SIDE : 2 * SIDE]
    o_ref, lse_ref, keys, vals, queries = refs[2 * SIDE :]
    rows = q_refs[0].shape[1]
    width = heads * HEAD_DIM
    for r in range(SIDE):
        cols = slice(r * rows, (r + 1) * rows)
        vals[:, cols] = kv_refs[r][width:, :]
        queries[:, cols] = q_refs[r][...]
        for h in range(heads):
            keys[h, cols, :] = kv_refs[r][head_rows(h), :].T

    def step(r, carry):
        cols = pl.ds(pl.multiple_of(r * rows, rows), rows)
        for h in range(heads):
            at = head_rows(h)
            scores = nn(keys[h], queries[at, cols])
            top = jnp.max(scores, axis=0, keepdims=True)
            weights = jnp.exp(scores - top)
            total = jnp.sum(weights, axis=0, keepdims=True)
            out = nn(vals[at, :], weights.astype(BF16)) / total
            o_ref[at, cols] = out.astype(BF16)
            lse_ref[h : h + 1, cols] = top + jnp.log(total)
        return carry

    lax.fori_loop(0, SIDE, step, 0)


def stats_body(heads, o_ref, lse_ref, *refs):
    g_refs, out_ref = refs[:SIDE], refs[SIDE]
    rows = g_refs[0].shape[1]
    out_ref[...] = jnp.zeros_like(out_ref)
    out_ref[:heads, :] = lse_ref[...]
    for r in range(SIDE):
        cols = slice(r * rows, (r + 1) * rows)
        for h in range(heads):
            at = head_rows(h)
            out_ref[heads + h : heads + h + 1, cols] = jnp.sum(
                o_ref[at, cols].astype(F32) * g_refs[r][at, :].astype(F32), axis=0, keepdims=True
            )


def combine_body(heads, o_ref, *refs):
    peers, outs = refs[:SIDE], refs[SIDE:]
    lse_out, off_out, blocks = outs[0], outs[1], outs[2:]
    rows = o_ref.shape[1] // SIDE
    for r in range(SIDE):
        cols = slice(r * rows, (r + 1) * rows)
        theirs = []
        for s in range(SIDE):
            at = (r - s) % SIDE
            theirs.append(peers[s][:, at * rows : (at + 1) * rows])
        lse = [t[:heads] for t in theirs]
        off = [t[heads : 2 * heads] for t in theirs]
        top = jnp.maximum(jnp.maximum(lse[0], lse[1]), jnp.maximum(lse[2], lse[3]))
        logsum = top + jnp.log(sum(jnp.exp(v - top) for v in lse))
        shares = [jnp.exp(v - logsum) for v in lse]
        lse_out[:heads, cols] = logsum
        off_out[:heads, cols] = sum(w * v for w, v in zip(shares, off))
        for h in range(heads):
            at = head_rows(h)
            blocks[r][at, :] = (o_ref[at, cols].astype(F32) * shares[0][h : h + 1]).astype(BF16)


def bwd_body(first, last, heads, q_block, k_block, *refs):
    q_refs, kv_refs, g_refs = refs[:SIDE], refs[SIDE : 2 * SIDE], refs[2 * SIDE : 3 * SIDE]
    lse_ref, off_ref = refs[3 * SIDE : 3 * SIDE + 2]
    refs = refs[3 * SIDE + 2 :]
    carried = refs[: 2 * SIDE] if first else ()
    refs = refs[len(carried) :]
    dq_refs, dkv_refs = refs[:SIDE], refs[SIDE : 2 * SIDE]
    keys, vals, kt, qt, gt, stat, dq, dk, dv = refs[2 * SIDE :]
    count = last - first
    rows = q_refs[0].shape[1]
    span = SIDE * rows
    mine = slice(first * HEAD_DIM, last * HEAD_DIM)
    for r in range(SIDE):
        cols = slice(r * rows, (r + 1) * rows)
        qt[:, cols] = q_refs[r][mine, :]
        gt[:, cols] = g_refs[r][mine, :]
        kt[:, cols] = kv_refs[r][mine, :]
        for h in range(count):
            keys[h, cols, :] = kv_refs[r][head_rows(first + h), :].T
            vals[h, cols, :] = kv_refs[r][head_rows(heads + first + h), :].T
    for h in range(count):
        stat[h : h + 1, :] = lse_ref[first + h : first + h + 1, :]
        stat[count + h : count + h + 1, :] = off_ref[first + h : first + h + 1, :]
    dk[...] = jnp.zeros_like(dk)
    dv[...] = jnp.zeros_like(dv)
    dq[...] = jnp.zeros_like(dq)

    def q_step(qi, carry):
        q_cols = pl.ds(pl.multiple_of(qi * q_block, q_block), q_block)

        def k_step(ki, carry):
            k_rows = pl.ds(pl.multiple_of(ki * k_block, k_block), k_block)
            for h in range(count):
                at = head_rows(h)
                q = qt[at, q_cols]
                g = gt[at, q_cols]
                scores = nn(keys[h, k_rows, :], q)
                prob = jnp.exp(scores - stat[h : h + 1, q_cols])
                grad_prob = nn(vals[h, k_rows, :], g)
                off = stat[count + h : count + h + 1, q_cols]
                grad_score = (prob * (grad_prob - off)).astype(BF16)
                dq[at, q_cols] += nn(kt[at, k_rows], grad_score)
                dk[at, k_rows] += nt(q, grad_score)
                dv[at, k_rows] += nt(g, prob.astype(BF16))
            return carry

        lax.fori_loop(0, span // k_block, k_step, 0)
        return carry

    lax.fori_loop(0, span // q_block, q_step, 0)
    done = first * HEAD_DIM
    for r in range(SIDE):
        cols = slice(r * rows, (r + 1) * rows)
        dq_refs[r][done:, :] = (dq[:, cols] * HEAD_DIM ** (-0.5)).astype(BF16)
        half = last * HEAD_DIM
        dkv_refs[r][done:half, :] = dk[:, cols].astype(BF16)
        dkv_refs[r][half + done :, :] = dv[:, cols].astype(BF16)
        if first:
            dq_refs[r][:done, :] = carried[r][...]
            dkv_refs[r][:done, :] = carried[SIDE + r][:done, :]
            dkv_refs[r][half : half + done, :] = carried[SIDE + r][done:, :]


def sum_terms(refs):
    return sum(t[...].astype(F32) for t in refs)


def proj_body(*refs):
    terms, wo_ref = refs[:SIDE], refs[SIDE]
    att_out, own_out, other_out = refs[SIDE + 1 :]
    attended = sum_terms(terms).astype(BF16)
    half = own_out.shape[0]
    chunk = half // SIDE

    def step(d, carry):
        at = pl.multiple_of(d * chunk, chunk)
        rows = pl.ds(at, chunk)
        other_out[rows, :] = nn(wo_ref[pl.ds(half + at, chunk), :], attended).astype(BF16)
        own_out[rows, :] = nn(wo_ref[rows, :], attended)
        return carry

    lax.fori_loop(0, SIDE, step, 0)
    att_out[...] = attended


def out_weights_body(att_ref, full_ref, part_out):
    chunk = full_ref.shape[0] // SIDE

    def step(d, carry):
        cols = pl.ds(pl.multiple_of(d * chunk, chunk), chunk)
        part_out[:, cols] = nt(att_ref[...], full_ref[cols, :]).astype(BF16)
        return carry

    lax.fori_loop(0, SIDE, step, 0)


def pair_body(own_ref, got_ref, *outs):
    chunk = outs[0].shape[0]
    for d in range(SIDE):
        at = slice(d * chunk, (d + 1) * chunk)
        outs[d][...] = (own_ref[at, :] + got_ref[at, :].astype(F32)).astype(BF16)


def weights_body(heads, *refs):
    dq, dkv = refs[:SIDE], refs[SIDE : 2 * SIDE]
    normed_ref, out_part_ref, gp_out, part_out = refs[2 * SIDE :]
    width = heads * HEAD_DIM
    grad_q = sum_terms(dq).astype(BF16)
    grad_kv = sum_terms(dkv).astype(BF16)
    for h in range(heads):
        at = h * 3 * HEAD_DIM
        gp_out[at : at + HEAD_DIM, :] = grad_q[head_rows(h)]
        gp_out[at + HEAD_DIM : at + 2 * HEAD_DIM, :] = grad_kv[head_rows(h)]
        gp_out[at + 2 * HEAD_DIM : at + 3 * HEAD_DIM, :] = grad_kv[head_rows(heads + h)]

    def step(h, carry):
        rows = pl.ds(pl.multiple_of(h * 3 * HEAD_DIM, 3 * HEAD_DIM), 3 * HEAD_DIM)
        part_out[rows, :] = nt(gp_out[rows, :], normed_ref[...]).astype(BF16)
        return carry

    lax.fori_loop(0, heads, step, 0)
    part_out[3 * width :, :] = out_part_ref[...]


def split(v):
    high = v.astype(BF16)
    return high, (v - high.astype(F32)).astype(BF16)


def grads_body(heads, width, all_gp, q_ref, kv_ref, wq_ref, own_out, other_out):
    size = 3 * HEAD_DIM
    dots = jnp.zeros((1, q_ref.shape[1]), F32)
    for h in range(heads):
        at = h * size
        gp = all_gp[at : at + size, :].astype(F32)
        q = q_ref[head_rows(h), :].astype(F32) * HEAD_DIM**0.5
        k = kv_ref[head_rows(h), :].astype(F32)
        v = kv_ref[head_rows(heads + h), :].astype(F32)
        for j, held in enumerate((q, k, v)):
            dots = dots + jnp.sum(
                gp[j * HEAD_DIM : (j + 1) * HEAD_DIM] * held, axis=0, keepdims=True
            )
    dots = dots / width
    half = wq_ref.shape[0] // 2
    chunk = half // SIDE

    def step(d, carry):
        at = pl.multiple_of(d * chunk, chunk)
        rows = pl.ds(at, chunk)
        other_out[rows, :] = nn(wq_ref[pl.ds(half + at, chunk), :], all_gp[...]).astype(BF16)
        own_out[rows, :] = nn(wq_ref[rows, :], all_gp[...])
        return carry

    lax.fori_loop(0, SIDE, step, 0)
    high, low = split(dots)
    other_out[half:, :] = jnp.concatenate(
        [high, low, jnp.zeros((PAD - 2, dots.shape[1]), BF16)], axis=0
    )
    own_out[half:, :] = jnp.broadcast_to(dots, (8, dots.shape[1]))


def grads_pair_body(own_ref, got_ref, *outs):
    chunk = outs[0].shape[0] - PAD
    half = SIDE * chunk
    got = got_ref[half:, :].astype(F32)
    dots = own_ref[half : half + 1, :] + got[0:1] + got[1:2]
    high, low = split(dots)
    tail = jnp.concatenate([high, low, jnp.zeros((PAD - 2, dots.shape[1]), BF16)], axis=0)
    for d in range(SIDE):
        at = slice(d * chunk, (d + 1) * chunk)
        outs[d][:chunk, :] = (own_ref[at, :] + got_ref[at, :].astype(F32)).astype(BF16)
        outs[d][chunk:, :] = tail


def reduce_body(in_ref, small_ref, first_out, second_out):
    members, rows, width = in_ref.shape
    half = rows // 2
    lanes = 128

    def step(i, carry):
        cols = pl.ds(pl.multiple_of(i * lanes, lanes), lanes)
        total = sum(in_ref[m, :, cols].astype(F32) for m in range(members)).astype(BF16)
        first_out[:, cols] = total[:half]
        second_out[:, cols] = total[half:]
        return carry

    lax.fori_loop(0, width // lanes, step, 0)
    first_out[:, width:] = small_ref[:half, :]
    second_out[:, width:] = small_ref[half:, :]


def finish_body(heads, *refs):
    firsts, seconds = refs[:SIDE], refs[SIDE : 2 * SIDE]
    qkv_out, proj_out, small_out = refs[2 * SIDE :]
    half = firsts[0].shape[1]
    each = 2 * half
    width = qkv_out.shape[2]
    step = 8
    qkv_rows = 3 * heads * HEAD_DIM
    qkv_members = qkv_rows // each
    small_out[...] = jnp.zeros_like(small_out)

    def place(ref, e, m, start):
        @pl.when(m < qkv_members)
        def _():
            for i in range(0, half, step):
                row = m * each + (start + i)
                block = lax.div(row, HEAD_DIM)
                at = lax.div(block, 3) * HEAD_DIM + lax.rem(row, HEAD_DIM)
                at = pl.ds(pl.multiple_of(at, step), step)
                qkv_out[lax.rem(block, 3), at, :] = ref[e, i : i + step, :width].astype(F32)

        @pl.when(m >= qkv_members)
        def _():
            for i in range(0, half, step):
                at = pl.ds(pl.multiple_of(m * each + (start + i) - qkv_rows, step), step)
                proj_out[at, :] = ref[e, i : i + step, :width].astype(F32)

    for d in range(SIDE):

        def spread(e, carry):
            place(firsts[d], e, place_tm(d, e), 0)
            place(seconds[d], e, place_tm(e, d), half)
            small_out[:half, :] += firsts[d][e, :, width:].astype(F32)
            small_out[half:, :] += seconds[d][e, :, width:].astype(F32)
            return carry

        lax.fori_loop(0, SIDE, spread, 0)


def tie(value, *others):
    return lax.optimization_barrier((value, *others))[0]


def shards(frames, norm_gain, w_qkv, w_out, conv_kernel, grad_out):
    own_width, rows = frames.shape
    head_cols, width = w_qkv.shape[1:]
    heads = head_cols // HEAD_DIM
    members = lax.axis_size("tm")
    taps = conv_kernel.shape[0]
    span = SIDE * rows

    def with_swap(blocks):
        return blocks + [swap_core(jnp.concatenate(blocks, axis=0))]

    up_left, up_right = halos(grad_out)
    in_blocks = ring(shift_y, [frames] * SIDE, 1)
    back_sum, back_cast = call(
        back_kernel,
        [((own_width, rows), F32), ((own_width, rows), BF16)],
        [up_left, grad_out, up_right, conv_kernel], None,
        [
            pltpu.VMEM((rows + 2 * PAD, own_width), F32),
            pltpu.VMEM((rows, own_width), F32),
            pltpu.VMEM((STEP + 2 * PAD, own_width), F32),
        ],
        flops=8 * own_width * rows * taps,
    )
    in_blocks = with_swap(in_blocks)
    back_blocks = ring(shift_y, [back_cast] * SIDE, 1)
    normed, inverse, queries, keys_values = call(
        norm_body,
        [((width, rows), BF16), ((1, rows), F32), ((head_cols, rows), BF16), ((2 * head_cols, rows), BF16)],
        [*in_blocks, norm_gain[None], w_qkv], None, [pltpu.VMEM((width, 8), F32)],
        flops=2 * 3 * head_cols * width * rows,
    )
    group_kv = ring(shift_z, [keys_values] * SIDE, 1)
    group_q = ring(shift_x, [queries] * SIDE, 1)

    back_blocks = list(lax.optimization_barrier((*back_blocks, keys_values)))[:SIDE]
    back_blocks = with_swap(back_blocks)
    back_full, grad_attn = call(
        back_arrange_body,
        [((width, rows), BF16), ((head_cols, rows), BF16)],
        [*back_blocks, w_out],
        flops=2 * head_cols * width * rows,
    )
    group_g = ring(shift_x, [grad_attn] * SIDE, 1)

    part_out, part_lse = call(
        functools.partial(fwd_loop_body, heads),
        [((head_cols, span), BF16), ((heads, span), F32)],
        [tie(group_q[0], grad_attn), *group_q[1:], *group_kv], None,
        [
            pltpu.VMEM((heads, span, HEAD_DIM), BF16),
            pltpu.VMEM((head_cols, span), BF16),
            pltpu.VMEM((head_cols, span), BF16),
        ],
        flops=16 * head_cols * span * span, exps=heads * span * span,
    )
    (stats,) = call(
        functools.partial(stats_body, heads),
        [((8, span), F32)], [part_out, part_lse, *group_g],
    )
    peers = ring(shift_x, [stats] * SIDE, 1)
    wq_rel, wo_rel = call(
        prep_body,
        [((width, 3 * head_cols), BF16), ((width, head_cols), BF16)],
        [stats[:, :128], w_qkv, w_out], None,
        [
            pltpu.VMEM((3 * head_cols, width), BF16),
            pltpu.VMEM((width, 3 * head_cols), BF16),
            pltpu.VMEM((width, head_cols), BF16),
        ],
    )
    logsum, offset, *out_blocks = call(
        functools.partial(combine_body, heads),
        [((8, span), F32), ((8, span), F32)] + [((head_cols, rows), BF16)] * SIDE,
        [tie(part_out, wo_rel), *peers],
    )
    out_terms = ring(shift_x, out_blocks, -1)

    q_block, k_block = min(256, span), min(2048, span)

    def head_grads(first, last, logsum, carried):
        count = last - first
        size = count * HEAD_DIM
        return call(
            functools.partial(bwd_body, first, last, heads, q_block, k_block),
            [((last * HEAD_DIM, rows), BF16)] * SIDE + [((2 * last * HEAD_DIM, rows), BF16)] * SIDE,
            [*group_q, *group_kv, *group_g, logsum, offset, *carried], None,
            [pltpu.VMEM((count, span, HEAD_DIM), BF16)] * 2
            + [pltpu.VMEM((size, span), BF16)] * 3
            + [pltpu.VMEM((8, span), F32)]
            + [pltpu.VMEM((size, span), F32)] * 3,
            flops=40 * size * span * span, exps=count * span * span,
        )

    early = head_grads(0, 1, logsum, ())
    half = SIDE * own_width
    attended, proj_own, proj_other = call(
        proj_body,
        [((head_cols, rows), BF16), ((half, rows), F32), ((half, rows), BF16)],
        [tie(out_terms[0], early[0]), *out_terms[1:], wo_rel],
        flops=2 * head_cols * width * rows,
    )
    proj_got = swap_core(proj_other)
    proj_blocks = call(pair_body, [((own_width, rows), BF16)] * SIDE, [proj_own, proj_got])
    proj_terms = ring(shift_y, proj_blocks, 1)

    grads = head_grads(1, heads, tie(logsum, *proj_blocks), early)
    dq, dkv = grads[:SIDE], grads[SIDE:]
    dkv_terms = ring(shift_z, dkv, -1)
    dq_terms = ring(shift_x, dq, -1)

    mixed = sum(t.astype(F32) for t in [tie(proj_terms[0], dq[0])] + proj_terms[1:])
    residual = (frames.astype(F32) + mixed).astype(BF16)
    res_left, res_right = halos(residual)
    (out_part,) = call(
        out_weights_body, [((head_cols, width), BF16)],
        [tie(attended, dq[0]), back_full], flops=2 * head_cols * width * rows,
    )
    all_gp, part = call(
        functools.partial(weights_body, heads),
        [((3 * head_cols, rows), BF16), ((4 * head_cols, width), BF16)],
        [*dq_terms, *dkv_terms, normed, tie(out_part, res_left, res_right)],
        flops=2 * 3 * head_cols * width * rows,
    )
    each = part.shape[0] // members
    got = lax.all_to_all(part.reshape(members, each, width), "tm", 0, 0, tiled=True)

    gn_own, gn_other = call(
        functools.partial(grads_body, heads, width),
        [((half + 8, rows), F32), ((half + PAD, rows), BF16)],
        [tie(all_gp, part), queries, keys_values, wq_rel],
        flops=2 * 3 * head_cols * width * rows,
    )
    gn_got = swap_core(gn_other)
    gn_blocks = call(grads_pair_body, [((own_width + PAD, rows), BF16)] * SIDE, [gn_own, gn_got])
    gn_terms = ring(shift_y, gn_blocks, 1)
    block_out, kernel_part = call(
        conv_body,
        [((own_width, rows), BF16), ((taps, own_width), F32)],
        [tie(res_left, *gn_blocks), residual, res_right, grad_out, conv_kernel], None,
        [
            pltpu.VMEM((rows + 2 * PAD, own_width), F32),
            pltpu.VMEM((rows, own_width), F32),
            pltpu.VMEM((taps, 8, own_width), F32),
            pltpu.VMEM((STEP + 2 * PAD, own_width), F32),
        ],
        flops=16 * own_width * rows * taps,
    )

    summed = sum(t.astype(F32) for t in [tie(gn_terms[0], kernel_part)] + gn_terms[1:])
    grad_own = summed[:own_width]
    dots = summed[own_width : own_width + 1] + summed[own_width + 1 : own_width + 2]
    column_start = lax.axis_index("mp") * own_width
    gain_own = lax.dynamic_slice_in_dim(norm_gain, column_start, own_width, 0)[:, None]
    normed_own = frames.astype(F32) * inverse
    grad_frames = (
        back_sum + inverse * (grad_own * gain_own) - normed_own * inverse * dots
    ).astype(BF16)
    gain_part = jnp.sum(grad_own * normed_own, axis=1)
    small = jnp.concatenate([kernel_part.astype(BF16), gain_part.astype(BF16)[None]], axis=0)
    small_cols = small.size // each
    first, second = call(
        reduce_body, [((each // 2, width + small_cols), BF16)] * 2,
        [got, small.reshape(each, small_cols)],
    )
    first_row = jnp.stack(ring(shift_x, [first] * SIDE, 1))
    second_row = jnp.stack(ring(shift_z, [second] * SIDE, 1))
    first_all = ring(shift_z, [first_row] * SIDE, 1)
    second_all = ring(shift_x, [second_row] * SIDE, 1)
    qkv_grads, out_grads, small_sum = call(
        functools.partial(finish_body, heads),
        [((3, head_cols, width), F32), ((head_cols, width), F32), ((each, small_cols), F32)],
        [*first_all, *second_all],
    )
    small_sum = small_sum.reshape(taps + 1, own_width)
    return block_out, grad_frames, small_sum[taps], qkv_grads, out_grads, small_sum[:taps]


def solution(mesh):
    return jax.shard_map(
        shards,
        mesh=mesh,
        in_specs=(
            P("mp", "tm"),
            P(),
            P(None, "mp", None),
            P("mp", None),
            P(None, "mp"),
            P("mp", "tm"),
        ),
        out_specs=(
            P("mp", "tm"),
            P("mp", "tm"),
            P("mp"),
            P(None, "mp", None),
            P("mp", None),
            P(None, "mp"),
        ),
        check_vma=False,
    )
```

```python
import functools

import jax
import jax.numpy as jnp
from jax import lax
from jax.experimental import pallas as pl
from jax.experimental.pallas import tpu as pltpu
from jax.sharding import PartitionSpec as P


HEAD_DIM = 64
SIDE = 4
PAD = 16
F32 = jnp.float32
BF16 = jnp.bfloat16


def nn(a, b):
    return jnp.dot(a, b, preferred_element_type=F32)


def nt(a, b):
    return lax.dot_general(a, b, (((1,), (1,)), ((), ())), preferred_element_type=F32)


VM = pl.BlockSpec(memory_space=pltpu.VMEM)


STEP = 64


def fill(pad_ref, left_ref, own_ref, right_ref):
    count = own_ref.shape[1]
    slab = left_ref.shape[1]
    pad_ref[PAD : PAD + count, :] = own_ref[...].astype(F32).T
    pad_ref[:PAD, :] = left_ref[...].astype(F32).T[slab - PAD :, :]
    pad_ref[PAD + count :, :] = right_ref[...].astype(F32).T[:PAD, :]


def back_kernel(left_ref, own_ref, right_ref, taps_ref, sum_ref, cast_ref, pad_ref, acc_ref, near):
    count = own_ref.shape[1]
    fill(pad_ref, left_ref, own_ref, right_ref)
    taps = taps_ref.shape[0]
    half = taps // 2

    def step(i, carry):
        base = pl.multiple_of(i * STEP, STEP)
        near[...] = pad_ref[pl.ds(base, STEP + 2 * PAD), :]
        acc = near[PAD : PAD + STEP, :]
        for j in range(taps):
            start = PAD + half - j
            acc = acc + taps_ref[j : j + 1, :] * near[start : start + STEP, :]
        acc_ref[pl.ds(base, STEP), :] = acc
        return carry

    lax.fori_loop(0, count // STEP, step, 0)
    acc = acc_ref[...].T
    sum_ref[...] = acc
    cast_ref[...] = acc.astype(BF16)


def conv_body(left_ref, own_ref, right_ref, up_ref, taps_ref, out_ref, grad_ref, pad_ref, upt_ref, sums, near):
    count = own_ref.shape[1]
    fill(pad_ref, left_ref, own_ref, right_ref)
    upt_ref[...] = up_ref[...].astype(F32).T
    taps = taps_ref.shape[0]
    half = taps // 2
    sums[...] = jnp.zeros_like(sums)

    def step(i, carry):
        base = pl.multiple_of(i * STEP, STEP)
        near[...] = pad_ref[pl.ds(base, STEP + 2 * PAD), :]
        acc = near[PAD : PAD + STEP, :]
        up = upt_ref[pl.ds(base, STEP), :]
        for j in range(taps):
            start = PAD + j - half
            part = near[start : start + STEP, :]
            acc = acc + taps_ref[j : j + 1, :] * part
            prod = up * part
            sums[j] += sum(prod[8 * s : 8 * s + 8] for s in range(STEP // 8))
        upt_ref[pl.ds(base, STEP), :] = acc
        return carry

    lax.fori_loop(0, count // STEP, step, 0)
    for j in range(taps):
        grad_ref[j : j + 1, :] = jnp.sum(sums[j], axis=0, keepdims=True)
    out_ref[...] = upt_ref[...].T.astype(BF16)


def shift_x(a, by):
    pairs = [
        (z * SIDE + x, z * SIDE + (x + by) % SIDE) for z in range(SIDE) for x in range(SIDE)
    ]
    return lax.ppermute(a, "tm", pairs)


def shift_z(a, by):
    pairs = [
        (z * SIDE + x, ((z + by) % SIDE) * SIDE + x) for z in range(SIDE) for x in range(SIDE)
    ]
    return lax.ppermute(a, "tm", pairs)


def halos(a, slab=128):
    count = lax.axis_size("tm")
    ends = count - 1
    left = lax.ppermute(a[:, a.shape[1] - slab :], "tm", [(i, i + 1) for i in range(ends)])
    right = lax.ppermute(a[:, :slab], "tm", [(i + 1, i) for i in range(ends)])
    return left, right


def place_mp(step, core_step):
    index = lax.axis_index("mp")
    y, core = lax.div(index, 2), lax.rem(index, 2)
    core = 1 - core if core_step else core
    return lax.rem(y + step + SIDE, SIDE) * 2 + core


def place_tm(dz, dx):
    index = lax.axis_index("tm")
    z, x = lax.div(index, SIDE), lax.rem(index, SIDE)
    return lax.rem(z - dz + SIDE, SIDE) * SIDE + lax.rem(x - dx + SIDE, SIDE)


def shift_y(a, by):
    count = lax.axis_size("mp") // 2
    pairs = [(y * 2 + c, ((y + by) % count) * 2 + c) for y in range(count) for c in range(2)]
    return lax.ppermute(a, "mp", pairs)


def swap_core(a):
    count = lax.axis_size("mp")
    return lax.ppermute(a, "mp", [(i, i ^ 1) for i in range(count)])


def call(body, outs, args, specs=None, scratch=(), flops=0, exps=0, limit=20):
    out_shape = tuple(jax.ShapeDtypeStruct(s, t) for s, t in outs)
    moved = sum(a.size * a.dtype.itemsize for a in args)
    moved += sum(o.size * o.dtype.itemsize for o in out_shape)
    return pl.pallas_call(
        body,
        out_shape=out_shape,
        in_specs=specs or [VM] * len(args),
        out_specs=[VM] * len(outs),
        scratch_shapes=list(scratch),
        compiler_params=pltpu.CompilerParams(vmem_limit_bytes=limit * 2**20),
        cost_estimate=pl.CostEstimate(flops=flops, bytes_accessed=moved, transcendentals=exps),
    )(*args)


def ring(shift, blocks, sign):
    return [blocks[0]] + [shift(blocks[r], sign * r) for r in range(1, SIDE)]


def head_rows(h):
    return slice(h * HEAD_DIM, (h + 1) * HEAD_DIM)


def prep_body(after_ref, w_ref, wo_ref, wq_out, wo_out, mixed, turned, turned_out):
    head_cols, width = wo_ref.shape
    heads = head_cols // HEAD_DIM
    for h in range(heads):
        for j in range(3):
            at = (h * 3 + j) * HEAD_DIM
            mixed[at : at + HEAD_DIM, :] = w_ref[j, head_rows(h), :]
    lanes = 128

    def turn(i, carry):
        cols = pl.ds(pl.multiple_of(i * lanes, lanes), lanes)
        turned[cols, :] = mixed[:, cols].T
        turned_out[cols, :] = wo_ref[:, cols].T
        return carry

    lax.fori_loop(0, width // lanes, turn, 0)
    chunk = width // 8
    for r in range(8):
        at = place_mp(r % SIDE, r // SIDE)
        rows = pl.ds(pl.multiple_of(at * chunk, chunk), chunk)
        wq_out[r * chunk : (r + 1) * chunk, :] = turned[rows, :]
        wo_out[r * chunk : (r + 1) * chunk, :] = turned_out[rows, :]


def norm_body(b0, b1, b2, b3, other, gain_ref, w_ref, normed_out, inv_out, q_out, kv_out, gain):
    own = [b0, b1, b2, b3]
    chunk, rows = b0.shape
    width = normed_out.shape[0]

    def block(r):
        part = own[r][...] if r < 4 else other[(r - 4) * chunk : (r - 3) * chunk, :]
        return part.astype(F32)

    gain[...] = jnp.broadcast_to(gain_ref[...], (8, width)).T
    total = jnp.zeros((1, rows), F32)
    for r in range(8):
        x = block(r)
        total = total + jnp.sum(x * x, axis=0, keepdims=True)
    inverse = lax.rsqrt(total / width + 1e-06)
    inv_out[...] = inverse
    for r in range(8):
        at = pl.ds(pl.multiple_of(place_mp(-(r % SIDE), r // SIDE) * chunk, chunk), chunk)
        normed_out[at, :] = (block(r) * inverse * gain[at, :1]).astype(BF16)
    normed = normed_out[...]
    q_out[...] = nn(w_ref[0], normed).astype(BF16) * jnp.asarray(HEAD_DIM ** (-0.5), BF16)
    head_cols = q_out.shape[0]

    def step(j, carry):
        at = pl.ds(pl.multiple_of((j - 1) * head_cols, head_cols), head_cols)
        kv_out[at, :] = nn(w_ref[j], normed_out[...]).astype(BF16)
        return carry

    lax.fori_loop(1, 3, step, 0)


def back_arrange_body(b0, b1, b2, b3, other, wo_ref, full_out, grad_out):
    own = [b0, b1, b2, b3]
    chunk = b0.shape[0]
    for r in range(8):
        at = pl.ds(pl.multiple_of(place_mp(-(r % SIDE), r // SIDE) * chunk, chunk), chunk)
        full_out[at, :] = own[r][...] if r < 4 else other[(r - 4) * chunk : (r - 3) * chunk, :]
    grad_out[...] = nn(wo_ref[...], full_out[...]).astype(BF16)


def fwd_loop_body(heads, *refs):
    q_refs, kv_refs = refs[:SIDE], refs[SIDE : 2 * SIDE]
    o_ref, lse_ref, keys, vals, queries = refs[2 * SIDE :]
    rows = q_refs[0].shape[1]
    width = heads * HEAD_DIM
    for r in range(SIDE):
        cols = slice(r * rows, (r + 1) * rows)
        vals[:, cols] = kv_refs[r][width:, :]
        queries[:, cols] = q_refs[r][...]
        for h in range(heads):
            keys[h, cols, :] = kv_refs[r][head_rows(h), :].T

    def step(r, carry):
        cols = pl.ds(pl.multiple_of(r * rows, rows), rows)
        for h in range(heads):
            at = head_rows(h)
            scores = nn(keys[h], queries[at, cols])
            top = jnp.max(scores, axis=0, keepdims=True)
            weights = jnp.exp(scores - top)
            total = jnp.sum(weights, axis=0, keepdims=True)
            out = nn(vals[at, :], weights.astype(BF16)) / total
            o_ref[at, cols] = out.astype(BF16)
            lse_ref[h : h + 1, cols] = top + jnp.log(total)
        return carry

    lax.fori_loop(0, SIDE, step, 0)


def stats_body(heads, o_ref, lse_ref, *refs):
    g_refs, out_ref = refs[:SIDE], refs[SIDE]
    rows = g_refs[0].shape[1]
    out_ref[...] = jnp.zeros_like(out_ref)
    out_ref[:heads, :] = lse_ref[...]
    for r in range(SIDE):
        cols = slice(r * rows, (r + 1) * rows)
        for h in range(heads):
            at = head_rows(h)
            out_ref[heads + h : heads + h + 1, cols] = jnp.sum(
                o_ref[at, cols].astype(F32) * g_refs[r][at, :].astype(F32), axis=0, keepdims=True
            )


def combine_body(heads, o_ref, *refs):
    peers, outs = refs[:SIDE], refs[SIDE:]
    lse_out, off_out, blocks = outs[0], outs[1], outs[2:]
    rows = o_ref.shape[1] // SIDE
    for r in range(SIDE):
        cols = slice(r * rows, (r + 1) * rows)
        theirs = []
        for s in range(SIDE):
            at = (r - s) % SIDE
            theirs.append(peers[s][:, at * rows : (at + 1) * rows])
        lse = [t[:heads] for t in theirs]
        off = [t[heads : 2 * heads] for t in theirs]
        top = jnp.maximum(jnp.maximum(lse[0], lse[1]), jnp.maximum(lse[2], lse[3]))
        logsum = top + jnp.log(sum(jnp.exp(v - top) for v in lse))
        shares = [jnp.exp(v - logsum) for v in lse]
        lse_out[:heads, cols] = logsum
        off_out[:heads, cols] = sum(w * v for w, v in zip(shares, off))
        for h in range(heads):
            at = head_rows(h)
            blocks[r][at, :] = (o_ref[at, cols].astype(F32) * shares[0][h : h + 1]).astype(BF16)


def bwd_body(first, last, heads, q_block, k_block, *refs):
    q_refs, kv_refs, g_refs = refs[:SIDE], refs[SIDE : 2 * SIDE], refs[2 * SIDE : 3 * SIDE]
    lse_ref, off_ref = refs[3 * SIDE : 3 * SIDE + 2]
    refs = refs[3 * SIDE + 2 :]
    carried = refs[: 2 * SIDE] if first else ()
    refs = refs[len(carried) :]
    dq_refs, dkv_refs = refs[:SIDE], refs[SIDE : 2 * SIDE]
    keys, vals, kt, qt, gt, stat, dq, dk, dv = refs[2 * SIDE :]
    count = last - first
    rows = q_refs[0].shape[1]
    span = SIDE * rows
    mine = slice(first * HEAD_DIM, last * HEAD_DIM)
    for r in range(SIDE):
        cols = slice(r * rows, (r + 1) * rows)
        qt[:, cols] = q_refs[r][mine, :]
        gt[:, cols] = g_refs[r][mine, :]
        kt[:, cols] = kv_refs[r][mine, :]
        for h in range(count):
            keys[h, cols, :] = kv_refs[r][head_rows(first + h), :].T
            vals[h, cols, :] = kv_refs[r][head_rows(heads + first + h), :].T
    for h in range(count):
        stat[h : h + 1, :] = lse_ref[first + h : first + h + 1, :]
        stat[count + h : count + h + 1, :] = off_ref[first + h : first + h + 1, :]
    dk[...] = jnp.zeros_like(dk)
    dv[...] = jnp.zeros_like(dv)
    dq[...] = jnp.zeros_like(dq)

    def q_step(qi, carry):
        q_cols = pl.ds(pl.multiple_of(qi * q_block, q_block), q_block)

        def k_step(ki, carry):
            k_rows = pl.ds(pl.multiple_of(ki * k_block, k_block), k_block)
            for h in range(count):
                at = head_rows(h)
                q = qt[at, q_cols]
                g = gt[at, q_cols]
                scores = nn(keys[h, k_rows, :], q)
                prob = jnp.exp(scores - stat[h : h + 1, q_cols])
                grad_prob = nn(vals[h, k_rows, :], g)
                off = stat[count + h : count + h + 1, q_cols]
                grad_score = (prob * (grad_prob - off)).astype(BF16)
                dq[at, q_cols] += nn(kt[at, k_rows], grad_score)
                dk[at, k_rows] += nt(q, grad_score)
                dv[at, k_rows] += nt(g, prob.astype(BF16))
            return carry

        lax.fori_loop(0, span // k_block, k_step, 0)
        return carry

    lax.fori_loop(0, span // q_block, q_step, 0)
    done = first * HEAD_DIM
    for r in range(SIDE):
        cols = slice(r * rows, (r + 1) * rows)
        dq_refs[r][done:, :] = (dq[:, cols] * HEAD_DIM ** (-0.5)).astype(BF16)
        half = last * HEAD_DIM
        dkv_refs[r][done:half, :] = dk[:, cols].astype(BF16)
        dkv_refs[r][half + done :, :] = dv[:, cols].astype(BF16)
        if first:
            dq_refs[r][:done, :] = carried[r][...]
            dkv_refs[r][:done, :] = carried[SIDE + r][:done, :]
            dkv_refs[r][half : half + done, :] = carried[SIDE + r][done:, :]


def sum_terms(refs):
    return sum(t[...].astype(F32) for t in refs)


def proj_body(*refs):
    terms, wo_ref = refs[:SIDE], refs[SIDE]
    att_out, own_out, other_out = refs[SIDE + 1 :]
    attended = sum_terms(terms).astype(BF16)
    half = own_out.shape[0]
    chunk = half // SIDE

    def step(d, carry):
        at = pl.multiple_of(d * chunk, chunk)
        rows = pl.ds(at, chunk)
        other_out[rows, :] = nn(wo_ref[pl.ds(half + at, chunk), :], attended).astype(BF16)
        own_out[rows, :] = nn(wo_ref[rows, :], attended)
        return carry

    lax.fori_loop(0, SIDE, step, 0)
    att_out[...] = attended


def out_weights_body(att_ref, full_ref, part_out):
    chunk = full_ref.shape[0] // SIDE

    def step(d, carry):
        cols = pl.ds(pl.multiple_of(d * chunk, chunk), chunk)
        part_out[:, cols] = nt(att_ref[...], full_ref[cols, :]).astype(BF16)
        return carry

    lax.fori_loop(0, SIDE, step, 0)


def pair_body(own_ref, got_ref, *outs):
    chunk = outs[0].shape[0]
    for d in range(SIDE):
        at = slice(d * chunk, (d + 1) * chunk)
        outs[d][...] = (own_ref[at, :] + got_ref[at, :].astype(F32)).astype(BF16)


def weights_body(heads, *refs):
    dq, dkv = refs[:SIDE], refs[SIDE : 2 * SIDE]
    normed_ref, out_part_ref, gp_out, part_out = refs[2 * SIDE :]
    width = heads * HEAD_DIM
    grad_q = sum_terms(dq).astype(BF16)
    grad_kv = sum_terms(dkv).astype(BF16)
    for h in range(heads):
        at = h * 3 * HEAD_DIM
        gp_out[at : at + HEAD_DIM, :] = grad_q[head_rows(h)]
        gp_out[at + HEAD_DIM : at + 2 * HEAD_DIM, :] = grad_kv[head_rows(h)]
        gp_out[at + 2 * HEAD_DIM : at + 3 * HEAD_DIM, :] = grad_kv[head_rows(heads + h)]

    def step(h, carry):
        rows = pl.ds(pl.multiple_of(h * 3 * HEAD_DIM, 3 * HEAD_DIM), 3 * HEAD_DIM)
        part_out[rows, :] = nt(gp_out[rows, :], normed_ref[...]).astype(BF16)
        return carry

    lax.fori_loop(0, heads, step, 0)
    part_out[3 * width :, :] = out_part_ref[...]


def split(v):
    high = v.astype(BF16)
    return high, (v - high.astype(F32)).astype(BF16)


def grads_body(heads, width, all_gp, q_ref, kv_ref, wq_ref, own_out, other_out):
    size = 3 * HEAD_DIM
    dots = jnp.zeros((1, q_ref.shape[1]), F32)
    for h in range(heads):
        at = h * size
        gp = all_gp[at : at + size, :].astype(F32)
        q = q_ref[head_rows(h), :].astype(F32) * HEAD_DIM**0.5
        k = kv_ref[head_rows(h), :].astype(F32)
        v = kv_ref[head_rows(heads + h), :].astype(F32)
        for j, held in enumerate((q, k, v)):
            dots = dots + jnp.sum(
                gp[j * HEAD_DIM : (j + 1) * HEAD_DIM] * held, axis=0, keepdims=True
            )
    dots = dots / width
    half = wq_ref.shape[0] // 2
    chunk = half // SIDE

    def step(d, carry):
        at = pl.multiple_of(d * chunk, chunk)
        rows = pl.ds(at, chunk)
        other_out[rows, :] = nn(wq_ref[pl.ds(half + at, chunk), :], all_gp[...]).astype(BF16)
        own_out[rows, :] = nn(wq_ref[rows, :], all_gp[...])
        return carry

    lax.fori_loop(0, SIDE, step, 0)
    high, low = split(dots)
    other_out[half:, :] = jnp.concatenate(
        [high, low, jnp.zeros((PAD - 2, dots.shape[1]), BF16)], axis=0
    )
    own_out[half:, :] = jnp.broadcast_to(dots, (8, dots.shape[1]))


def grads_pair_body(own_ref, got_ref, *outs):
    chunk = outs[0].shape[0] - PAD
    half = SIDE * chunk
    got = got_ref[half:, :].astype(F32)
    dots = own_ref[half : half + 1, :] + got[0:1] + got[1:2]
    high, low = split(dots)
    tail = jnp.concatenate([high, low, jnp.zeros((PAD - 2, dots.shape[1]), BF16)], axis=0)
    for d in range(SIDE):
        at = slice(d * chunk, (d + 1) * chunk)
        outs[d][:chunk, :] = (own_ref[at, :] + got_ref[at, :].astype(F32)).astype(BF16)
        outs[d][chunk:, :] = tail


def reduce_body(in_ref, small_ref, first_out, second_out):
    members, rows, width = in_ref.shape
    half = rows // 2
    lanes = 128

    def step(i, carry):
        cols = pl.ds(pl.multiple_of(i * lanes, lanes), lanes)
        total = sum(in_ref[m, :, cols].astype(F32) for m in range(members)).astype(BF16)
        first_out[:, cols] = total[:half]
        second_out[:, cols] = total[half:]
        return carry

    lax.fori_loop(0, width // lanes, step, 0)
    first_out[:, width:] = small_ref[:half, :]
    second_out[:, width:] = small_ref[half:, :]


def finish_body(heads, *refs):
    firsts, seconds = refs[:SIDE], refs[SIDE : 2 * SIDE]
    qkv_out, proj_out, small_out = refs[2 * SIDE :]
    half = firsts[0].shape[1]
    each = 2 * half
    width = qkv_out.shape[2]
    step = 8
    qkv_rows = 3 * heads * HEAD_DIM
    qkv_members = qkv_rows // each
    small_out[...] = jnp.zeros_like(small_out)

    def place(ref, e, m, start):
        @pl.when(m < qkv_members)
        def _():
            for i in range(0, half, step):
                row = m * each + (start + i)
                block = lax.div(row, HEAD_DIM)
                at = lax.div(block, 3) * HEAD_DIM + lax.rem(row, HEAD_DIM)
                at = pl.ds(pl.multiple_of(at, step), step)
                qkv_out[lax.rem(block, 3), at, :] = ref[e, i : i + step, :width].astype(F32)

        @pl.when(m >= qkv_members)
        def _():
            for i in range(0, half, step):
                at = pl.ds(pl.multiple_of(m * each + (start + i) - qkv_rows, step), step)
                proj_out[at, :] = ref[e, i : i + step, :width].astype(F32)

    for d in range(SIDE):

        def spread(e, carry):
            place(firsts[d], e, place_tm(d, e), 0)
            place(seconds[d], e, place_tm(e, d), half)
            small_out[:half, :] += firsts[d][e, :, width:].astype(F32)
            small_out[half:, :] += seconds[d][e, :, width:].astype(F32)
            return carry

        lax.fori_loop(0, SIDE, spread, 0)


def tie(value, *others):
    return lax.optimization_barrier((value, *others))[0]


def shards(frames, norm_gain, w_qkv, w_out, conv_kernel, grad_out):
    own_width, rows = frames.shape
    head_cols, width = w_qkv.shape[1:]
    heads = head_cols // HEAD_DIM
    members = lax.axis_size("tm")
    taps = conv_kernel.shape[0]
    span = SIDE * rows

    def with_swap(blocks):
        return blocks + [swap_core(jnp.concatenate(blocks, axis=0))]

    up_left, up_right = halos(grad_out)
    in_blocks = ring(shift_y, [frames] * SIDE, 1)
    back_sum, back_cast = call(
        back_kernel,
        [((own_width, rows), F32), ((own_width, rows), BF16)],
        [up_left, grad_out, up_right, conv_kernel], None,
        [
            pltpu.VMEM((rows + 2 * PAD, own_width), F32),
            pltpu.VMEM((rows, own_width), F32),
            pltpu.VMEM((STEP + 2 * PAD, own_width), F32),
        ],
        flops=8 * own_width * rows * taps,
    )
    in_blocks = list(lax.optimization_barrier((*in_blocks, back_cast)))
    back_cast = in_blocks.pop()
    in_blocks = with_swap(in_blocks)
    back_blocks = ring(shift_y, [back_cast] * SIDE, 1)
    normed, inverse, queries, keys_values = call(
        norm_body,
        [((width, rows), BF16), ((1, rows), F32), ((head_cols, rows), BF16), ((2 * head_cols, rows), BF16)],
        [*in_blocks, norm_gain[None], w_qkv], None, [pltpu.VMEM((width, 8), F32)],
        flops=2 * 3 * head_cols * width * rows,
    )
    group_kv = ring(shift_z, [keys_values] * SIDE, 1)
    group_q = ring(shift_x, [queries] * SIDE, 1)

    back_blocks = list(lax.optimization_barrier((*back_blocks, keys_values)))[:SIDE]
    back_blocks = with_swap(back_blocks)
    back_full, grad_attn = call(
        back_arrange_body,
        [((width, rows), BF16), ((head_cols, rows), BF16)],
        [*back_blocks, w_out],
        flops=2 * head_cols * width * rows,
    )
    group_g = ring(shift_x, [grad_attn] * SIDE, 1)

    part_out, part_lse = call(
        functools.partial(fwd_loop_body, heads),
        [((head_cols, span), BF16), ((heads, span), F32)],
        [tie(group_q[0], grad_attn), *group_q[1:], *group_kv], None,
        [
            pltpu.VMEM((heads, span, HEAD_DIM), BF16),
            pltpu.VMEM((head_cols, span), BF16),
            pltpu.VMEM((head_cols, span), BF16),
        ],
        flops=16 * head_cols * span * span, exps=heads * span * span, limit=40,
    )
    (stats,) = call(
        functools.partial(stats_body, heads),
        [((8, span), F32)], [part_out, part_lse, *group_g],
    )
    peers = ring(shift_x, [stats] * SIDE, 1)
    wq_rel, wo_rel = call(
        prep_body,
        [((width, 3 * head_cols), BF16), ((width, head_cols), BF16)],
        [stats[:, :128], w_qkv, w_out], None,
        [
            pltpu.VMEM((3 * head_cols, width), BF16),
            pltpu.VMEM((width, 3 * head_cols), BF16),
            pltpu.VMEM((width, head_cols), BF16),
        ],
    )
    logsum, offset, *out_blocks = call(
        functools.partial(combine_body, heads),
        [((8, span), F32), ((8, span), F32)] + [((head_cols, rows), BF16)] * SIDE,
        [tie(part_out, wo_rel), *peers],
    )
    out_terms = ring(shift_x, out_blocks, -1)

    q_block, k_block = min(256, span), min(2048, span)

    def head_grads(first, last, logsum, carried):
        count = last - first
        size = count * HEAD_DIM
        return call(
            functools.partial(bwd_body, first, last, heads, q_block, k_block),
            [((last * HEAD_DIM, rows), BF16)] * SIDE + [((2 * last * HEAD_DIM, rows), BF16)] * SIDE,
            [*group_q, *group_kv, *group_g, logsum, offset, *carried], None,
            [pltpu.VMEM((count, span, HEAD_DIM), BF16)] * 2
            + [pltpu.VMEM((size, span), BF16)] * 3
            + [pltpu.VMEM((8, span), F32)]
            + [pltpu.VMEM((size, span), F32)] * 3,
            flops=40 * size * span * span, exps=count * span * span, limit=40,
        )

    early = head_grads(0, 1, logsum, ())
    half = SIDE * own_width
    attended, proj_own, proj_other = call(
        proj_body,
        [((head_cols, rows), BF16), ((half, rows), F32), ((half, rows), BF16)],
        [tie(out_terms[0], early[0]), *out_terms[1:], wo_rel],
        flops=2 * head_cols * width * rows,
    )
    proj_got = swap_core(proj_other)
    proj_blocks = call(pair_body, [((own_width, rows), BF16)] * SIDE, [proj_own, proj_got])
    proj_terms = ring(shift_y, proj_blocks, 1)

    grads = head_grads(1, heads, tie(logsum, *proj_blocks), early)
    dq, dkv = grads[:SIDE], grads[SIDE:]
    dkv_terms = ring(shift_z, dkv, -1)
    dq_terms = ring(shift_x, dq, -1)

    mixed = sum(t.astype(F32) for t in [tie(proj_terms[0], dq[0])] + proj_terms[1:])
    residual = (frames.astype(F32) + mixed).astype(BF16)
    res_left, res_right = halos(residual)
    (out_part,) = call(
        out_weights_body, [((head_cols, width), BF16)],
        [tie(attended, dq[0]), back_full], flops=2 * head_cols * width * rows,
    )
    all_gp, part = call(
        functools.partial(weights_body, heads),
        [((3 * head_cols, rows), BF16), ((4 * head_cols, width), BF16)],
        [*dq_terms, *dkv_terms, normed, tie(out_part, res_left, res_right)],
        flops=2 * 3 * head_cols * width * rows,
    )
    each = part.shape[0] // members
    got = lax.all_to_all(part.reshape(members, each, width), "tm", 0, 0, tiled=True)

    gn_own, gn_other = call(
        functools.partial(grads_body, heads, width),
        [((half + 8, rows), F32), ((half + PAD, rows), BF16)],
        [tie(all_gp, part), queries, keys_values, wq_rel],
        flops=2 * 3 * head_cols * width * rows,
    )
    gn_got = swap_core(gn_other)
    gn_blocks = call(grads_pair_body, [((own_width + PAD, rows), BF16)] * SIDE, [gn_own, gn_got])
    gn_terms = ring(shift_y, gn_blocks, 1)
    block_out, kernel_part = call(
        conv_body,
        [((own_width, rows), BF16), ((taps, own_width), F32)],
        [tie(res_left, *gn_blocks), residual, res_right, grad_out, conv_kernel], None,
        [
            pltpu.VMEM((rows + 2 * PAD, own_width), F32),
            pltpu.VMEM((rows, own_width), F32),
            pltpu.VMEM((taps, 8, own_width), F32),
            pltpu.VMEM((STEP + 2 * PAD, own_width), F32),
        ],
        flops=16 * own_width * rows * taps,
    )

    summed = sum(t.astype(F32) for t in [tie(gn_terms[0], kernel_part)] + gn_terms[1:])
    grad_own = summed[:own_width]
    dots = summed[own_width : own_width + 1] + summed[own_width + 1 : own_width + 2]
    column_start = lax.axis_index("mp") * own_width
    gain_own = lax.dynamic_slice_in_dim(norm_gain, column_start, own_width, 0)[:, None]
    normed_own = frames.astype(F32) * inverse
    grad_frames = (
        back_sum + inverse * (grad_own * gain_own) - normed_own * inverse * dots
    ).astype(BF16)
    gain_part = jnp.sum(grad_own * normed_own, axis=1)
    small = jnp.concatenate([kernel_part.astype(BF16), gain_part.astype(BF16)[None]], axis=0)
    small_cols = small.size // each
    first, second = call(
        reduce_body, [((each // 2, width + small_cols), BF16)] * 2,
        [got, small.reshape(each, small_cols)],
    )
    first_row = jnp.stack(ring(shift_x, [first] * SIDE, 1))
    second_row = jnp.stack(ring(shift_z, [second] * SIDE, 1))
    first_all = ring(shift_z, [first_row] * SIDE, 1)
    second_all = ring(shift_x, [second_row] * SIDE, 1)
    qkv_grads, out_grads, small_sum = call(
        functools.partial(finish_body, heads),
        [((3, head_cols, width), F32), ((head_cols, width), F32), ((each, small_cols), F32)],
        [*first_all, *second_all],
    )
    small_sum = small_sum.reshape(taps + 1, own_width)
    return block_out, grad_frames, small_sum[taps], qkv_grads, out_grads, small_sum[:taps]


def solution(mesh):
    return jax.shard_map(
        shards,
        mesh=mesh,
        in_specs=(
            P("mp", "tm"),
            P(),
            P(None, "mp", None),
            P("mp", None),
            P(None, "mp"),
            P("mp", "tm"),
        ),
        out_specs=(
            P("mp", "tm"),
            P("mp", "tm"),
            P("mp"),
            P(None, "mp", None),
            P("mp", None),
            P(None, "mp"),
        ),
        check_vma=False,
    )
```

```python
import functools

import jax
import jax.numpy as jnp
from jax import lax
from jax.experimental import pallas as pl
from jax.experimental.pallas import tpu as pltpu
from jax.sharding import PartitionSpec as P


HEAD_DIM = 64
SIDE = 4
PAD = 16
F32 = jnp.float32
BF16 = jnp.bfloat16


def nn(a, b):
    return jnp.dot(a, b, preferred_element_type=F32)


def nt(a, b):
    return lax.dot_general(a, b, (((1,), (1,)), ((), ())), preferred_element_type=F32)


VM = pl.BlockSpec(memory_space=pltpu.VMEM)


STEP = 32


def fill(pad_ref, left_ref, own_ref, right_ref):
    count = own_ref.shape[1]
    slab = left_ref.shape[1]
    pad_ref[PAD : PAD + count, :] = own_ref[...].astype(F32).T
    pad_ref[:PAD, :] = left_ref[...].astype(F32).T[slab - PAD :, :]
    pad_ref[PAD + count :, :] = right_ref[...].astype(F32).T[:PAD, :]


def back_kernel(left_ref, own_ref, right_ref, taps_ref, sum_ref, cast_ref, pad_ref, acc_ref, near):
    count = own_ref.shape[1]
    fill(pad_ref, left_ref, own_ref, right_ref)
    taps = taps_ref.shape[0]
    half = taps // 2

    def step(i, carry):
        base = pl.multiple_of(i * STEP, STEP)
        near[...] = pad_ref[pl.ds(base, STEP + 2 * PAD), :]
        acc = near[PAD : PAD + STEP, :]
        for j in range(taps):
            start = PAD + half - j
            acc = acc + taps_ref[j : j + 1, :] * near[start : start + STEP, :]
        acc_ref[pl.ds(base, STEP), :] = acc
        return carry

    lax.fori_loop(0, count // STEP, step, 0)
    acc = acc_ref[...].T
    sum_ref[...] = acc
    cast_ref[...] = acc.astype(BF16)


def conv_body(left_ref, own_ref, right_ref, up_ref, taps_ref, out_ref, grad_ref, pad_ref, upt_ref, sums, near):
    count = own_ref.shape[1]
    fill(pad_ref, left_ref, own_ref, right_ref)
    upt_ref[...] = up_ref[...].astype(F32).T
    taps = taps_ref.shape[0]
    half = taps // 2
    sums[...] = jnp.zeros_like(sums)

    def step(i, carry):
        base = pl.multiple_of(i * STEP, STEP)
        near[...] = pad_ref[pl.ds(base, STEP + 2 * PAD), :]
        acc = near[PAD : PAD + STEP, :]
        up = upt_ref[pl.ds(base, STEP), :]
        for j in range(taps):
            start = PAD + j - half
            part = near[start : start + STEP, :]
            acc = acc + taps_ref[j : j + 1, :] * part
            prod = up * part
            sums[j] += sum(prod[8 * s : 8 * s + 8] for s in range(STEP // 8))
        upt_ref[pl.ds(base, STEP), :] = acc
        return carry

    lax.fori_loop(0, count // STEP, step, 0)
    for j in range(taps):
        grad_ref[j : j + 1, :] = jnp.sum(sums[j], axis=0, keepdims=True)
    out_ref[...] = upt_ref[...].T.astype(BF16)


def shift_x(a, by):
    pairs = [
        (z * SIDE + x, z * SIDE + (x + by) % SIDE) for z in range(SIDE) for x in range(SIDE)
    ]
    return lax.ppermute(a, "tm", pairs)


def shift_z(a, by):
    pairs = [
        (z * SIDE + x, ((z + by) % SIDE) * SIDE + x) for z in range(SIDE) for x in range(SIDE)
    ]
    return lax.ppermute(a, "tm", pairs)


def halos(a, slab=128):
    count = lax.axis_size("tm")
    ends = count - 1
    left = lax.ppermute(a[:, a.shape[1] - slab :], "tm", [(i, i + 1) for i in range(ends)])
    right = lax.ppermute(a[:, :slab], "tm", [(i + 1, i) for i in range(ends)])
    return left, right


def place_mp(step, core_step):
    index = lax.axis_index("mp")
    y, core = lax.div(index, 2), lax.rem(index, 2)
    core = 1 - core if core_step else core
    return lax.rem(y + step + SIDE, SIDE) * 2 + core


def place_tm(dz, dx):
    index = lax.axis_index("tm")
    z, x = lax.div(index, SIDE), lax.rem(index, SIDE)
    return lax.rem(z - dz + SIDE, SIDE) * SIDE + lax.rem(x - dx + SIDE, SIDE)


def shift_y(a, by):
    count = lax.axis_size("mp") // 2
    pairs = [(y * 2 + c, ((y + by) % count) * 2 + c) for y in range(count) for c in range(2)]
    return lax.ppermute(a, "mp", pairs)


def swap_core(a):
    count = lax.axis_size("mp")
    return lax.ppermute(a, "mp", [(i, i ^ 1) for i in range(count)])


def call(body, outs, args, specs=None, scratch=(), flops=0, exps=0, limit=20):
    out_shape = tuple(jax.ShapeDtypeStruct(s, t) for s, t in outs)
    moved = sum(a.size * a.dtype.itemsize for a in args)
    moved += sum(o.size * o.dtype.itemsize for o in out_shape)
    return pl.pallas_call(
        body,
        out_shape=out_shape,
        in_specs=specs or [VM] * len(args),
        out_specs=[VM] * len(outs),
        scratch_shapes=list(scratch),
        compiler_params=pltpu.CompilerParams(vmem_limit_bytes=limit * 2**20),
        cost_estimate=pl.CostEstimate(flops=flops, bytes_accessed=moved, transcendentals=exps),
    )(*args)


def ring(shift, blocks, sign):
    return [blocks[0]] + [shift(blocks[r], sign * r) for r in range(1, SIDE)]


def head_rows(h):
    return slice(h * HEAD_DIM, (h + 1) * HEAD_DIM)


def prep_body(after_ref, w_ref, wo_ref, wq_out, wo_out, mixed, turned, turned_out):
    head_cols, width = wo_ref.shape
    heads = head_cols // HEAD_DIM
    for h in range(heads):
        for j in range(3):
            at = (h * 3 + j) * HEAD_DIM
            mixed[at : at + HEAD_DIM, :] = w_ref[j, head_rows(h), :]
    lanes = 128

    def turn(i, carry):
        cols = pl.ds(pl.multiple_of(i * lanes, lanes), lanes)
        turned[cols, :] = mixed[:, cols].T
        turned_out[cols, :] = wo_ref[:, cols].T
        return carry

    lax.fori_loop(0, width // lanes, turn, 0)
    chunk = width // 8
    for r in range(8):
        at = place_mp(r % SIDE, r // SIDE)
        rows = pl.ds(pl.multiple_of(at * chunk, chunk), chunk)
        wq_out[r * chunk : (r + 1) * chunk, :] = turned[rows, :]
        wo_out[r * chunk : (r + 1) * chunk, :] = turned_out[rows, :]


def norm_body(b0, b1, b2, b3, other, gain_ref, w_ref, normed_out, inv_out, q_out, kv_out, gain):
    own = [b0, b1, b2, b3]
    chunk, rows = b0.shape
    width = normed_out.shape[0]

    def block(r):
        part = own[r][...] if r < 4 else other[(r - 4) * chunk : (r - 3) * chunk, :]
        return part.astype(F32)

    gain[...] = jnp.broadcast_to(gain_ref[...], (8, width)).T
    total = jnp.zeros((1, rows), F32)
    for r in range(8):
        x = block(r)
        total = total + jnp.sum(x * x, axis=0, keepdims=True)
    inverse = lax.rsqrt(total / width + 1e-06)
    inv_out[...] = inverse
    for r in range(8):
        at = pl.ds(pl.multiple_of(place_mp(-(r % SIDE), r // SIDE) * chunk, chunk), chunk)
        normed_out[at, :] = (block(r) * inverse * gain[at, :1]).astype(BF16)
    normed = normed_out[...]
    q_out[...] = nn(w_ref[0], normed).astype(BF16) * jnp.asarray(HEAD_DIM ** (-0.5), BF16)
    head_cols = q_out.shape[0]

    def step(j, carry):
        at = pl.ds(pl.multiple_of((j - 1) * head_cols, head_cols), head_cols)
        kv_out[at, :] = nn(w_ref[j], normed_out[...]).astype(BF16)
        return carry

    lax.fori_loop(1, 3, step, 0)


def back_arrange_body(b0, b1, b2, b3, other, wo_ref, full_out, grad_out):
    own = [b0, b1, b2, b3]
    chunk = b0.shape[0]
    for r in range(8):
        at = pl.ds(pl.multiple_of(place_mp(-(r % SIDE), r // SIDE) * chunk, chunk), chunk)
        full_out[at, :] = own[r][...] if r < 4 else other[(r - 4) * chunk : (r - 3) * chunk, :]
    grad_out[...] = nn(wo_ref[...], full_out[...]).astype(BF16)


def fwd_loop_body(heads, *refs):
    q_refs, kv_refs = refs[:SIDE], refs[SIDE : 2 * SIDE]
    o_ref, lse_ref, keys, vals, queries = refs[2 * SIDE :]
    rows = q_refs[0].shape[1]
    width = heads * HEAD_DIM
    for r in range(SIDE):
        cols = slice(r * rows, (r + 1) * rows)
        vals[:, cols] = kv_refs[r][width:, :]
        queries[:, cols] = q_refs[r][...]
        for h in range(heads):
            keys[h, cols, :] = kv_refs[r][head_rows(h), :].T

    def step(r, carry):
        cols = pl.ds(pl.multiple_of(r * rows, rows), rows)
        for h in range(heads):
            at = head_rows(h)
            scores = nn(keys[h], queries[at, cols])
            top = jnp.max(scores, axis=0, keepdims=True)
            weights = jnp.exp(scores - top)
            total = jnp.sum(weights, axis=0, keepdims=True)
            out = nn(vals[at, :], weights.astype(BF16)) / total
            o_ref[at, cols] = out.astype(BF16)
            lse_ref[h : h + 1, cols] = top + jnp.log(total)
        return carry

    lax.fori_loop(0, SIDE, step, 0)


def stats_body(heads, o_ref, lse_ref, *refs):
    g_refs, out_ref = refs[:SIDE], refs[SIDE]
    rows = g_refs[0].shape[1]
    out_ref[...] = jnp.zeros_like(out_ref)
    out_ref[:heads, :] = lse_ref[...]
    for r in range(SIDE):
        cols = slice(r * rows, (r + 1) * rows)
        for h in range(heads):
            at = head_rows(h)
            out_ref[heads + h : heads + h + 1, cols] = jnp.sum(
                o_ref[at, cols].astype(F32) * g_refs[r][at, :].astype(F32), axis=0, keepdims=True
            )


def combine_body(heads, o_ref, *refs):
    peers, outs = refs[:SIDE], refs[SIDE:]
    lse_out, off_out, blocks = outs[0], outs[1], outs[2:]
    rows = o_ref.shape[1] // SIDE
    for r in range(SIDE):
        cols = slice(r * rows, (r + 1) * rows)
        theirs = []
        for s in range(SIDE):
            at = (r - s) % SIDE
            theirs.append(peers[s][:, at * rows : (at + 1) * rows])
        lse = [t[:heads] for t in theirs]
        off = [t[heads : 2 * heads] for t in theirs]
        top = jnp.maximum(jnp.maximum(lse[0], lse[1]), jnp.maximum(lse[2], lse[3]))
        logsum = top + jnp.log(sum(jnp.exp(v - top) for v in lse))
        shares = [jnp.exp(v - logsum) for v in lse]
        lse_out[:heads, cols] = logsum
        off_out[:heads, cols] = sum(w * v for w, v in zip(shares, off))
        for h in range(heads):
            at = head_rows(h)
            blocks[r][at, :] = (o_ref[at, cols].astype(F32) * shares[0][h : h + 1]).astype(BF16)


def bwd_body(first, last, heads, q_block, k_block, *refs):
    q_refs, kv_refs, g_refs = refs[:SIDE], refs[SIDE : 2 * SIDE], refs[2 * SIDE : 3 * SIDE]
    lse_ref, off_ref = refs[3 * SIDE : 3 * SIDE + 2]
    refs = refs[3 * SIDE + 2 :]
    carried = refs[: 2 * SIDE] if first else ()
    refs = refs[len(carried) :]
    dq_refs, dkv_refs = refs[:SIDE], refs[SIDE : 2 * SIDE]
    keys, vals, kt, qt, gt, stat, dq, dk, dv = refs[2 * SIDE :]
    count = last - first
    rows = q_refs[0].shape[1]
    span = SIDE * rows
    mine = slice(first * HEAD_DIM, last * HEAD_DIM)
    for r in range(SIDE):
        cols = slice(r * rows, (r + 1) * rows)
        qt[:, cols] = q_refs[r][mine, :]
        gt[:, cols] = g_refs[r][mine, :]
        kt[:, cols] = kv_refs[r][mine, :]
        for h in range(count):
            keys[h, cols, :] = kv_refs[r][head_rows(first + h), :].T
            vals[h, cols, :] = kv_refs[r][head_rows(heads + first + h), :].T
    for h in range(count):
        stat[h : h + 1, :] = lse_ref[first + h : first + h + 1, :]
        stat[count + h : count + h + 1, :] = off_ref[first + h : first + h + 1, :]
    dk[...] = jnp.zeros_like(dk)
    dv[...] = jnp.zeros_like(dv)
    dq[...] = jnp.zeros_like(dq)

    def q_step(qi, carry):
        q_cols = pl.ds(pl.multiple_of(qi * q_block, q_block), q_block)

        def k_step(ki, carry):
            k_rows = pl.ds(pl.multiple_of(ki * k_block, k_block), k_block)
            for h in range(count):
                at = head_rows(h)
                q = qt[at, q_cols]
                g = gt[at, q_cols]
                scores = nn(keys[h, k_rows, :], q)
                prob = jnp.exp(scores - stat[h : h + 1, q_cols])
                grad_prob = nn(vals[h, k_rows, :], g)
                off = stat[count + h : count + h + 1, q_cols]
                grad_score = (prob * (grad_prob - off)).astype(BF16)
                dq[at, q_cols] += nn(kt[at, k_rows], grad_score)
                dk[at, k_rows] += nt(q, grad_score)
                dv[at, k_rows] += nt(g, prob.astype(BF16))
            return carry

        lax.fori_loop(0, span // k_block, k_step, 0)
        return carry

    lax.fori_loop(0, span // q_block, q_step, 0)
    done = first * HEAD_DIM
    for r in range(SIDE):
        cols = slice(r * rows, (r + 1) * rows)
        dq_refs[r][done:, :] = (dq[:, cols] * HEAD_DIM ** (-0.5)).astype(BF16)
        half = last * HEAD_DIM
        dkv_refs[r][done:half, :] = dk[:, cols].astype(BF16)
        dkv_refs[r][half + done :, :] = dv[:, cols].astype(BF16)
        if first:
            dq_refs[r][:done, :] = carried[r][...]
            dkv_refs[r][:done, :] = carried[SIDE + r][:done, :]
            dkv_refs[r][half : half + done, :] = carried[SIDE + r][done:, :]


def sum_terms(refs):
    return sum(t[...].astype(F32) for t in refs)


def proj_body(*refs):
    terms, wo_ref = refs[:SIDE], refs[SIDE]
    att_out, own_out, other_out = refs[SIDE + 1 :]
    attended = sum_terms(terms).astype(BF16)
    half = own_out.shape[0]
    chunk = half // SIDE

    def step(d, carry):
        at = pl.multiple_of(d * chunk, chunk)
        rows = pl.ds(at, chunk)
        other_out[rows, :] = nn(wo_ref[pl.ds(half + at, chunk), :], attended).astype(BF16)
        own_out[rows, :] = nn(wo_ref[rows, :], attended)
        return carry

    lax.fori_loop(0, SIDE, step, 0)
    att_out[...] = attended


def out_weights_body(att_ref, full_ref, part_out):
    chunk = full_ref.shape[0] // SIDE

    def step(d, carry):
        cols = pl.ds(pl.multiple_of(d * chunk, chunk), chunk)
        part_out[:, cols] = nt(att_ref[...], full_ref[cols, :]).astype(BF16)
        return carry

    lax.fori_loop(0, SIDE, step, 0)


def pair_body(own_ref, got_ref, *outs):
    chunk = outs[0].shape[0]
    for d in range(SIDE):
        at = slice(d * chunk, (d + 1) * chunk)
        outs[d][...] = (own_ref[at, :] + got_ref[at, :].astype(F32)).astype(BF16)


def weights_body(heads, *refs):
    dq, dkv = refs[:SIDE], refs[SIDE : 2 * SIDE]
    normed_ref, out_part_ref, gp_out = refs[2 * SIDE : 2 * SIDE + 3]
    to_x, to_z = refs[2 * SIDE + 3 : 3 * SIDE + 3], refs[3 * SIDE + 3 : 4 * SIDE + 3]
    held = refs[4 * SIDE + 3]
    width = heads * HEAD_DIM
    grad_q = sum_terms(dq).astype(BF16)
    grad_kv = sum_terms(dkv).astype(BF16)
    for h in range(heads):
        at = h * 3 * HEAD_DIM
        gp_out[at : at + HEAD_DIM, :] = grad_q[head_rows(h)]
        gp_out[at + HEAD_DIM : at + 2 * HEAD_DIM, :] = grad_kv[head_rows(h)]
        gp_out[at + 2 * HEAD_DIM : at + 3 * HEAD_DIM, :] = grad_kv[head_rows(heads + h)]

    def step(h, carry):
        rows = pl.ds(pl.multiple_of(h * 3 * HEAD_DIM, 3 * HEAD_DIM), 3 * HEAD_DIM)
        held[rows, :] = nt(gp_out[rows, :], normed_ref[...])
        return carry

    lax.fori_loop(0, heads, step, 0)
    held[3 * width :, :] = out_part_ref[...].astype(F32)
    half = to_x[0].shape[1]
    for r in range(SIDE):

        def pick(e, carry):
            at = pl.multiple_of(place_tm(e, r) * 2 * half, 8)
            to_x[r][e] = held[pl.ds(at, half), :].astype(BF16)
            at = pl.multiple_of(place_tm(r, e) * 2 * half + half, 8)
            to_z[r][e] = held[pl.ds(at, half), :].astype(BF16)
            return carry

        lax.fori_loop(0, SIDE, pick, 0)


def split(v):
    high = v.astype(BF16)
    return high, (v - high.astype(F32)).astype(BF16)


def grads_body(heads, width, all_gp, q_ref, kv_ref, wq_ref, own_out, other_out):
    size = 3 * HEAD_DIM
    dots = jnp.zeros((1, q_ref.shape[1]), F32)
    for h in range(heads):
        at = h * size
        gp = all_gp[at : at + size, :].astype(F32)
        q = q_ref[head_rows(h), :].astype(F32) * HEAD_DIM**0.5
        k = kv_ref[head_rows(h), :].astype(F32)
        v = kv_ref[head_rows(heads + h), :].astype(F32)
        for j, held in enumerate((q, k, v)):
            dots = dots + jnp.sum(
                gp[j * HEAD_DIM : (j + 1) * HEAD_DIM] * held, axis=0, keepdims=True
            )
    dots = dots / width
    half = wq_ref.shape[0] // 2
    chunk = half // SIDE

    def step(d, carry):
        at = pl.multiple_of(d * chunk, chunk)
        rows = pl.ds(at, chunk)
        other_out[rows, :] = nn(wq_ref[pl.ds(half + at, chunk), :], all_gp[...]).astype(BF16)
        own_out[rows, :] = nn(wq_ref[rows, :], all_gp[...])
        return carry

    lax.fori_loop(0, SIDE, step, 0)
    high, low = split(dots)
    other_out[half:, :] = jnp.concatenate(
        [high, low, jnp.zeros((PAD - 2, dots.shape[1]), BF16)], axis=0
    )
    own_out[half:, :] = jnp.broadcast_to(dots, (8, dots.shape[1]))


def grads_pair_body(own_ref, got_ref, *outs):
    chunk = outs[0].shape[0] - PAD
    half = SIDE * chunk
    got = got_ref[half:, :].astype(F32)
    dots = own_ref[half : half + 1, :] + got[0:1] + got[1:2]
    high, low = split(dots)
    tail = jnp.concatenate([high, low, jnp.zeros((PAD - 2, dots.shape[1]), BF16)], axis=0)
    for d in range(SIDE):
        at = slice(d * chunk, (d + 1) * chunk)
        outs[d][:chunk, :] = (own_ref[at, :] + got_ref[at, :].astype(F32)).astype(BF16)
        outs[d][chunk:, :] = tail


def row_sums_body(*refs):
    firsts, seconds, outs = refs[:SIDE], refs[SIDE : 2 * SIDE], refs[2 * SIDE :]
    lanes = 128

    def step(i, carry):
        cols = pl.ds(pl.multiple_of(i * lanes, lanes), lanes)
        for e in range(SIDE):
            outs[e][:, cols] = sum(t[e, :, cols].astype(F32) for t in firsts).astype(BF16)
            outs[SIDE + e][:, cols] = sum(t[e, :, cols].astype(F32) for t in seconds).astype(BF16)
        return carry

    lax.fori_loop(0, outs[0].shape[1] // lanes, step, 0)


def reduce_body(*refs):
    firsts, seconds = refs[:SIDE], refs[SIDE : 2 * SIDE]
    small_ref, first_out, second_out = refs[2 * SIDE :]
    half, width = firsts[0].shape
    lanes = 256

    def step(i, carry):
        cols = pl.ds(pl.multiple_of(i * lanes, lanes), lanes)
        first_out[:, cols] = sum(t[:, cols].astype(F32) for t in firsts).astype(BF16)
        second_out[:, cols] = sum(t[:, cols].astype(F32) for t in seconds).astype(BF16)
        return carry

    lax.fori_loop(0, width // lanes, step, 0)
    first_out[:, width:] = small_ref[:half, :]
    second_out[:, width:] = small_ref[half:, :]


def finish_body(heads, *refs):
    firsts, seconds = refs[:SIDE], refs[SIDE : 2 * SIDE]
    qkv_out, proj_out, small_out = refs[2 * SIDE :]
    half = firsts[0].shape[1]
    each = 2 * half
    width = qkv_out.shape[2]
    step = 8
    qkv_rows = 3 * heads * HEAD_DIM
    qkv_members = qkv_rows // each
    small_out[...] = jnp.zeros_like(small_out)

    def place(ref, e, m, start):
        @pl.when(m < qkv_members)
        def _():
            for i in range(0, half, step):
                row = m * each + (start + i)
                block = lax.div(row, HEAD_DIM)
                at = lax.div(block, 3) * HEAD_DIM + lax.rem(row, HEAD_DIM)
                at = pl.ds(pl.multiple_of(at, step), step)
                qkv_out[lax.rem(block, 3), at, :] = ref[e, i : i + step, :width].astype(F32)

        @pl.when(m >= qkv_members)
        def _():
            for i in range(0, half, step):
                at = pl.ds(pl.multiple_of(m * each + (start + i) - qkv_rows, step), step)
                proj_out[at, :] = ref[e, i : i + step, :width].astype(F32)

    for d in range(SIDE):

        def spread(e, carry):
            place(firsts[d], e, place_tm(d, e), 0)
            place(seconds[d], e, place_tm(e, d), half)
            small_out[:half, :] += firsts[d][e, :, width:].astype(F32)
            small_out[half:, :] += seconds[d][e, :, width:].astype(F32)
            return carry

        lax.fori_loop(0, SIDE, spread, 0)


def tie(value, *others):
    return lax.optimization_barrier((value, *others))[0]


def shards(frames, norm_gain, w_qkv, w_out, conv_kernel, grad_out):
    own_width, rows = frames.shape
    head_cols, width = w_qkv.shape[1:]
    heads = head_cols // HEAD_DIM
    members = lax.axis_size("tm")
    taps = conv_kernel.shape[0]
    span = SIDE * rows

    def with_swap(blocks):
        return blocks + [swap_core(jnp.concatenate(blocks, axis=0))]

    up_left, up_right = halos(grad_out)
    in_blocks = ring(shift_y, [frames] * SIDE, 1)
    back_sum, back_cast = call(
        back_kernel,
        [((own_width, rows), F32), ((own_width, rows), BF16)],
        [up_left, grad_out, up_right, conv_kernel], None,
        [
            pltpu.VMEM((rows + 2 * PAD, own_width), F32),
            pltpu.VMEM((rows, own_width), F32),
            pltpu.VMEM((STEP + 2 * PAD, own_width), F32),
        ],
        flops=8 * own_width * rows * taps,
    )
    in_blocks = list(lax.optimization_barrier((*in_blocks, back_cast)))
    back_cast = in_blocks.pop()
    in_blocks = with_swap(in_blocks)
    back_blocks = ring(shift_y, [back_cast] * SIDE, 1)
    normed, inverse, queries, keys_values = call(
        norm_body,
        [((width, rows), BF16), ((1, rows), F32), ((head_cols, rows), BF16), ((2 * head_cols, rows), BF16)],
        [*in_blocks, norm_gain[None], w_qkv], None, [pltpu.VMEM((width, 8), F32)],
        flops=2 * 3 * head_cols * width * rows,
    )
    group_kv = ring(shift_z, [keys_values] * SIDE, 1)
    group_q = ring(shift_x, [queries] * SIDE, 1)

    back_blocks = list(lax.optimization_barrier((*back_blocks, keys_values)))[:SIDE]
    back_blocks = with_swap(back_blocks)
    back_full, grad_attn = call(
        back_arrange_body,
        [((width, rows), BF16), ((head_cols, rows), BF16)],
        [*back_blocks, w_out],
        flops=2 * head_cols * width * rows,
    )
    group_g = ring(shift_x, [grad_attn] * SIDE, 1)

    part_out, part_lse = call(
        functools.partial(fwd_loop_body, heads),
        [((head_cols, span), BF16), ((heads, span), F32)],
        [tie(group_q[0], grad_attn), *group_q[1:], *group_kv], None,
        [
            pltpu.VMEM((heads, span, HEAD_DIM), BF16),
            pltpu.VMEM((head_cols, span), BF16),
            pltpu.VMEM((head_cols, span), BF16),
        ],
        flops=16 * head_cols * span * span, exps=heads * span * span, limit=40,
    )
    (stats,) = call(
        functools.partial(stats_body, heads),
        [((8, span), F32)], [part_out, part_lse, *group_g],
    )
    peers = ring(shift_x, [stats] * SIDE, 1)
    wq_rel, wo_rel = call(
        prep_body,
        [((width, 3 * head_cols), BF16), ((width, head_cols), BF16)],
        [stats[:, :128], w_qkv, w_out], None,
        [
            pltpu.VMEM((3 * head_cols, width), BF16),
            pltpu.VMEM((width, 3 * head_cols), BF16),
            pltpu.VMEM((width, head_cols), BF16),
        ],
    )
    logsum, offset, *out_blocks = call(
        functools.partial(combine_body, heads),
        [((8, span), F32), ((8, span), F32)] + [((head_cols, rows), BF16)] * SIDE,
        [tie(part_out, wo_rel), *peers],
    )
    out_terms = ring(shift_x, out_blocks, -1)

    q_block, k_block = min(256, span), min(2048, span)

    def head_grads(first, last, logsum, carried):
        count = last - first
        size = count * HEAD_DIM
        return call(
            functools.partial(bwd_body, first, last, heads, q_block, k_block),
            [((last * HEAD_DIM, rows), BF16)] * SIDE + [((2 * last * HEAD_DIM, rows), BF16)] * SIDE,
            [*group_q, *group_kv, *group_g, logsum, offset, *carried], None,
            [pltpu.VMEM((count, span, HEAD_DIM), BF16)] * 2
            + [pltpu.VMEM((size, span), BF16)] * 3
            + [pltpu.VMEM((8, span), F32)]
            + [pltpu.VMEM((size, span), F32)] * 3,
            flops=40 * size * span * span, exps=count * span * span, limit=40,
        )

    early = head_grads(0, 1, logsum, ())
    half = SIDE * own_width
    attended, proj_own, proj_other = call(
        proj_body,
        [((head_cols, rows), BF16), ((half, rows), F32), ((half, rows), BF16)],
        [tie(out_terms[0], early[0]), *out_terms[1:], wo_rel],
        flops=2 * head_cols * width * rows,
    )
    proj_got = swap_core(proj_other)
    proj_blocks = call(pair_body, [((own_width, rows), BF16)] * SIDE, [proj_own, proj_got])
    proj_terms = ring(shift_y, proj_blocks, 1)

    grads = head_grads(1, heads, tie(logsum, *proj_blocks), early)
    dq, dkv = grads[:SIDE], grads[SIDE:]
    dkv_terms = ring(shift_z, dkv, -1)
    dq_terms = ring(shift_x, dq, -1)

    mixed = sum(t.astype(F32) for t in [tie(proj_terms[0], dq[0])] + proj_terms[1:])
    residual = (frames.astype(F32) + mixed).astype(BF16)
    res_left, res_right = halos(residual)
    (out_part,) = call(
        out_weights_body, [((head_cols, width), BF16)],
        [tie(attended, dq[0]), back_full], flops=2 * head_cols * width * rows,
    )
    each = 4 * head_cols // members
    all_gp, *chunks = call(
        functools.partial(weights_body, heads),
        [((3 * head_cols, rows), BF16)] + [((SIDE, each // 2, width), BF16)] * 2 * SIDE,
        [*dq_terms, *dkv_terms, normed, tie(out_part, res_left, res_right)], None,
        [pltpu.VMEM((4 * head_cols, width), F32)],
        flops=2 * 3 * head_cols * width * rows,
    )
    first_terms = ring(shift_x, chunks[:SIDE], -1)
    second_terms = ring(shift_z, chunks[SIDE:], -1)

    gn_own, gn_other = call(
        functools.partial(grads_body, heads, width),
        [((half + 8, rows), F32), ((half + PAD, rows), BF16)],
        [tie(all_gp, chunks[0]), queries, keys_values, wq_rel],
        flops=2 * 3 * head_cols * width * rows,
    )
    gn_got = swap_core(gn_other)
    gn_blocks = call(grads_pair_body, [((own_width + PAD, rows), BF16)] * SIDE, [gn_own, gn_got])
    gn_terms = ring(shift_y, gn_blocks, 1)
    sums = call(
        row_sums_body, [((each // 2, width), BF16)] * 2 * SIDE,
        [tie(first_terms[0], *gn_blocks), *first_terms[1:], *second_terms],
    )
    first_terms = ring(shift_z, sums[:SIDE], -1)
    second_terms = ring(shift_x, sums[SIDE:], -1)
    block_out, kernel_part = call(
        conv_body,
        [((own_width, rows), BF16), ((taps, own_width), F32)],
        [tie(res_left, *gn_blocks), residual, res_right, grad_out, conv_kernel], None,
        [
            pltpu.VMEM((rows + 2 * PAD, own_width), F32),
            pltpu.VMEM((rows, own_width), F32),
            pltpu.VMEM((taps, 8, own_width), F32),
            pltpu.VMEM((STEP + 2 * PAD, own_width), F32),
        ],
        flops=16 * own_width * rows * taps,
    )

    summed = sum(t.astype(F32) for t in [tie(gn_terms[0], kernel_part)] + gn_terms[1:])
    grad_own = summed[:own_width]
    dots = summed[own_width : own_width + 1] + summed[own_width + 1 : own_width + 2]
    column_start = lax.axis_index("mp") * own_width
    gain_own = lax.dynamic_slice_in_dim(norm_gain, column_start, own_width, 0)[:, None]
    normed_own = frames.astype(F32) * inverse
    grad_frames = (
        back_sum + inverse * (grad_own * gain_own) - normed_own * inverse * dots
    ).astype(BF16)
    gain_part = jnp.sum(grad_own * normed_own, axis=1)
    small = jnp.concatenate([kernel_part.astype(BF16), gain_part.astype(BF16)[None]], axis=0)
    small_cols = small.size // each
    first, second = call(
        reduce_body, [((each // 2, width + small_cols), BF16)] * 2,
        [*first_terms, *second_terms, small.reshape(each, small_cols)],
    )
    first_row = jnp.stack(ring(shift_x, [first] * SIDE, 1))
    second_row = jnp.stack(ring(shift_z, [second] * SIDE, 1))
    first_all = ring(shift_z, [first_row] * SIDE, 1)
    second_all = ring(shift_x, [second_row] * SIDE, 1)
    qkv_grads, out_grads, small_sum = call(
        functools.partial(finish_body, heads),
        [((3, head_cols, width), F32), ((head_cols, width), F32), ((each, small_cols), F32)],
        [*first_all, *second_all],
    )
    small_sum = small_sum.reshape(taps + 1, own_width)
    return block_out, grad_frames, small_sum[taps], qkv_grads, out_grads, small_sum[:taps]


def solution(mesh):
    return jax.shard_map(
        shards,
        mesh=mesh,
        in_specs=(
            P("mp", "tm"),
            P(),
            P(None, "mp", None),
            P("mp", None),
            P(None, "mp"),
            P("mp", "tm"),
        ),
        out_specs=(
            P("mp", "tm"),
            P("mp", "tm"),
            P("mp"),
            P(None, "mp", None),
            P("mp", None),
            P(None, "mp"),
        ),
        check_vma=False,
    )
```
